32 devices in a mesh: dp: 16 (over z, y, x), mp: 2 (over core).
Axes of the slice: x: 2, y: 2, z: 4, core: 2. Of those that a mesh axis runs over, the one named last changes fastest.
Arguments:
- tokens: bfloat16 [2, 512, 16, 768], P('mp', 'dp'), may hold values from -6 to 6
- cotangent: bfloat16 [2, 512, 16, 768], P('mp', 'dp'), may hold values from -6 to 6
- lengths: int32 [16], replicated, may hold values from 128 to 1024, as said below
- deal_order: int32 [16], replicated, may hold values from 0 to 15, as said below
- attn_in: bfloat16 [1, 3, 768, 768], P(None, None, 'dp', 'mp'), may hold values from -0.21875 to 0.21875
- attn_out: bfloat16 [1, 768, 768], P(None, 'mp', 'dp'), may hold values from -0.875 to 0.875
- ffn_in: bfloat16 [1, 768, 3072], P(None, 'dp', 'mp'), may hold values from -0.21875 to 0.21875
- ffn_out: bfloat16 [1, 3072, 768], P(None, 'mp', 'dp'), may hold values from -0.109375 to 0.109375
- attn_bias: bfloat16 [1, 2, 768], replicated, may hold values from -3 to 3
- ffn_bias: bfloat16 [1, 3072], replicated, may hold values from -3 to 3
- norm_gain: bfloat16 [1, 2, 768], replicated, may hold values from 0.5 to 1.5
- shifts: bfloat16 [1, 4, 768], replicated, may hold values from -3 to 3
Outputs:
- output: bfloat16 [2, 512, 16, 768], P('mp', 'dp')
- input_grad: bfloat16 [2, 512, 16, 768], P('mp', 'dp')
- attn_in_grad: float32 [1, 3, 768, 768], P(None, None, 'dp', 'mp')
- attn_out_grad: float32 [1, 768, 768], P(None, 'mp', 'dp')
- ffn_in_grad: float32 [1, 768, 3072], P(None, 'dp', 'mp')
- ffn_out_grad: float32 [1, 3072, 768], P(None, 'mp', 'dp')
- attn_bias_grad: float32 [1, 2, 768], replicated
- ffn_bias_grad: float32 [1, 3072], replicated
- norm_gain_grad: float32 [1, 2, 768], replicated
- shifts_grad: float32 [1, 4, 768], replicated
The draws below stay inside these ranges and needn't reach their ends.
Inputs may be any that keep to these rules, and one draw needn't show every extreme that they name: `lengths`: some sequence has exactly 1024 valid tokens. `deal_order`: a permutation of the sequences; slot s is processed by data group s.
All inputs are finite; a program needn't handle non-finite values.
Results may differ from the reference program's by a relative error of at most 0.02.
Values may be sent and summed in bfloat16 or wider, within the bound.
No kernel may reach another device: no remote copies, remote signals or barrier semaphores. Data moves between devices by JAX's collectives and lax.ppermute only.
A program may use at most 128 MiB of HBM per device.

```python
import jax
import jax.numpy as jnp
from jax import lax

D = 768
HEADS = 12
HEAD_DIM = 64
FF = 3072
LAYERS = 1
SEQ_LEN = 1024
SEQ_GRP = 1
SEQS = 16
N_MP = 2


def length_table(key):
    spread = jax.random.randint(jax.random.fold_in(key, 11), (SEQS,), SEQ_LEN // 8, SEQ_LEN + 1, dtype=jnp.int32)
    chosen = jax.random.randint(jax.random.fold_in(key, 12), (), 0, SEQS, dtype=jnp.int32)
    return jnp.where(jnp.arange(SEQS, dtype=jnp.int32) == chosen, SEQ_LEN, spread).astype(jnp.int32)


def draw_lengths(key, part):
    return length_table(key)


def draw_deal_order(key, part):
    length_rows = length_table(key)
    ascending = jnp.argsort(length_rows * SEQS + jnp.arange(SEQS, dtype=jnp.int32)).astype(jnp.int32)
    groups = SEQS // SEQ_GRP
    rank_list = jnp.arange(SEQS, dtype=jnp.int32)
    rounds = rank_list // groups
    places = rank_list % groups
    target = jnp.where(rounds % 2 == 0, places, groups - 1 - places)
    slot_list = target * SEQ_GRP + rounds
    return jnp.zeros((SEQS,), jnp.int32).at[slot_list].set(ascending)


def block_scale(key, extent, pieces, low, top_value):
    def one(dim, blocks):
        heights = jax.random.uniform(jax.random.fold_in(jax.random.fold_in(key, 6), dim), (blocks,), jnp.float32, low / len(pieces), top_value / len(pieces))
        return jnp.repeat(jnp.exp(heights), extent[dim] // blocks).reshape((-1,) + (1,) * (len(extent) - dim - 1))

    level = one(*pieces[0])
    for cut in pieces[1:]:
        level = level * one(*cut)
    return level


def gaussian(own_key, extent, width, limit, split=(), kind=jnp.bfloat16):
    values = width * jax.random.normal(own_key, extent, jnp.float32)
    if split:
        values = values * block_scale(own_key, extent, split, -0.22, 0.18)
    return jnp.clip(values, -limit, limit).astype(kind)


def setup_inputs(seed: int = 0) -> dict:
    streams_of = jax.random.split(jax.random.key(seed), 13)
    tokens = gaussian(streams_of[0], (N_MP, SEQ_LEN // N_MP, SEQS, D), 1.0, 6.0, ((0, 2), (1, 16)))
    cotangent = gaussian(streams_of[1], (N_MP, SEQ_LEN // N_MP, SEQS, D), 1.0, 6.0, ((0, 2), (1, 16)))
    lengths = draw_lengths(jax.random.fold_in(streams_of[12], 71), 0)
    deal_order = draw_deal_order(jax.random.fold_in(streams_of[12], 71), 0)
    attn_in = gaussian(streams_of[4], (LAYERS, 3, D, D), D ** -0.5, 0.21875, ((2, 16), (3, 2)))
    attn_out = gaussian(streams_of[5], (LAYERS, D, D), (D // 16) ** -0.5, 0.875, ((1, 2), (2, 16)))
    ffn_in = gaussian(streams_of[6], (LAYERS, D, FF), D ** -0.5, 0.21875, ((1, 16), (2, 2)))
    ffn_out = gaussian(streams_of[7], (LAYERS, FF, D), FF ** -0.5, 0.109375, ((1, 2), (2, 16)))
    attn_bias = gaussian(streams_of[8], (LAYERS, 2, D), 0.5, 3.0)
    ffn_bias = gaussian(streams_of[9], (LAYERS, FF), 0.5, 3.0)
    norm_gain = jnp.clip(1.0 + 0.1 * jax.random.normal(streams_of[10], (LAYERS, 2, D), jnp.float32), 0.5, 1.5).astype(jnp.bfloat16)
    shifts = gaussian(streams_of[11], (LAYERS, 4, D), 0.5, 3.0)
    return {"tokens": tokens, "cotangent": cotangent, "lengths": lengths, "deal_order": deal_order, "attn_in": attn_in, "attn_out": attn_out, "ffn_in": ffn_in, "ffn_out": ffn_out, "attn_bias": attn_bias, "ffn_bias": ffn_bias, "norm_gain": norm_gain, "shifts": shifts}


@jax.custom_vjp
def low(v):
    return lax.optimization_barrier(v.astype(jnp.bfloat16)).astype(jnp.float32)

@jax.custom_vjp
def low_back(v):
    return v

def low_keep(v):
    return (low(v), None)

def low_pass(kept, grad):
    return (grad,)

def back_keep(v):
    return (v, None)

def back_low(kept, grad):
    return (low(grad),)
low.defvjp(low_keep, low_pass)
low_back.defvjp(back_keep, back_low)
highest = lax.Precision.HIGHEST
eps_norm = 1e-12
root_half = 0.7071067811865476
negative_fill = -1000000000.0

def norm_rows(mixed_rows, gain, shift):
    center = mixed_rows - lax.optimization_barrier(jnp.mean(mixed_rows, axis=-1, keepdims=True))
    normed = center * lax.rsqrt(lax.optimization_barrier(jnp.mean(center * center, axis=-1, keepdims=True)) + eps_norm)
    return normed * gain + shift

def project(rows, matrix):
    return jnp.einsum('bld,de->ble', rows, matrix, precision=highest)

def one_layer(hidden, key_valid, params):
    attn_in, attn_out, ffn_in, ffn_out, attn_bias, ffn_bias, norm_gain, shifts = params
    batch_seqs = hidden.shape[0]
    shaped = (batch_seqs, SEQ_LEN, HEADS, HEAD_DIM)
    rounded = low(hidden)
    queries = low(low_back(project(rounded, attn_in[0])) + attn_bias[0]).reshape(shaped)
    key_rows = low(low_back(project(rounded, attn_in[1]))).reshape(shaped)
    values = low(low_back(project(rounded, attn_in[2])) + attn_bias[1]).reshape(shaped)
    raw_scores = low_back(jnp.einsum('bqhe,bkhe->bhqk', queries, key_rows, precision=highest))
    scores = jnp.where(key_valid[:, None, None, :], raw_scores * HEAD_DIM ** (-0.5), negative_fill)
    exponent = jnp.exp(scores - lax.optimization_barrier(jnp.max(scores, axis=-1, keepdims=True)))
    probs = exponent / lax.optimization_barrier(jnp.sum(exponent, axis=-1, keepdims=True))
    context = low(low_back(jnp.einsum('bhqk,bkhe->bqhe', low(probs), values, precision=highest)))
    attended = low_back(project(context.reshape(batch_seqs, SEQ_LEN, D), attn_out)) + shifts[0]
    middle = norm_rows(hidden + attended, norm_gain[0], shifts[1])
    hidden_pre = low_back(project(low(middle), ffn_in)) + ffn_bias
    activated = low(0.5 * hidden_pre * (1.0 + lax.erf(hidden_pre * root_half)))
    down_rows = low_back(project(activated, ffn_out)) + shifts[2]
    return norm_rows(middle + down_rows, norm_gain[1], shifts[3])

def stack_layers(hidden, key_valid, params):
    for which_layer in range(LAYERS):
        hidden = one_layer(hidden, key_valid, tuple((param[which_layer] for param in params)))
    return hidden

def reference(tokens, cotangent, lengths, deal_order, attn_in, attn_out, ffn_in, ffn_out, attn_bias, ffn_bias, norm_gain, shifts):
    group_size = 4 if SEQS % 4 == 0 else 1
    count_groups = SEQS // group_size

    def by_sequence(array):
        whole = array.astype(jnp.float32).reshape(SEQ_LEN, SEQS, D).transpose(1, 0, 2)
        return whole.reshape(count_groups, group_size, SEQ_LEN, D)
    inputs = by_sequence(tokens)
    grads_in = by_sequence(cotangent)
    key_valid = (jnp.arange(SEQ_LEN, dtype=jnp.int32)[None, :] < lengths[:, None]).reshape(count_groups, group_size, SEQ_LEN)
    params = tuple((param.astype(jnp.float32) for param in (attn_in, attn_out, ffn_in, ffn_out, attn_bias, ffn_bias, norm_gain, shifts)))
    run_group = jax.checkpoint(stack_layers)

    def forward(layer_inputs, layer_params):
        return lax.map(lambda pair: run_group(pair[0], pair[1], layer_params), (layer_inputs, key_valid))
    outputs, pull = jax.vjp(forward, inputs, params)
    grad_inputs, grad_params = pull(grads_in)

    def dealt(array):
        whole = array.reshape(SEQS, SEQ_LEN, D)[deal_order]
        return whole.transpose(1, 0, 2).reshape(N_MP, SEQ_LEN // N_MP, SEQS, D).astype(jnp.bfloat16)
    return (dealt(outputs), dealt(grad_inputs), grad_params[0], grad_params[1], grad_params[2], grad_params[3], grad_params[4], grad_params[5], grad_params[6], grad_params[7])
```

```python
import functools

import jax
import jax.numpy as jnp
from jax import lax
from jax.experimental import pallas as pl
from jax.experimental.pallas import tpu as pltpu
from jax.sharding import PartitionSpec as P

HEAD_DIM = 64
PAIR = 2 * HEAD_DIM

eps_norm = 1e-12
root_half = 0.7071067811865476
inv_root_two_pi = 0.3989422804014327
negative_fill = -1000000000.0
F32 = jnp.float32
BF16 = jnp.bfloat16


def matmul(a, b):
    return lax.dot_general(a, b, (((1,), (0,)), ((), ())), preferred_element_type=F32)


def matmul_nt(a, b):
    return lax.dot_general(a, b, (((1,), (1,)), ((), ())), preferred_element_type=F32)


def matmul_tn(a, b):
    return lax.dot_general(a, b, (((0,), (0,)), ((), ())), preferred_element_type=F32)


def xor_permute(x, axis, mask):
    n = lax.axis_size(axis)
    return lax.ppermute(x, axis, [(i, i ^ mask) for i in range(n)])


def dp_axes(n):
    bits = n.bit_length() - 1
    out, at = [], 0
    while at < bits:
        width = 1 if at < 2 else min(2, bits - at)
        out.append((at, 1 << width))
        at += width
    return out[::-1]


def stage_gather(x, axis, shift, size):
    return jnp.concatenate(
        [x] + [xor_permute(x, axis, j << shift) for j in range(1, size)], axis=0
    )


def unscramble_kernel(count, order_of, x_ref, o_ref, sems):
    me = lax.axis_index("dp")
    copies = []
    for block in range(count):
        place = lax.bitwise_xor(me, block)
        spot = 0
        for stride, shift, size in order_of:
            spot = spot + stride * lax.bitwise_and(lax.shift_right_logical(place, shift), size - 1)
        copies.append(pltpu.make_async_copy(x_ref.at[spot], o_ref.at[block], sems.at[block]))
    for copy in copies:
        copy.start()
    for copy in copies:
        copy.wait()


def unscramble(x, stages):
    count = x.shape[0]
    strides, stride = [], 1
    for shift, size in stages:
        strides.append((stride, shift, size))
        stride *= size
    return pl.pallas_call(
        functools.partial(unscramble_kernel, count, tuple(strides)),
        out_shape=jax.ShapeDtypeStruct(x.shape, x.dtype),
        in_specs=[pl.BlockSpec(memory_space=pl.ANY)],
        out_specs=pl.BlockSpec(memory_space=pl.ANY),
        scratch_shapes=[pltpu.SemaphoreType.DMA((count,))],
        name="unscramble",
    )(x)


def gather_rows(x, stages):
    y = x[None]
    for shift, size in stages:
        y = stage_gather(y, "dp", shift, size)
    y = unscramble(y, stages)
    return y.reshape(-1, x.shape[1])


def scatter_sum(g, stages, axes):
    me = lax.axis_index("dp")
    sizes = [size for _, size in axes]
    cols = g.shape[1]
    rows = g.shape[0] // lax.axis_size("dp")
    x = g.reshape(tuple(sizes) + (rows, cols))
    left = list(axes)
    for number, (shift, size) in enumerate(stages):
        at = left.index((shift, size))
        coord = lax.bitwise_and(lax.shift_right_logical(me, shift), size - 1)
        parts = []
        for j in range(1, size):
            piece = lax.dynamic_index_in_dim(x, lax.bitwise_xor(coord, j), at, keepdims=False)
            parts.append(xor_permute(piece, "dp", j << shift))
        own = lax.dynamic_index_in_dim(x, coord, at, keepdims=False).astype(F32)
        parts = [own] + [part.astype(F32) for part in parts]
        while len(parts) > 1:
            parts = [parts[i] + parts[i + 1] for i in range(0, len(parts), 2)]
        x = parts[0]
        if number + 1 < len(stages):
            x = x.astype(BF16)
        left.pop(at)
    return x


def sum_all(v, axes):
    v = v + xor_permute(v, "mp", 1)
    for shift, size in reversed(axes):
        parts = [v] + [xor_permute(v, "dp", j << shift) for j in range(1, size)]
        while len(parts) > 1:
            parts = [parts[i] + parts[i + 1] for i in range(0, len(parts), 2)]
        v = parts[0]
    return v


def attend_forward_kernel(block, qkv_ref, bias_ref, ctx_ref, lse_ref):
    length = qkv_ref.shape[0]
    bias = bias_ref[...]
    for head in range(2):
        low = head * HEAD_DIM
        keys = qkv_ref[:, PAIR + low : PAIR + low + HEAD_DIM]
        values_t = qkv_ref[:, 2 * PAIR + low : 2 * PAIR + low + HEAD_DIM].T
        for start in range(0, length, block):
            queries = qkv_ref[start : start + block, low : low + HEAD_DIM]
            scores = matmul_nt(keys, queries) + bias
            top = jnp.max(scores, axis=0, keepdims=True)
            exponent = jnp.exp(scores - top)
            total = jnp.sum(exponent, axis=0, keepdims=True)
            context_t = matmul(values_t, exponent.astype(BF16)) * (1.0 / total)
            ctx_ref[start : start + block, low : low + HEAD_DIM] = context_t.T.astype(BF16)
            lse_ref[0, head : head + 1, start : start + block] = top + jnp.log(total)


def attend_forward(qkv, bias, pairs):
    length = qkv.shape[0]
    return pl.pallas_call(
        functools.partial(attend_forward_kernel, min(256, length)),
        grid=(pairs,),
        out_shape=(
            jax.ShapeDtypeStruct((length, pairs * PAIR), BF16),
            jax.ShapeDtypeStruct((pairs, 2, length), F32),
        ),
        in_specs=[
            pl.BlockSpec((length, 3 * PAIR), lambda p: (0, p)),
            pl.BlockSpec((length, 1), lambda p: (0, 0)),
        ],
        out_specs=(
            pl.BlockSpec((length, PAIR), lambda p: (0, p)),
            pl.BlockSpec((1, 2, length), lambda p: (p, 0, 0)),
        ),
        compiler_params=pltpu.CompilerParams(vmem_limit_bytes=48 << 20),
        cost_estimate=pl.CostEstimate(
            flops=pairs * 2 * 4 * length * length * HEAD_DIM * 8,
            transcendentals=pairs * 2 * length * length,
            bytes_accessed=pairs * length * PAIR * 8,
        ),
        name="attend_forward",
    )(qkv, bias)


def attend_backward_kernel(block, qkv_ref, dctx_ref, lse_ref, bias_ref, out_ref, sums_ref, dk_ref, dv_ref):
    length = qkv_ref.shape[0]
    bias = bias_ref[...]
    for head in range(2):
        low = head * HEAD_DIM
        keys = qkv_ref[:, PAIR + low : PAIR + low + HEAD_DIM]
        keys_t = keys.T
        values = qkv_ref[:, 2 * PAIR + low : 2 * PAIR + low + HEAD_DIM]
        query_sum = jnp.zeros((1, HEAD_DIM), F32)
        for start in range(0, length, block):
            queries = qkv_ref[start : start + block, low : low + HEAD_DIM]
            grads = dctx_ref[start : start + block, low : low + HEAD_DIM]
            lse = lse_ref[0, head : head + 1, start : start + block]
            probs = jnp.exp(matmul_nt(keys, queries) + bias - lse)
            grad_probs = matmul_nt(values, grads)
            inner = jnp.sum(probs * grad_probs, axis=0, keepdims=True)
            grad_scores = (probs * (grad_probs - inner)).astype(BF16)
            dv = matmul(probs.astype(BF16), grads)
            dk = matmul(grad_scores, queries)
            if start == 0:
                dk_ref[...] = dk
                dv_ref[...] = dv
            else:
                dk_ref[...] += dk
                dv_ref[...] += dv
            dq = (matmul(keys_t, grad_scores) * HEAD_DIM ** (-0.5)).T
            query_sum = query_sum + jnp.sum(dq, axis=0, keepdims=True)
            out_ref[start : start + block, low : low + HEAD_DIM] = dq.astype(BF16)
        dk = dk_ref[...]
        dv = dv_ref[...]
        out_ref[:, PAIR + low : PAIR + low + HEAD_DIM] = dk.astype(BF16)
        out_ref[:, 2 * PAIR + low : 2 * PAIR + low + HEAD_DIM] = dv.astype(BF16)
        sums_ref[0, 0:1, low : low + HEAD_DIM] = query_sum
        sums_ref[0, 1:2, low : low + HEAD_DIM] = jnp.sum(dv, axis=0, keepdims=True)


def attend_backward(qkv, dctx, lse, bias, pairs):
    length = qkv.shape[0]
    return pl.pallas_call(
        functools.partial(attend_backward_kernel, min(256, length)),
        grid=(pairs,),
        out_shape=(
            jax.ShapeDtypeStruct((length, pairs * 3 * PAIR), BF16),
            jax.ShapeDtypeStruct((pairs, 2, PAIR), F32),
        ),
        in_specs=[
            pl.BlockSpec((length, 3 * PAIR), lambda p: (0, p)),
            pl.BlockSpec((length, PAIR), lambda p: (0, p)),
            pl.BlockSpec((1, 2, length), lambda p: (p, 0, 0)),
            pl.BlockSpec((length, 1), lambda p: (0, 0)),
        ],
        out_specs=(
            pl.BlockSpec((length, 3 * PAIR), lambda p: (0, p)),
            pl.BlockSpec((1, 2, PAIR), lambda p: (p, 0, 0)),
        ),
        scratch_shapes=[pltpu.VMEM((length, HEAD_DIM), F32), pltpu.VMEM((length, HEAD_DIM), F32)],
        compiler_params=pltpu.CompilerParams(vmem_limit_bytes=48 << 20),
        cost_estimate=pl.CostEstimate(
            flops=pairs * 2 * 10 * length * length * HEAD_DIM * 8,
            transcendentals=pairs * 2 * length * length,
            bytes_accessed=pairs * length * PAIR * 16,
        ),
        name="attend_backward",
    )(qkv, dctx, lse, bias)


def norm_forward(rows):
    center = rows - jnp.mean(rows, axis=1, keepdims=True)
    rstd = lax.rsqrt(jnp.mean(center * center, axis=1, keepdims=True) + eps_norm)
    return center * rstd, rstd


def norm_backward(grad, normed, rstd, gain):
    scaled = grad * gain
    inner = (
        scaled
        - jnp.mean(scaled, axis=1, keepdims=True)
        - normed * jnp.mean(scaled * normed, axis=1, keepdims=True)
    )
    return rstd * inner, jnp.sum(grad * normed, axis=0), jnp.sum(grad, axis=0)


def gelu_value(u):
    return 0.5 * u * (1.0 + lax.erf(u * root_half))


def gelu_slope(u):
    return 0.5 * (1.0 + lax.erf(u * root_half)) + u * jnp.exp(-0.5 * u * u) * inv_root_two_pi


def both_halves(own):
    return jnp.concatenate([own, xor_permute(own, "mp", 1)], axis=0)


def sum_over_mp(part):
    half = part.shape[0] // 2
    other = xor_permute(part.astype(BF16), "mp", 1).astype(F32)
    return part + jnp.concatenate([other[half:], other[:half]], axis=0)


def exchange_in(x, deal_order):
    dealt = jnp.take(x[0], deal_order, axis=1).transpose(1, 0, 2)
    arrived = lax.all_to_all(dealt, "dp", split_axis=0, concat_axis=0, tiled=True)
    return arrived.reshape(-1, x.shape[3])


def exchange_out(rows):
    n = lax.axis_size("dp")
    sent = lax.all_to_all(
        rows.reshape(n, rows.shape[0] // n, rows.shape[1]), "dp", split_axis=0, concat_axis=0, tiled=True
    )
    return sent.transpose(1, 0, 2)[None]


def local(
    tokens, cotangent, lengths, deal_order, attn_in, attn_out, ffn_in, ffn_out,
    attn_bias, ffn_bias, norm_gain, shifts,
):
    dp_size = lax.axis_size("dp")
    mp_rank = lax.axis_index("mp")
    dp_rank = lax.axis_index("dp")
    axes = dp_axes(dp_size)
    low = axes[-2:]
    high = axes[:-2]
    order_one = high + low
    order_two = high + low[::-1]
    back_one = low[::-1] + high[::-1]
    back_two = low + high[::-1]

    width = tokens.shape[3]
    half_len = tokens.shape[1] * dp_size
    seq_len = 2 * half_len
    head_cols = attn_in.shape[3]
    hidden_cols = ffn_in.shape[2]
    pairs = head_cols // PAIR
    shard_rows = attn_in.shape[2]

    three = attn_in[0].reshape(3, shard_rows, pairs, PAIR).transpose(1, 2, 0, 3)
    three = three.reshape(shard_rows, 3 * head_cols)
    back_t = attn_out[0].T
    up = ffn_in[0]
    down_t = ffn_out[0].T
    attn_own = jnp.concatenate([three, back_t], axis=1)
    mid_col = attn_own.shape[1] // 2

    tok_own = exchange_in(tokens, deal_order)
    w_first = gather_rows(attn_own[:, :mid_col], order_one)
    w_second = gather_rows(attn_own[:, mid_col:], order_two)
    w_attn = jnp.concatenate([w_first, w_second], axis=1)
    w_three, w_back = w_attn[:, : 3 * head_cols], w_attn[:, 3 * head_cols :]
    w_up = gather_rows(up, order_one)
    w_down = lax.all_gather(down_t, "dp", axis=0, tiled=True)

    hb = both_halves(tok_own)
    hidden = hb.astype(F32)
    length = lengths[deal_order[dp_rank]]
    place = jnp.arange(seq_len, dtype=jnp.int32)
    place = jnp.where(mp_rank == 0, place, (place + half_len) % seq_len)
    bias_col = jnp.where(place < length, 0.0, negative_fill).astype(F32)[:, None]

    def own_cols(v, count):
        return lax.dynamic_slice_in_dim(v, mp_rank * count, count, v.ndim - 1)

    bias_pair = own_cols(attn_bias[0].astype(F32), head_cols).reshape(2, pairs, PAIR)
    bias_three = jnp.stack([bias_pair[0], jnp.zeros_like(bias_pair[0]), bias_pair[1]], axis=1)
    bias_up = own_cols(ffn_bias[0].astype(F32), hidden_cols)
    scale_three = jnp.concatenate(
        [jnp.full((pairs, 1, PAIR), HEAD_DIM ** (-0.5), F32), jnp.ones((pairs, 2, PAIR), F32)], axis=1
    ).reshape(-1)
    gain = norm_gain[0].astype(F32)
    shift = shifts[0].astype(F32)

    qkv = ((matmul(hb, w_three) + bias_three.reshape(-1)) * scale_three).astype(BF16)
    context, lse = attend_forward(qkv, bias_col, pairs)
    mixed_one = hidden + sum_over_mp(matmul_nt(context, w_back)) + shift[0]
    mid_normed, mid_rstd = norm_forward(mixed_one)
    middle = mid_normed * gain[0] + shift[1]
    mid_low = middle.astype(BF16)
    hidden_pre = matmul(mid_low, w_up) + bias_up
    hidden_low = gelu_value(hidden_pre).astype(BF16)
    mixed_two = middle + sum_over_mp(matmul_nt(hidden_low, w_down)) + shift[2]
    out_normed, out_rstd = norm_forward(mixed_two)
    result = (out_normed[:half_len] * gain[1] + shift[3]).astype(BF16)
    out_tokens = exchange_out(result)

    cot = both_halves(exchange_in(cotangent, deal_order)).astype(F32)
    grad_two, grad_gain_two, grad_shift_four = norm_backward(cot, out_normed, out_rstd, gain[1])
    grad_down_bias = jnp.sum(grad_two, axis=0)
    grad_two_low = grad_two.astype(BF16)
    grad_w_down = matmul_tn(grad_two_low, hidden_low).astype(BF16)
    down_sum = scatter_sum(grad_w_down, back_one, axes)
    grad_hidden = matmul(grad_two_low, w_down) * gelu_slope(hidden_pre)
    grad_up_bias = jnp.sum(grad_hidden, axis=0)
    grad_hidden_low = grad_hidden.astype(BF16)
    grad_w_up = matmul_tn(mid_low, grad_hidden_low).astype(BF16)
    up_sum = scatter_sum(grad_w_up, back_two, axes)
    grad_middle = grad_two + sum_over_mp(matmul_nt(grad_hidden_low, w_up))
    grad_one, grad_gain_one, grad_shift_two = norm_backward(grad_middle, mid_normed, mid_rstd, gain[0])
    grad_out_bias = jnp.sum(grad_one, axis=0)
    grad_one_low = grad_one.astype(BF16)
    grad_w_back = matmul_tn(grad_one_low, context).astype(BF16)
    grad_context = matmul(grad_one_low, w_back).astype(BF16)
    dqkv, pair_sums = attend_backward(qkv, grad_context, lse, bias_col, pairs)
    grad_w_three = matmul_tn(hb, dqkv).astype(BF16)
    grad_attn = jnp.concatenate([grad_w_three, grad_w_back], axis=1)
    first_sum = scatter_sum(grad_attn[:, :mid_col], back_one, axes)
    second_sum = scatter_sum(grad_attn[:, mid_col:], back_two, axes)
    attn_sum = jnp.concatenate([first_sum, second_sum], axis=1)
    grad_part = matmul_nt(dqkv, w_three)
    grad_in = (
        grad_one[:half_len]
        + grad_part[:half_len]
        + xor_permute(grad_part[half_len:].astype(BF16), "mp", 1).astype(F32)
    ).astype(BF16)
    out_grad = exchange_out(grad_in)

    def spread(v, count):
        full = jnp.zeros(v.shape[:-1] + (2 * count,), F32)
        return lax.dynamic_update_slice_in_dim(full, v, mp_rank * count, v.ndim - 1)

    sums_pair = pair_sums.transpose(1, 0, 2).reshape(2, head_cols)
    small = [
        spread(sums_pair, head_cols),
        spread(grad_up_bias, hidden_cols),
        0.5 * jnp.stack([grad_gain_one, grad_gain_two]),
        0.5 * jnp.stack([grad_out_bias, grad_shift_two, grad_down_bias, grad_shift_four]),
    ]
    flat = jnp.concatenate([v.reshape(-1, 128) for v in small], axis=0)
    flat = sum_all(flat, axes)
    outs, at = [], 0
    for v in small:
        rows = v.size // 128
        outs.append(flat[at : at + rows].reshape((1,) + v.shape))
        at += rows
    attn_bias_out, ffn_bias_out, gain_out, shift_out = outs

    three_out = attn_sum[:, : 3 * head_cols].reshape(shard_rows, pairs, 3, PAIR)
    three_out = three_out.transpose(2, 0, 1, 3).reshape(1, 3, shard_rows, head_cols)
    back_out = attn_sum[:, 3 * head_cols :].T[None]
    up_out = up_sum[None]
    down_out = down_sum.T[None]
    return (
        out_tokens, out_grad, three_out, back_out, up_out, down_out,
        attn_bias_out, ffn_bias_out, gain_out, shift_out,
    )


def solution(mesh):
    placed = (
        P("mp", "dp", None, None),
        P("mp", "dp", None, None),
        P(),
        P(),
        P(None, None, "dp", "mp"),
        P(None, "mp", "dp"),
        P(None, "dp", "mp"),
        P(None, "mp", "dp"),
        P(),
        P(),
        P(),
        P(),
    )
    return jax.shard_map(
        local,
        mesh=mesh,
        in_specs=placed,
        out_specs=(
            P("mp", "dp", None, None),
            P("mp", "dp", None, None),
            P(None, None, "dp", "mp"),
            P(None, "mp", "dp"),
            P(None, "dp", "mp"),
            P(None, "mp", "dp"),
            P(),
            P(),
            P(),
            P(),
        ),
        check_vma=False,
    )
```

```python
import functools

import jax
import jax.numpy as jnp
from jax import lax
from jax.experimental import pallas as pl
from jax.experimental.pallas import tpu as pltpu
from jax.sharding import PartitionSpec as P

HEAD_DIM = 64
PAIR = 2 * HEAD_DIM

eps_norm = 1e-12
root_half = 0.7071067811865476
inv_root_two_pi = 0.3989422804014327
negative_fill = -1000000000.0
F32 = jnp.float32
BF16 = jnp.bfloat16


def matmul(a, b):
    return lax.dot_general(a, b, (((1,), (0,)), ((), ())), preferred_element_type=F32)


def matmul_nt(a, b):
    return lax.dot_general(a, b, (((1,), (1,)), ((), ())), preferred_element_type=F32)


def matmul_tn(a, b):
    return lax.dot_general(a, b, (((0,), (0,)), ((), ())), preferred_element_type=F32)


FLOPS_PER_US = 1150000000


def cost(us):
    return pl.CostEstimate(flops=int(us * FLOPS_PER_US), transcendentals=0, bytes_accessed=1000)


def xor_permute(x, axis, mask):
    n = lax.axis_size(axis)
    return lax.ppermute(x, axis, [(i, i ^ mask) for i in range(n)])


def dp_axes(n):
    bits = n.bit_length() - 1
    out, at = [], 0
    while at < bits:
        width = 1 if at < 2 else min(2, bits - at)
        out.append((at, 1 << width))
        at += width
    return out[::-1]


def stage_gather(x, axis, shift, size):
    return jnp.concatenate(
        [x] + [xor_permute(x, axis, j << shift) for j in range(1, size)], axis=0
    )


def assemble_kernel(count, orders, cuts, *refs):
    me = lax.axis_index("dp")
    sources = [(refs[2 * i], refs[2 * i + 1]) for i in range(len(orders))]
    targets = refs[2 * len(orders) :]

    @pl.loop(0, count)
    def _(block):
        place = lax.bitwise_xor(me, block)
        at = 0
        for (own, received), order in zip(sources, orders):
            spot, stride = 0, 1
            for shift, size in order[:-1]:
                spot = spot + stride * lax.bitwise_and(lax.shift_right_logical(place, shift), size - 1)
                stride *= size
            side = lax.bitwise_and(lax.shift_right_logical(place, order[-1][0]), 1)
            cols = own.shape[2]

            def write(source, at=at, cols=cols, spot=spot):
                start = 0
                for target, (low, high) in zip(targets, cuts):
                    first, last = max(low, at), min(high, at + cols)
                    if first < last:
                        target[block, :, first - low : last - low] = source[spot, :, first - at : last - at]

            @pl.when(side == 0)
            def _():
                write(own)

            @pl.when(side == 1)
            def _():
                write(received)

            at += cols


def tie(x, *others):
    return lax.optimization_barrier((x,) + others)[0]


def gather_first(x, order, name):
    with jax.named_scope(name + "_first"):
        y = x[None]
        for shift, size in order[:-2]:
            y = stage_gather(y, "dp", shift, size)
        return y


def gather_next(y, order, name):
    with jax.named_scope(name + "_next"):
        return stage_gather(y, "dp", *order[-2])


def gather_last(y, order, name):
    with jax.named_scope(name + "_last"):
        return [y, xor_permute(y, "dp", 1 << order[-1][0])]


def assemble(sides, orders, widths):
    count = lax.axis_size("dp")
    rows = sides[0].shape[1]
    cuts, at = [], 0
    for w in widths:
        cuts.append((at, at + w))
        at += w
    vmem = pl.BlockSpec(memory_space=pltpu.VMEM)
    outs = pl.pallas_call(
        functools.partial(assemble_kernel, count, tuple(tuple(o) for o in orders), tuple(cuts)),
        out_shape=tuple(jax.ShapeDtypeStruct((count, rows, w), sides[0].dtype) for w in widths),
        in_specs=[vmem] * len(sides),
        out_specs=(vmem,) * len(widths),
        compiler_params=pltpu.CompilerParams(vmem_limit_bytes=6 << 20),
        cost_estimate=cost(1.0),
        name="assemble",
    )(*sides)
    return [o.reshape(count * rows, -1) for o in outs]


def route_kernel(plan, count_in, *refs):
    me = lax.axis_index("dp")
    ins, outs = refs[:count_in], list(refs[count_in:])
    for pieces, sizes, at, shift in plan:
        size = sizes[at]
        inner = 1
        for extent in sizes[at + 1 :]:
            inner *= extent
        rest = inner
        for extent in sizes[:at]:
            rest *= extent
        coord = lax.bitwise_and(lax.shift_right_logical(me, shift), size - 1)
        log_inner = inner.bit_length() - 1
        targets = [outs.pop(0) for _ in range(size)]
        for j, target in enumerate(targets):
            side = lax.bitwise_xor(coord, j)

            @pl.loop(0, rest)
            def _(r, target=target, side=side):
                upper = lax.shift_right_logical(r, log_inner)
                source = (upper * size + side) * inner + lax.bitwise_and(r, inner - 1)
                col = 0
                for piece in pieces:
                    width = piece[0][2] - piece[0][1]
                    first, low, high = piece[0]
                    value = ins[first][source, :, low:high]
                    if len(piece) > 1:
                        value = value.astype(F32)
                        for index, low, high in piece[1:]:
                            value = value + ins[index][source, :, low:high].astype(F32)
                    target[r, :, col : col + width] = value.astype(BF16)
                    col += width


def route(groups, name):
    arrays, plan, shapes = [], [], []
    for pieces, left, axis in groups:
        entries = []
        for piece in pieces:
            entry = []
            for array, low, high in piece:
                known = [i for i, other in enumerate(arrays) if other is array]
                if not known:
                    known = [len(arrays)]
                    arrays.append(array)
                entry.append((known[0], low, high))
            entries.append(tuple(entry))
        at = left.index(axis)
        plan.append((tuple(entries), tuple(size for _, size in left), at, axis[0]))
        total = sum(piece[0][2] - piece[0][1] for piece in pieces)
        array = pieces[0][0][0]
        shapes.append((axis[1], (array.shape[0] // axis[1], array.shape[1], total)))
    vmem = pl.BlockSpec(memory_space=pltpu.VMEM)
    out_shape = [jax.ShapeDtypeStruct(shape, BF16) for size, shape in shapes for _ in range(size)]
    flat = pl.pallas_call(
        functools.partial(route_kernel, tuple(plan), len(arrays)),
        out_shape=out_shape,
        in_specs=[vmem] * len(arrays),
        out_specs=[vmem] * len(out_shape),
        compiler_params=pltpu.CompilerParams(vmem_limit_bytes=6 << 20),
        cost_estimate=cost(1.0),
        name=name,
    )(*arrays)
    outs = []
    for size, _ in shapes:
        outs.append(list(flat[:size]))
        flat = flat[size:]
    return outs


class Scatter:
    def __init__(self, g, cuts, orders, axes, name):
        n = lax.axis_size("dp")
        self.name = name
        self.axes = list(axes)
        self.orders = [list(o) for o in orders]
        g = g.reshape(n, g.shape[0] // n, g.shape[1])
        self.lefts = [list(axes) for _ in orders]
        self.pieces = [[(g, low, high)] for low, high in cuts]
        self.count = 0

    def deal(self):
        self.count += 1
        merged = len(self.pieces) > 1 and len(self.lefts[0]) < 3 and self.lefts[0] == self.lefts[1]
        groups = []
        if merged:
            groups.append((self.pieces, self.lefts[0], self.orders[0][0]))
            self.orders, self.lefts = self.orders[:1], self.lefts[:1]
        else:
            for piece, left, order in zip(self.pieces, self.lefts, self.orders):
                groups.append(([piece], left, order[0]))
        self.dealt = route(groups, f"{self.name}_deal_{self.count}")
        return self.dealt

    def send(self):
        pieces, lefts, orders = [], [], []
        for parts, left, order in zip(self.dealt, self.lefts, self.orders):
            shift, size = order[0]
            with jax.named_scope(f"{self.name}_{self.count}"):
                got = [parts[0]] + [
                    xor_permute(parts[j], "dp", j << shift) for j in range(1, size)
                ]
            pieces.append([(x, 0, x.shape[2]) for x in got])
            lefts.append([axis for axis in left if axis != order[0]])
            orders.append(order[1:])
        self.pieces, self.lefts, self.orders = pieces, lefts, orders

    def after(self, *others):
        arrays = [x for piece in self.pieces for x, _, _ in piece[1:]]
        arrays = list(lax.optimization_barrier((tuple(arrays), others))[0])
        self.pieces = [
            [piece[0]] + [(arrays.pop(0), low, high) for _, low, high in piece[1:]] for piece in self.pieces
        ]

    def total(self):
        outs = []
        for piece in self.pieces:
            parts = [x[0].astype(F32) for x, _, _ in piece]
            while len(parts) > 1:
                parts = [parts[i] + parts[i + 1] for i in range(0, len(parts), 2)]
            outs.append(parts[0])
        return outs[0] if len(outs) == 1 else jnp.concatenate(outs, axis=1)

    def finish(self):
        while self.orders[0]:
            self.deal()
            self.send()
        return self.total()


def sum_stage(v, masks, axis="dp"):
    with jax.named_scope("small_sum"):
        parts = [v] + [xor_permute(v, axis, m) for m in masks]
        while len(parts) > 1:
            parts = [parts[i] + parts[i + 1] for i in range(0, len(parts), 2)]
        return parts[0]


def attend_forward_kernel(block, qkv_ref, bias_ref, *refs):
    ctx_ref, lse_ref = refs[-2:]
    length = qkv_ref.shape[0]
    bias = bias_ref[...]
    for head in range(2):
        low = head * HEAD_DIM
        keys = qkv_ref[:, PAIR + low : PAIR + low + HEAD_DIM]
        values_t = qkv_ref[:, 2 * PAIR + low : 2 * PAIR + low + HEAD_DIM].T
        for start in range(0, length, block):
            queries = qkv_ref[start : start + block, low : low + HEAD_DIM]
            scores = matmul_nt(keys, queries) + bias
            top = jnp.max(scores, axis=0, keepdims=True)
            exponent = jnp.exp(scores - top)
            total = jnp.sum(exponent, axis=0, keepdims=True)
            context_t = matmul(values_t, exponent.astype(BF16)) * (1.0 / total)
            ctx_ref[start : start + block, low : low + HEAD_DIM] = context_t.T.astype(BF16)
            lse_ref[0, head : head + 1, start : start + block] = top + jnp.log(total)


def attend_forward(qkv, bias, first, pairs, total, known=()):
    length = qkv.shape[0]
    return pl.pallas_call(
        functools.partial(attend_forward_kernel, min(256, length)),
        grid=(pairs,),
        out_shape=(
            jax.ShapeDtypeStruct((length, total * PAIR), BF16),
            jax.ShapeDtypeStruct((total, 2, length), F32),
        ),
        in_specs=[
            pl.BlockSpec((length, 3 * PAIR), lambda p: (0, p + first)),
            pl.BlockSpec((length, 1), lambda p: (0, 0)),
        ]
        + [pl.BlockSpec(memory_space=pl.ANY)] * len(known),
        out_specs=(
            pl.BlockSpec((length, PAIR), lambda p: (0, p + first)),
            pl.BlockSpec((1, 2, length), lambda p: (p + first, 0, 0)),
        ),
        input_output_aliases={2: 0, 3: 1} if known else {},
        compiler_params=pltpu.CompilerParams(vmem_limit_bytes=10 << 20),
        cost_estimate=cost(5.9 * pairs),
        name="attend_forward",
    )(qkv, bias, *known)


def attend_backward_kernel(block, qkv_ref, dctx_ref, lse_ref, bias_ref, *refs):
    out_ref, sums_ref, dk_ref, dv_ref = refs[-4:]
    length = qkv_ref.shape[0]
    bias = bias_ref[...]
    for head in range(2):
        low = head * HEAD_DIM
        keys = qkv_ref[:, PAIR + low : PAIR + low + HEAD_DIM]
        keys_t = keys.T
        values = qkv_ref[:, 2 * PAIR + low : 2 * PAIR + low + HEAD_DIM]
        query_sum = jnp.zeros((1, HEAD_DIM), F32)
        for start in range(0, length, block):
            queries = qkv_ref[start : start + block, low : low + HEAD_DIM]
            grads = dctx_ref[start : start + block, low : low + HEAD_DIM]
            lse = lse_ref[0, head : head + 1, start : start + block]
            probs = jnp.exp(matmul_nt(keys, queries) + bias - lse)
            grad_probs = matmul_nt(values, grads)
            inner = jnp.sum(probs * grad_probs, axis=0, keepdims=True)
            grad_scores = (probs * (grad_probs - inner)).astype(BF16)
            dv = matmul(probs.astype(BF16), grads)
            dk = matmul(grad_scores, queries)
            if start == 0:
                dk_ref[...] = dk
                dv_ref[...] = dv
            else:
                dk_ref[...] += dk
                dv_ref[...] += dv
            dq = (matmul(keys_t, grad_scores) * HEAD_DIM ** (-0.5)).T
            query_sum = query_sum + jnp.sum(dq, axis=0, keepdims=True)
            out_ref[start : start + block, low : low + HEAD_DIM] = dq.astype(BF16)
        dk = dk_ref[...]
        dv = dv_ref[...]
        out_ref[:, PAIR + low : PAIR + low + HEAD_DIM] = dk.astype(BF16)
        out_ref[:, 2 * PAIR + low : 2 * PAIR + low + HEAD_DIM] = dv.astype(BF16)
        sums_ref[0, 0:1, low : low + HEAD_DIM] = query_sum
        sums_ref[0, 1:2, low : low + HEAD_DIM] = jnp.sum(dv, axis=0, keepdims=True)


def attend_backward(qkv, dctx, lse, bias, first, pairs, total, known=()):
    length = qkv.shape[0]
    return pl.pallas_call(
        functools.partial(attend_backward_kernel, min(256, length)),
        grid=(pairs,),
        out_shape=(
            jax.ShapeDtypeStruct((length, total * 3 * PAIR), BF16),
            jax.ShapeDtypeStruct((total, 2, PAIR), F32),
        ),
        in_specs=[
            pl.BlockSpec((length, 3 * PAIR), lambda p: (0, p + first)),
            pl.BlockSpec((length, PAIR), lambda p: (0, p + first)),
            pl.BlockSpec((1, 2, length), lambda p: (p + first, 0, 0)),
            pl.BlockSpec((length, 1), lambda p: (0, 0)),
        ]
        + [pl.BlockSpec(memory_space=pl.ANY)] * len(known),
        out_specs=(
            pl.BlockSpec((length, 3 * PAIR), lambda p: (0, p + first)),
            pl.BlockSpec((1, 2, PAIR), lambda p: (p + first, 0, 0)),
        ),
        input_output_aliases={4: 0, 5: 1} if known else {},
        scratch_shapes=[pltpu.VMEM((length, HEAD_DIM), F32), pltpu.VMEM((length, HEAD_DIM), F32)],
        compiler_params=pltpu.CompilerParams(vmem_limit_bytes=10 << 20),
        cost_estimate=cost(7.3 * pairs),
        name="attend_backward",
    )(qkv, dctx, lse, bias, *known)


def call(kernel, outs, args, name, us, vmem_mib=10):
    spec = pl.BlockSpec(memory_space=pltpu.VMEM)
    return pl.pallas_call(
        kernel,
        out_shape=[jax.ShapeDtypeStruct(shape, kind) for shape, kind in outs],
        in_specs=[spec] * len(args),
        out_specs=[spec] * len(outs),
        compiler_params=pltpu.CompilerParams(vmem_limit_bytes=vmem_mib << 20),
        cost_estimate=cost(us),
        name=name,
    )(*args)


def row_blocks(rows, block):
    block = min(block, rows)
    return rows // block, block


def rows_at(i, block):
    return pl.ds(pl.multiple_of(i * block, block), block)


def project_kernel(x_ref, w_ref, bias_ref, scale_ref, out_ref):
    count, block = row_blocks(x_ref.shape[0], 512)

    @pl.loop(0, count)
    def _(i):
        at = rows_at(i, block)
        out_ref[at, :] = ((matmul(x_ref[at, :], w_ref[...]) + bias_ref[...]) * scale_ref[...]).astype(BF16)


def part_kernel(low, high, x_ref, w_ref, out_ref):
    out_ref[...] = matmul_nt(x_ref[low:high, :], w_ref[...]).astype(BF16)


def exchanged_parts(x, w, name):
    half = x.shape[0] // 2
    own, got = [], []
    for number in range(2):
        (part,) = call(
            functools.partial(part_kernel, number * half, (number + 1) * half),
            [((half, w.shape[0]), BF16)],
            (x, w),
            f"{name}_{number}",
            1.5,
        )
        if number == 0:
            x = tie(x, part)
        own.append(part)
        with jax.named_scope(f"{name}_{number}"):
            got.append(xor_permute(part, "mp", 1))
    return own + got[::-1]


def halves(parts, body, rows, block):
    count, block = row_blocks(rows // 2, block)
    for number in range(2):
        own_ref, got_ref = parts[number], parts[2 + number]

        @pl.loop(0, count)
        def _(i, number=number, own_ref=own_ref, got_ref=got_ref):
            at = rows_at(i, block)
            total = own_ref[at, :].astype(F32) + got_ref[at, :].astype(F32)
            body(number, at, rows_at(i + number * count, block), total)


def middle_kernel(x_ref, p0, p1, p2, p3, vec_ref, w_ref, bias_ref, normed_ref, rstd_ref, low_ref, act_ref, slope_ref):
    def body(number, half_at, at, total):
        mixed = x_ref[at, :].astype(F32) + total + vec_ref[2:3, :]
        normed, rstd = norm_forward(mixed)
        normed_ref[at, :] = normed
        rstd_ref[at, :] = rstd
        low = (normed * vec_ref[0:1, :] + vec_ref[3:4, :]).astype(BF16)
        low_ref[at, :] = low
        u = matmul(low, w_ref[...]) + bias_ref[...]
        half_cdf = 0.5 * (1.0 + lax.erf(u * root_half))
        act_ref[at, :] = (u * half_cdf).astype(BF16)
        slope_ref[at, :] = (half_cdf + u * jnp.exp(-0.5 * u * u) * inv_root_two_pi).astype(BF16)

    halves((p0, p1, p2, p3), body, x_ref.shape[0], 256)


def outer_kernel(normed_ref, p0, p1, p2, p3, cot_own_ref, cot_got_ref, vec_ref, out_ref, grad_ref, low_ref, sums_ref):
    sums_ref[...] = jnp.zeros_like(sums_ref)

    def body(number, half_at, at, total):
        mixed = normed_ref[at, :] * vec_ref[0:1, :] + vec_ref[3:4, :] + total + vec_ref[4:5, :]
        normed, rstd = norm_forward(mixed)
        if number == 0:
            out_ref[at, :] = (normed * vec_ref[1:2, :] + vec_ref[5:6, :]).astype(BF16)
        cot = (cot_got_ref if number else cot_own_ref)[half_at, :].astype(F32)
        grad, grad_gain, grad_shift = norm_backward(cot, normed, rstd, vec_ref[1:2, :])
        grad_ref[at, :] = grad
        low_ref[at, :] = grad.astype(BF16)
        sums_ref[0:1, :] += grad_gain
        sums_ref[1:2, :] += grad_shift
        sums_ref[2:3, :] += jnp.sum(grad, axis=0, keepdims=True)

    halves((p0, p1, p2, p3), body, normed_ref.shape[0], 256)


def hidden_grad_kernel(grad_ref, w_ref, slope_ref, out_ref, sums_ref):
    count, block = row_blocks(grad_ref.shape[0], 256)
    sums_ref[...] = jnp.zeros_like(sums_ref)

    @pl.loop(0, count)
    def _(i):
        at = rows_at(i, block)
        grad = matmul(grad_ref[at, :], w_ref[...]) * slope_ref[at, :].astype(F32)
        out_ref[at, :] = grad.astype(BF16)
        sums_ref[...] += jnp.sum(grad, axis=0, keepdims=True)


def inner_kernel(
    grad_in_ref, p0, p1, p2, p3, normed_ref, rstd_ref, vec_ref, w_ref, own_grad_ref, low_ref, ctx_ref, sums_ref
):
    sums_ref[...] = jnp.zeros_like(sums_ref)

    def body(number, half_at, at, total):
        given = grad_in_ref[at, :] + total
        grad, grad_gain, grad_shift = norm_backward(given, normed_ref[at, :], rstd_ref[at, :], vec_ref[0:1, :])
        low = grad.astype(BF16)
        low_ref[at, :] = low
        ctx_ref[at, :] = matmul(low, w_ref[...]).astype(BF16)
        sums_ref[0:1, :] += grad_gain
        sums_ref[1:2, :] += grad_shift
        sums_ref[2:3, :] += jnp.sum(grad, axis=0, keepdims=True)
        if number == 0:
            own_grad_ref[at, :] = grad

    halves((p0, p1, p2, p3), body, normed_ref.shape[0], 256)


def input_grad_kernel(x_ref, w_ref, grad_ref, keep_ref, send_ref):
    half = keep_ref.shape[0]
    send_ref[...] = matmul_nt(x_ref[half:, :], w_ref[...]).astype(BF16)
    keep_ref[...] = grad_ref[...] + matmul_nt(x_ref[:half, :], w_ref[...])


def norm_forward(rows):
    center = rows - jnp.mean(rows, axis=1, keepdims=True)
    rstd = lax.rsqrt(jnp.mean(center * center, axis=1, keepdims=True) + eps_norm)
    return center * rstd, rstd


def norm_backward(grad, normed, rstd, gain):
    scaled = grad * gain
    inner = (
        scaled
        - jnp.mean(scaled, axis=1, keepdims=True)
        - normed * jnp.mean(scaled * normed, axis=1, keepdims=True)
    )
    return (
        rstd * inner,
        jnp.sum(grad * normed, axis=0, keepdims=True),
        jnp.sum(grad, axis=0, keepdims=True),
    )


def both_halves(own):
    return jnp.concatenate([own, xor_permute(own, "mp", 1)], axis=0)


def exchange_in(x, deal_order):
    dealt = x[0].at[:, deal_order].get(mode="promise_in_bounds").transpose(1, 0, 2)
    arrived = lax.all_to_all(dealt, "dp", split_axis=0, concat_axis=0, tiled=True)
    return arrived.reshape(-1, x.shape[3])


def exchange_out(rows):
    n = lax.axis_size("dp")
    with jax.named_scope("out_rows"):
        blocks = rows.reshape(n, rows.shape[0] // n, rows.shape[1])
        sent = lax.all_to_all(blocks, "dp", split_axis=0, concat_axis=0, tiled=True)
        return sent.transpose(1, 0, 2)[None]


def local(
    tokens, cotangent, lengths, deal_order, attn_in, attn_out, ffn_in, ffn_out,
    attn_bias, ffn_bias, norm_gain, shifts,
):
    dp_size = lax.axis_size("dp")
    mp_rank = lax.axis_index("mp")
    dp_rank = lax.axis_index("dp")
    axes = dp_axes(dp_size)
    low = axes[-2:]
    high = axes[:-2]
    order_one = high + low
    order_two = high + low[::-1]
    back_one = low[::-1] + high[::-1]
    back_two = low + high[::-1]

    width = tokens.shape[3]
    half_len = tokens.shape[1] * dp_size
    seq_len = 2 * half_len
    head_cols = attn_in.shape[3]
    hidden_cols = ffn_in.shape[2]
    pairs = head_cols // PAIR
    shard_rows = attn_in.shape[2]

    three = attn_in[0].reshape(3, shard_rows, pairs, PAIR).transpose(1, 2, 0, 3)
    three = three.reshape(shard_rows, 3 * head_cols)
    back_t = attn_out[0].T
    up = ffn_in[0]
    down_t = ffn_out[0].T

    cut_three = 128 * ((3 * head_cols // 128 + 1) // 2)
    pieces_three = [three[:, :cut_three], three[:, cut_three:]]
    rest = jnp.concatenate([back_t, up], axis=1)
    cut_rest = 128 * ((rest.shape[1] // 128 + 1) // 2)
    orders = [tuple(order_one), tuple(order_two)]

    first_three = gather_first(three, order_one, "ag_three")
    with jax.named_scope("in_tokens"):
        tok_own = exchange_in(tokens, deal_order)
    w_down = lax.all_gather(down_t, "dp", axis=0, tiled=True)
    next_three = [
        gather_next(first_three[:, :, :cut_three], order_one, "ag_three"),
        gather_next(first_three[:, :, cut_three:], order_two, "ag_three"),
    ]
    rest, *next_three = lax.optimization_barrier((rest, *next_three))
    first_rest = gather_first(rest, order_one, "ag_rest")
    sides_three = gather_last(next_three[0], order_one, "ag_three") + gather_last(
        next_three[1], order_two, "ag_three"
    )
    (w_three,) = assemble(sides_three, orders, [3 * head_cols])
    own_rest = [first_rest[:, :, :cut_rest], first_rest[:, :, cut_rest:]]
    with jax.named_scope("ag_rest_next"):
        got_rest = [xor_permute(y, "dp", 1 << o[-2][0]) for y, o in zip(own_rest, orders)]

    hb = both_halves(tok_own)
    length = lengths[deal_order[dp_rank]]
    place = jnp.arange(seq_len, dtype=jnp.int32)
    place = jnp.where(mp_rank == 0, place, (place + half_len) % seq_len)
    bias_col = jnp.where(place < length, 0.0, negative_fill).astype(F32)[:, None]

    def own_cols(v, count):
        return lax.dynamic_slice_in_dim(v, mp_rank * count, count, v.ndim - 1)

    bias_pair = own_cols(attn_bias[0].astype(F32), head_cols).reshape(2, pairs, PAIR)
    bias_three = jnp.stack([bias_pair[0], jnp.zeros_like(bias_pair[0]), bias_pair[1]], axis=1).reshape(1, -1)
    bias_up = own_cols(ffn_bias[0].astype(F32), hidden_cols)[None]
    scale_three = jnp.concatenate(
        [jnp.full((pairs, 1, PAIR), HEAD_DIM ** (-0.5), F32), jnp.ones((pairs, 2, PAIR), F32)], axis=1
    ).reshape(1, -1)
    vec = jnp.concatenate([norm_gain[0], shifts[0]], axis=0).astype(F32)
    big, wide, hidden_shape = (seq_len, width), (seq_len, head_cols), (seq_len, hidden_cols)

    (qkv,) = call(
        project_kernel, [((seq_len, 3 * head_cols), BF16)], (hb, w_three, bias_three, scale_three), "project", 2.4
    )
    attended = attend_forward(qkv, bias_col, 0, 1, pairs)
    attended, *got_rest = lax.optimization_barrier((attended, *got_rest))
    next_rest = [jnp.concatenate(pair, axis=0) for pair in zip(own_rest, got_rest)]
    attended, late_order, *next_rest = lax.optimization_barrier((attended, deal_order, *next_rest))
    sides_rest = gather_last(next_rest[0], order_one, "ag_rest") + gather_last(
        next_rest[1], order_two, "ag_rest"
    )
    with jax.named_scope("in_cot"):
        cot_own = exchange_in(cotangent, late_order)
    if pairs > 1:
        attended = attend_forward(qkv, bias_col, 1, pairs - 1, pairs, attended)
    context, lse = attended
    context, cot_own, w_down = lax.optimization_barrier((context, cot_own, w_down))
    w_back, w_up = assemble(sides_rest, orders, [head_cols, hidden_cols])
    mid_normed, mid_rstd, mid_low, hidden_low, slope = call(
        middle_kernel,
        [(big, F32), ((seq_len, 1), F32), (big, BF16), (hidden_shape, BF16), (hidden_shape, BF16)],
        (hb, *exchanged_parts(context, w_back, "attn_part"), vec, w_up, bias_up),
        "middle",
        8,
    )

    result, grad_two, grad_two_low, sums_two = call(
        outer_kernel,
        [((half_len, width), BF16), (big, F32), (big, BF16), ((3, width), F32)],
        (
            mid_normed,
            *exchanged_parts(hidden_low, w_down, "ffn_part"),
            cot_own,
            xor_permute(cot_own, "mp", 1),
            vec,
        ),
        "outer",
        4.5,
    )
    out_tokens = exchange_out(result)
    grad_w_down = matmul_tn(grad_two_low, hidden_low).astype(BF16)
    down = Scatter(grad_w_down, [(0, hidden_cols)], [back_one], axes, "rs_down")
    down.deal()
    grad_two_low, down.dealt = lax.optimization_barrier((grad_two_low, down.dealt))
    down.send()
    grad_hidden_low, grad_up_bias = call(
        hidden_grad_kernel,
        [(hidden_shape, BF16), ((1, hidden_cols), F32)],
        (grad_two_low, w_down, slope),
        "hidden_grad",
        3.3,
    )
    parts = exchanged_parts(grad_hidden_low, w_up, "mid_part")
    grad_hidden_low = tie(grad_hidden_low, parts[1])
    grad_w_up = matmul_tn(mid_low, grad_hidden_low).astype(BF16)
    up = Scatter(grad_w_up, [(0, hidden_cols)], [back_two], axes, "rs_up")
    up.deal()
    parts[2], up.dealt = lax.optimization_barrier((parts[2], up.dealt))
    up.send()
    grad_one, grad_one_low, grad_context, sums_one = call(
        inner_kernel,
        [((half_len, width), F32), (big, BF16), (wide, BF16), ((3, width), F32)],
        (grad_two, *parts, mid_normed, mid_rstd, vec, w_back),
        "inner",
        3.5,
    )
    grad_w_back = matmul_tn(grad_one_low, context).astype(BF16)

    down.after(grad_context)
    down.deal()
    grad_context, down.dealt = lax.optimization_barrier((grad_context, down.dealt))
    down.send()
    given = attend_backward(qkv, grad_context, lse, bias_col, 0, 1, pairs)
    up.after(given)
    up.deal()
    given, up.dealt = lax.optimization_barrier((given, up.dealt))
    up.send()
    if pairs > 2:
        given = attend_backward(qkv, grad_context, lse, bias_col, 1, pairs - 2, pairs, given)
    down.after(given)
    down.deal()
    given, down.dealt = lax.optimization_barrier((given, down.dealt))
    down.send()
    if pairs > 1:
        given = attend_backward(qkv, grad_context, lse, bias_col, pairs - 1, 1, pairs, given)
    up.after(given)
    up.deal()
    given, up.dealt = lax.optimization_barrier((given, up.dealt))
    up.send()
    dqkv, pair_sums = given
    grad_w_three = matmul_tn(hb, dqkv).astype(BF16)
    grad_attn = jnp.concatenate([grad_w_three, grad_w_back], axis=1)
    cut_attn = 128 * ((grad_attn.shape[1] // 128 + 1) // 2)
    tail = Scatter(
        grad_attn, [(0, cut_attn), (cut_attn, grad_attn.shape[1])], [back_one, back_two], axes, "rs_attn"
    )
    tail.deal()
    dqkv, tail.dealt = lax.optimization_barrier((dqkv, tail.dealt))
    tail.send()
    keep, sent = call(
        input_grad_kernel,
        [((half_len, width), F32), ((half_len, width), BF16)],
        (dqkv, w_three, grad_one),
        "input_grad",
        2.3,
    )
    grad_in = (keep + xor_permute(sent, "mp", 1).astype(F32)).astype(BF16)
    def spread(v, count):
        full = jnp.zeros(v.shape[:-1] + (2 * count,), F32)
        return lax.dynamic_update_slice_in_dim(full, v, mp_rank * count, v.ndim - 1)

    sums_pair = pair_sums.transpose(1, 0, 2).reshape(2, head_cols)
    small = [
        spread(sums_pair, head_cols),
        spread(grad_up_bias[0], hidden_cols),
        0.5 * jnp.stack([sums_one[0], sums_two[0]]),
        0.5 * jnp.stack([sums_one[2], sums_one[1], sums_two[2], sums_two[1]]),
    ]
    flat = jnp.concatenate([v.reshape(-1, 128) for v in small], axis=0)
    flat = sum_stage(flat, [1], "mp")
    down_sum = down.total()
    up_sum = up.total()
    tail.after(grad_in)
    tail.deal()
    grad_in, down_sum, up_sum, tail.dealt, flat = lax.optimization_barrier(
        (grad_in, down_sum, up_sum, tail.dealt, flat)
    )
    tail.send()
    flat = sum_stage(flat, range(1, 1 << len(low)))
    out_grad = exchange_out(grad_in)
    tail.deal()
    tail.dealt, flat = lax.optimization_barrier((tail.dealt, flat))
    tail.send()
    for shift, size in high:
        flat = sum_stage(flat, [j << shift for j in range(1, size)])
    attn_sum = tail.finish()
    three_sum, back_sum = attn_sum[:, : 3 * head_cols], attn_sum[:, 3 * head_cols :]

    outs, at = [], 0
    for v in small:
        rows = v.size // 128
        outs.append(flat[at : at + rows].reshape((1,) + v.shape))
        at += rows
    attn_bias_out, ffn_bias_out, gain_out, shift_out = outs

    three_out = three_sum.reshape(shard_rows, pairs, 3, PAIR)
    three_out = three_out.transpose(2, 0, 1, 3).reshape(1, 3, shard_rows, head_cols)
    back_out = back_sum.T[None]
    up_out = up_sum[None]
    down_out = down_sum.T[None]
    return (
        out_tokens, out_grad, three_out, back_out, up_out, down_out,
        attn_bias_out, ffn_bias_out, gain_out, shift_out,
    )


def solution(mesh):
    placed = (
        P("mp", "dp", None, None),
        P("mp", "dp", None, None),
        P(),
        P(),
        P(None, None, "dp", "mp"),
        P(None, "mp", "dp"),
        P(None, "dp", "mp"),
        P(None, "mp", "dp"),
        P(),
        P(),
        P(),
        P(),
    )
    return jax.shard_map(
        local,
        mesh=mesh,
        in_specs=placed,
        out_specs=(
            P("mp", "dp", None, None),
            P("mp", "dp", None, None),
            P(None, None, "dp", "mp"),
            P(None, "mp", "dp"),
            P(None, "dp", "mp"),
            P(None, "mp", "dp"),
            P(),
            P(),
            P(),
            P(),
        ),
        check_vma=False,
    )
```

```python
import functools

import jax
import jax.numpy as jnp
from jax import lax
from jax.experimental import pallas as pl
from jax.experimental.pallas import tpu as pltpu
from jax.sharding import PartitionSpec as P

HEAD_DIM = 64
PAIR = 2 * HEAD_DIM

eps_norm = 1e-12
root_half = 0.7071067811865476
inv_root_two_pi = 0.3989422804014327
negative_fill = -1000000000.0
F32 = jnp.float32
BF16 = jnp.bfloat16


def matmul(a, b):
    return lax.dot_general(a, b, (((1,), (0,)), ((), ())), preferred_element_type=F32)


def matmul_nt(a, b):
    return lax.dot_general(a, b, (((1,), (1,)), ((), ())), preferred_element_type=F32)


def gradient(x, y):
    blocks = lax.axis_size("dp")
    if x.shape[1] % (16 * blocks) == 0:
        return Product(x, y, blocks)
    return matmul_tn(x, y).astype(BF16)


def matmul_tn(a, b):
    return lax.dot_general(a, b, (((0,), (0,)), ((), ())), preferred_element_type=F32)


FLOPS_PER_US = 172500000


def cost(us):
    return pl.CostEstimate(flops=int(us * FLOPS_PER_US), transcendentals=0, bytes_accessed=1000)


def xor_permute(x, axis, mask):
    n = lax.axis_size(axis)
    return lax.ppermute(x, axis, [(i, i ^ mask) for i in range(n)])


def dp_axes(n):
    bits = n.bit_length() - 1
    out, at = [], 0
    while at < bits:
        width = 1 if at < 2 else min(2, bits - at)
        out.append((at, 1 << width))
        at += width
    return out[::-1]


def stage_parts(x, shift, size):
    return [x] + [xor_permute(x, "dp", j << shift) for j in range(1, size)]


def stage_gather(x, axis, shift, size):
    return jnp.concatenate(stage_parts(x, shift, size), axis=0)


def assemble_kernel(count, orders, cuts, *refs):
    me = lax.axis_index("dp")
    sources = [(refs[2 * i], refs[2 * i + 1]) for i in range(len(orders))]
    targets = refs[2 * len(orders) :]

    @pl.loop(0, count)
    def _(block):
        place = lax.bitwise_xor(me, block)
        at = 0
        for (own, received), order in zip(sources, orders):
            spot, stride = 0, 1
            for shift, size in order[:-1]:
                spot = spot + stride * lax.bitwise_and(lax.shift_right_logical(place, shift), size - 1)
                stride *= size
            side = lax.bitwise_and(lax.shift_right_logical(place, order[-1][0]), 1)
            cols = own.shape[2]

            def write(source, at=at, cols=cols, spot=spot):
                start = 0
                for target, (low, high) in zip(targets, cuts):
                    first, last = max(low, at), min(high, at + cols)
                    if first < last:
                        target[block, :, first - low : last - low] = source[spot, :, first - at : last - at]

            @pl.when(side == 0)
            def _():
                write(own)

            @pl.when(side == 1)
            def _():
                write(received)

            at += cols


def tie(x, *others):
    return lax.optimization_barrier((x,) + others)[0]


def gather_first(x, order, name):
    with jax.named_scope(name + "_first"):
        y = x[None]
        for shift, size in order[:-2]:
            y = stage_gather(y, "dp", shift, size)
        return y


def gather_next(y, order, name):
    with jax.named_scope(name + "_next"):
        return stage_gather(y, "dp", *order[-2])


def gather_last(y, order, name):
    with jax.named_scope(name + "_last"):
        return [y, xor_permute(y, "dp", 1 << order[-1][0])]


def assemble(sides, orders, widths):
    count = lax.axis_size("dp")
    rows = sides[0].shape[1]
    cuts, at = [], 0
    for w in widths:
        cuts.append((at, at + w))
        at += w
    vmem = pl.BlockSpec(memory_space=pltpu.VMEM)
    outs = pl.pallas_call(
        functools.partial(assemble_kernel, count, tuple(tuple(o) for o in orders), tuple(cuts)),
        out_shape=tuple(jax.ShapeDtypeStruct((count, rows, w), sides[0].dtype) for w in widths),
        in_specs=[vmem] * len(sides),
        out_specs=(vmem,) * len(widths),
        compiler_params=pltpu.CompilerParams(vmem_limit_bytes=6 << 20),
        cost_estimate=cost(1.0),
        name="assemble",
    )(*sides)
    return [o.reshape(count * rows, -1) for o in outs]


class Product:
    def __init__(self, x, y, blocks):
        self.x, self.y = x, y
        self.shape = (blocks, x.shape[1] // blocks, y.shape[1])
        self.size = x.shape[1] * y.shape[1]


def route_kernel(plan, kinds, count_out, *refs):
    me = lax.axis_index("dp")
    ins, outs, refs = [], [], list(refs)
    for is_product in kinds:
        ins.append((refs.pop(0), refs.pop(0)) if is_product else refs.pop(0))
    outs, made = refs[:count_out], refs[count_out:]
    for index, is_product in enumerate(kinds):
        if is_product:
            x_ref, y_ref = ins[index]
            ins[index] = made.pop(0)
            ins[index][...] = matmul_tn(x_ref[...], y_ref[...]).astype(BF16).reshape(ins[index].shape)
    for pieces, sizes, at, shift, grouped in plan:
        size = sizes[at]
        inner = 1
        for extent in sizes[at + 1 :]:
            inner *= extent
        rest = inner
        for extent in sizes[:at]:
            rest *= extent
        coord = lax.bitwise_and(lax.shift_right_logical(me, shift), size - 1)
        log_inner = inner.bit_length() - 1
        if grouped:
            whole = outs.pop(0)
            targets = [whole.at[j * rest : (j + 1) * rest] for j in range(size)]
        else:
            targets = [outs.pop(0) for _ in range(size)]
        for j, target in enumerate(targets):
            side = j if grouped else lax.bitwise_xor(coord, j)

            @pl.loop(0, rest)
            def _(r, target=target, side=side):
                upper = lax.shift_right_logical(r, log_inner)
                source = (upper * size + side) * inner + lax.bitwise_and(r, inner - 1)
                col = 0
                for piece in pieces:
                    width = piece[0][2] - piece[0][1]
                    first, low, high = piece[0]
                    value = ins[first][source, :, low:high]
                    if len(piece) > 1:
                        value = value.astype(F32)
                        for index, low, high in piece[1:]:
                            value = value + ins[index][source, :, low:high].astype(F32)
                    target[r, :, col : col + width] = value.astype(BF16)
                    col += width


def route(groups, name, grouped=False):
    arrays, plan, shapes = [], [], []
    for pieces, left, axis in groups:
        entries = []
        for piece in pieces:
            entry = []
            for array, low, high in piece:
                known = [i for i, other in enumerate(arrays) if other is array]
                if not known:
                    known = [len(arrays)]
                    arrays.append(array)
                entry.append((known[0], low, high))
            entries.append(tuple(entry))
        at = left.index(axis)
        plan.append((tuple(entries), tuple(size for _, size in left), at, axis[0], grouped))
        total = sum(piece[0][2] - piece[0][1] for piece in pieces)
        array = pieces[0][0][0]
        if grouped:
            shapes.append((1, (array.shape[0], array.shape[1], total)))
        else:
            shapes.append((axis[1], (array.shape[0] // axis[1], array.shape[1], total)))
    vmem = pl.BlockSpec(memory_space=pltpu.VMEM)
    out_shape = [jax.ShapeDtypeStruct(shape, BF16) for size, shape in shapes for _ in range(size)]
    kinds = tuple(isinstance(array, Product) for array in arrays)
    operands, scratch = [], []
    for array, is_product in zip(arrays, kinds):
        operands += [array.x, array.y] if is_product else [array]
        if is_product:
            scratch.append(pltpu.VMEM(array.shape, BF16))
    flat = pl.pallas_call(
        functools.partial(route_kernel, tuple(plan), kinds, len(out_shape)),
        out_shape=out_shape,
        in_specs=[vmem] * len(operands),
        out_specs=[vmem] * len(out_shape),
        scratch_shapes=scratch,
        compiler_params=pltpu.CompilerParams(vmem_limit_bytes=(20 if scratch else 6) << 20),
        cost_estimate=cost(1.0),
        name=name,
    )(*operands)
    outs = []
    for size, _ in shapes:
        outs.append(list(flat[:size]))
        flat = flat[size:]
    return outs


class Scatter:
    def __init__(self, arrays, orders, axes, name, group_last=False):
        self.group_last = group_last
        n = lax.axis_size("dp")
        self.name = name
        self.orders = [list(o) for o in orders]
        self.lefts = [list(axes) for _ in orders]
        self.pieces = []
        shaped = {}
        for parts in arrays:
            pieces = []
            if parts is None:
                self.pieces.append(None)
                continue
            for g, low, high in parts:
                if id(g) not in shaped:
                    shaped[id(g)] = g if isinstance(g, Product) else g.reshape(n, g.shape[0] // n, g.shape[1])
                pieces.append([(shaped[id(g)], low, high)])
            self.pieces.append(pieces)
        self.count = 0

    def deal(self):
        self.count += 1
        merged = len(self.pieces) > 1 and len(self.lefts[0]) < 3 and self.lefts[0] == self.lefts[1]
        groups = []
        if merged:
            groups.append((sum(self.pieces, []), self.lefts[0], self.orders[0][0]))
            self.orders, self.lefts = self.orders[:1], self.lefts[:1]
        else:
            for parts, left, order in zip(self.pieces, self.lefts, self.orders):
                groups.append((parts, left, order[0]))
        self.grouped = self.group_last and len(groups) == 1 and len(self.lefts[0]) == 1
        self.dealt = route(groups, f"{self.name}_deal_{self.count}", self.grouped)
        return self.dealt

    def send(self):
        pieces, lefts, orders = [], [], []
        for parts, left, order in zip(self.dealt, self.lefts, self.orders):
            shift, size = order[0]
            with jax.named_scope(f"{self.name}_{self.count}"):
                if self.grouped:
                    n = lax.axis_size("dp")
                    members = [[i | (j << shift) for j in range(size)] for i in range(n) if not (i >> shift) % size]
                    whole = lax.all_to_all(
                        parts[0], "dp", split_axis=0, concat_axis=0, axis_index_groups=members, tiled=True
                    )
                    rest = whole.shape[0] // size
                    got = [whole[j * rest : (j + 1) * rest] for j in range(size)]
                else:
                    got = [parts[0]] + [
                        xor_permute(parts[j], "dp", j << shift) for j in range(1, size)
                    ]
            pieces.append([[(x, 0, x.shape[2]) for x in got]])
            lefts.append([axis for axis in left if axis != order[0]])
            orders.append(order[1:])
        self.pieces, self.lefts, self.orders = pieces, lefts, orders

    def set_part(self, i, parts):
        self.pieces[i] = Scatter([parts], [self.orders[i]], self.lefts[i], self.name).pieces[0]

    def deal_one(self, i):
        return route([(self.pieces[i], self.lefts[i], self.orders[i][0])], f"{self.name}_deal_1{i}")[0]

    def send_one(self, i, parts):
        self.count = 1
        shift, size = self.orders[i][0]
        with jax.named_scope(f"{self.name}_1{i}"):
            got = [parts[0]] + [xor_permute(parts[j], "dp", j << shift) for j in range(1, size)]
        self.pieces[i] = [[(x, 0, x.shape[2]) for x in got]]
        self.lefts[i] = [axis for axis in self.lefts[i] if axis != self.orders[i][0]]
        self.orders[i] = self.orders[i][1:]

    def after(self, *others):
        arrays = [x for (piece,) in self.pieces for x, _, _ in piece[1:]]
        arrays = list(lax.optimization_barrier((tuple(arrays), others))[0])
        self.pieces = [
            [[piece[0]] + [(arrays.pop(0), low, high) for _, low, high in piece[1:]]] for (piece,) in self.pieces
        ]

    def before(self, x):
        arrays = [y for (piece,) in self.pieces for y, _, _ in piece]
        x, arrays = lax.optimization_barrier((x, tuple(arrays)))
        arrays = list(arrays)
        self.pieces = [[[(arrays.pop(0), low, high) for _, low, high in piece]] for (piece,) in self.pieces]
        return x

    def total(self):
        outs = []
        for (piece,) in self.pieces:
            parts = [x[0].astype(F32) for x, _, _ in piece]
            while len(parts) > 1:
                parts = [parts[i] + parts[i + 1] for i in range(0, len(parts), 2)]
            outs.append(parts[0])
        return outs[0] if len(outs) == 1 else jnp.concatenate(outs, axis=1)

    def finish_stages(self):
        while self.orders[0]:
            self.deal()
            self.send()

    def finish(self):
        self.finish_stages()
        return self.total()


def attend_forward_kernel(block, qkv_ref, bias_ref, *refs):
    ctx_ref, lse_ref = refs[-2:]
    length = qkv_ref.shape[0]
    bias = bias_ref[...]
    for head in range(2):
        low = head * HEAD_DIM
        keys = qkv_ref[:, PAIR + low : PAIR + low + HEAD_DIM]
        values_t = qkv_ref[:, 2 * PAIR + low : 2 * PAIR + low + HEAD_DIM].T
        for start in range(0, length, block):
            queries = qkv_ref[start : start + block, low : low + HEAD_DIM]
            scores = matmul_nt(keys, queries) + bias
            top = jnp.max(scores, axis=0, keepdims=True)
            exponent = jnp.exp(scores - top)
            total = jnp.sum(exponent, axis=0, keepdims=True)
            context_t = matmul(values_t, exponent.astype(BF16)) * (1.0 / total)
            ctx_ref[start : start + block, low : low + HEAD_DIM] = context_t.T.astype(BF16)
            lse_ref[0, head : head + 1, start : start + block] = top + jnp.log(total)


def attend_forward(qkv, bias, first, pairs, total, known=()):
    length = qkv.shape[0]
    return pl.pallas_call(
        functools.partial(attend_forward_kernel, min(256, length)),
        grid=(pairs,),
        out_shape=(
            jax.ShapeDtypeStruct((length, total * PAIR), BF16),
            jax.ShapeDtypeStruct((total, 2, length), F32),
        ),
        in_specs=[
            pl.BlockSpec((length, 3 * PAIR), lambda p: (0, p + first)),
            pl.BlockSpec((length, 1), lambda p: (0, 0)),
        ]
        + [pl.BlockSpec(memory_space=pl.ANY)] * len(known),
        out_specs=(
            pl.BlockSpec((length, PAIR), lambda p: (0, p + first)),
            pl.BlockSpec((1, 2, length), lambda p: (p + first, 0, 0)),
        ),
        input_output_aliases={2: 0, 3: 1} if known else {},
        compiler_params=pltpu.CompilerParams(vmem_limit_bytes=10 << 20),
        cost_estimate=cost(5.9 * pairs),
        name="attend_forward",
    )(qkv, bias, *known)


def attend_backward_kernel(block, qkv_ref, dctx_ref, lse_ref, bias_ref, *refs):
    out_ref, sums_ref, dk_ref, dv_ref = refs[-4:]
    length = qkv_ref.shape[0]
    bias = bias_ref[...]
    for head in range(2):
        low = head * HEAD_DIM
        keys = qkv_ref[:, PAIR + low : PAIR + low + HEAD_DIM]
        keys_t = keys.T
        values = qkv_ref[:, 2 * PAIR + low : 2 * PAIR + low + HEAD_DIM]
        query_sum = jnp.zeros((1, HEAD_DIM), F32)
        for start in range(0, length, block):
            queries = qkv_ref[start : start + block, low : low + HEAD_DIM]
            grads = dctx_ref[start : start + block, low : low + HEAD_DIM]
            lse = lse_ref[0, head : head + 1, start : start + block]
            probs = jnp.exp(matmul_nt(keys, queries) + bias - lse)
            grad_probs = matmul_nt(values, grads)
            inner = jnp.sum(probs * grad_probs, axis=0, keepdims=True)
            grad_scores = (probs * (grad_probs - inner)).astype(BF16)
            dv = matmul(probs.astype(BF16), grads)
            dk = matmul(grad_scores, queries)
            if start == 0:
                dk_ref[...] = dk
                dv_ref[...] = dv
            else:
                dk_ref[...] += dk
                dv_ref[...] += dv
            dq = (matmul(keys_t, grad_scores) * HEAD_DIM ** (-0.5)).T
            query_sum = query_sum + jnp.sum(dq, axis=0, keepdims=True)
            out_ref[start : start + block, low : low + HEAD_DIM] = dq.astype(BF16)
        dk = dk_ref[...]
        dv = dv_ref[...]
        out_ref[:, PAIR + low : PAIR + low + HEAD_DIM] = dk.astype(BF16)
        out_ref[:, 2 * PAIR + low : 2 * PAIR + low + HEAD_DIM] = dv.astype(BF16)
        sums_ref[0, 0:1, low : low + HEAD_DIM] = query_sum
        sums_ref[0, 1:2, low : low + HEAD_DIM] = jnp.sum(dv, axis=0, keepdims=True)


def attend_backward(qkv, dctx, lse, bias, first, pairs, total, known=()):
    length = qkv.shape[0]
    return pl.pallas_call(
        functools.partial(attend_backward_kernel, min(256, length)),
        grid=(pairs,),
        out_shape=(
            jax.ShapeDtypeStruct((length, total * 3 * PAIR), BF16),
            jax.ShapeDtypeStruct((total, 2, PAIR), F32),
        ),
        in_specs=[
            pl.BlockSpec((length, 3 * PAIR), lambda p: (0, p + first)),
            pl.BlockSpec((length, PAIR), lambda p: (0, p + first)),
            pl.BlockSpec((1, 2, length), lambda p: (p + first, 0, 0)),
            pl.BlockSpec((length, 1), lambda p: (0, 0)),
        ]
        + [pl.BlockSpec(memory_space=pl.ANY)] * len(known),
        out_specs=(
            pl.BlockSpec((length, 3 * PAIR), lambda p: (0, p + first)),
            pl.BlockSpec((1, 2, PAIR), lambda p: (p + first, 0, 0)),
        ),
        input_output_aliases={4: 0, 5: 1} if known else {},
        scratch_shapes=[pltpu.VMEM((length, HEAD_DIM), F32), pltpu.VMEM((length, HEAD_DIM), F32)],
        compiler_params=pltpu.CompilerParams(vmem_limit_bytes=10 << 20),
        cost_estimate=cost(7.3 * pairs),
        name="attend_backward",
    )(qkv, dctx, lse, bias, *known)


def call(kernel, outs, args, name, us, vmem_mib=10, scratch=()):
    spec = pl.BlockSpec(memory_space=pltpu.VMEM)
    return pl.pallas_call(
        kernel,
        out_shape=[jax.ShapeDtypeStruct(shape, kind) for shape, kind in outs],
        in_specs=[spec] * len(args),
        out_specs=[spec] * len(outs),
        scratch_shapes=list(scratch),
        compiler_params=pltpu.CompilerParams(vmem_limit_bytes=vmem_mib << 20),
        cost_estimate=cost(us),
        name=name,
    )(*args)


def row_blocks(rows, block):
    block = min(block, rows)
    return rows // block, block


def rows_at(i, block):
    return pl.ds(pl.multiple_of(i * block, block), block)


def project_kernel(x_ref, w_ref, bias_ref, scale_ref, out_ref):
    count, block = row_blocks(x_ref.shape[0], 512)

    @pl.loop(0, count)
    def _(i):
        at = rows_at(i, block)
        out_ref[at, :] = ((matmul(x_ref[at, :], w_ref[...]) + bias_ref[...]) * scale_ref[...]).astype(BF16)


def part_kernel(low, high, x_ref, w_ref, out_ref):
    out_ref[...] = matmul_nt(x_ref[low:high, :], w_ref[...]).astype(BF16)


def exchanged_parts(x, w, name):
    half = x.shape[0] // 2
    own, got = [], []
    for number in range(2):
        (part,) = call(
            functools.partial(part_kernel, number * half, (number + 1) * half),
            [((half, w.shape[0]), BF16)],
            (x, w),
            f"{name}_{number}",
            1.5,
        )
        if number == 0:
            x = tie(x, part)
        own.append(part)
        with jax.named_scope(f"{name}_{number}"):
            got.append(xor_permute(part, "mp", 1))
    return own + got[::-1]


def halves(parts, body, rows, block):
    count, block = row_blocks(rows // 2, block)
    for number in range(2):
        own_ref, got_ref = parts[number], parts[2 + number]

        @pl.loop(0, count)
        def _(i, number=number, own_ref=own_ref, got_ref=got_ref):
            at = rows_at(i, block)
            total = own_ref[at, :].astype(F32) + got_ref[at, :].astype(F32)
            body(number, at, rows_at(i + number * count, block), total)


def middle_kernel(x_ref, p0, p1, p2, p3, vec_ref, w_ref, bias_ref, normed_ref, rstd_ref, low_ref, act_ref, slope_ref):
    def body(number, half_at, at, total):
        mixed = x_ref[at, :].astype(F32) + total + vec_ref[2:3, :]
        normed, rstd = norm_forward(mixed)
        normed_ref[at, :] = normed.astype(BF16)
        rstd_ref[at, :] = rstd
        low = (normed * vec_ref[0:1, :] + vec_ref[3:4, :]).astype(BF16)
        low_ref[at, :] = low
        u = matmul(low, w_ref[...]) + bias_ref[...]
        half_cdf = 0.5 * (1.0 + lax.erf(u * root_half))
        act_ref[at, :] = (u * half_cdf).astype(BF16)
        slope_ref[at, :] = (half_cdf + u * jnp.exp(-0.5 * u * u) * inv_root_two_pi).astype(BF16)

    halves((p0, p1, p2, p3), body, x_ref.shape[0], 256)


def outer_kernel(normed_ref, p0, p1, p2, p3, cot_own_ref, cot_got0, cot_got1, vec_ref, out_ref, low_ref, sums_ref, cot_ref):
    sums_ref[...] = jnp.zeros_like(sums_ref)

    half = cot_own_ref.shape[0]
    for index, source in enumerate((cot_own_ref, cot_got0, cot_got1)):
        low = 0 if index == 0 else half + (index - 1) * (half // 2)
        cot_ref[low : low + source.shape[0], :] = source[...]

    def body(number, half_at, at, total):
        mixed = normed_ref[at, :].astype(F32) * vec_ref[0:1, :] + vec_ref[3:4, :] + total + vec_ref[4:5, :]
        normed, rstd = norm_forward(mixed)
        if number == 0:
            out_ref[at, :] = (normed * vec_ref[1:2, :] + vec_ref[5:6, :]).astype(BF16)
        cot = cot_ref[at, :].astype(F32)
        grad, grad_gain, grad_shift = norm_backward(cot, normed, rstd, vec_ref[1:2, :])
        low_ref[at, :] = grad.astype(BF16)
        sums_ref[0:1, :] += grad_gain
        sums_ref[1:2, :] += grad_shift
        sums_ref[2:3, :] += jnp.sum(grad, axis=0, keepdims=True)

    halves((p0, p1, p2, p3), body, normed_ref.shape[0], 256)


def hidden_grad_kernel(grad_ref, w_ref, slope_ref, out_ref, sums_ref):
    count, block = row_blocks(grad_ref.shape[0], 256)
    sums_ref[...] = jnp.zeros_like(sums_ref)

    @pl.loop(0, count)
    def _(i):
        at = rows_at(i, block)
        grad = matmul(grad_ref[at, :], w_ref[...]) * slope_ref[at, :].astype(F32)
        out_ref[at, :] = grad.astype(BF16)
        sums_ref[...] += jnp.sum(grad, axis=0, keepdims=True)


def inner_kernel(
    grad_in_ref, p0, p1, p2, p3, normed_ref, rstd_ref, vec_ref, w_ref, own_grad_ref, low_ref, ctx_ref, sums_ref
):
    sums_ref[...] = jnp.zeros_like(sums_ref)

    def body(number, half_at, at, total):
        given = grad_in_ref[at, :].astype(F32) + total
        grad, grad_gain, grad_shift = norm_backward(given, normed_ref[at, :].astype(F32), rstd_ref[at, :], vec_ref[0:1, :])
        low = grad.astype(BF16)
        low_ref[at, :] = low
        ctx_ref[at, :] = matmul(low, w_ref[...]).astype(BF16)
        sums_ref[0:1, :] += grad_gain
        sums_ref[1:2, :] += grad_shift
        sums_ref[2:3, :] += jnp.sum(grad, axis=0, keepdims=True)
        if number == 0:
            own_grad_ref[at, :] = grad

    halves((p0, p1, p2, p3), body, normed_ref.shape[0], 256)


def input_grad_kernel(x_ref, w_ref, grad_ref, keep_ref, send_ref):
    half = keep_ref.shape[0]
    send_ref[...] = matmul_nt(x_ref[half:, :], w_ref[...]).astype(BF16)
    keep_ref[...] = grad_ref[...] + matmul_nt(x_ref[:half, :], w_ref[...])


def norm_forward(rows):
    center = rows - jnp.mean(rows, axis=1, keepdims=True)
    rstd = lax.rsqrt(jnp.mean(center * center, axis=1, keepdims=True) + eps_norm)
    return center * rstd, rstd


def norm_backward(grad, normed, rstd, gain):
    scaled = grad * gain
    inner = (
        scaled
        - jnp.mean(scaled, axis=1, keepdims=True)
        - normed * jnp.mean(scaled * normed, axis=1, keepdims=True)
    )
    return (
        rstd * inner,
        jnp.sum(grad * normed, axis=0, keepdims=True),
        jnp.sum(grad, axis=0, keepdims=True),
    )


def from_other(x):
    half = x.shape[0] // 2
    return [xor_permute(x[:half], "mp", 1), xor_permute(x[half:], "mp", 1)]


def exchange_in(x, deal_order, *others):
    dealt = x[0].at[:, deal_order].get(mode="promise_in_bounds").transpose(1, 0, 2)
    if others:
        dealt = tie(dealt, *others)
    arrived = lax.all_to_all(dealt, "dp", split_axis=0, concat_axis=0, tiled=True)
    return arrived.reshape(-1, x.shape[3])


def exchange_out(rows, extra):
    n = lax.axis_size("dp")
    with jax.named_scope("out_rows"):
        blocks = rows.reshape(n, rows.shape[0] // n, rows.shape[1])
        blocks = jnp.concatenate([blocks, jnp.broadcast_to(extra, (n,) + extra.shape)], axis=1)
        sent = lax.all_to_all(blocks, "dp", split_axis=0, concat_axis=0, tiled=True)
        count = rows.shape[0] // n
        return sent[:, :count].transpose(1, 0, 2)[None], sent[:, count:]


def put_split(out_ref, row, count, value):
    high = value.astype(BF16)
    out_ref[row : row + 1, :] = high
    out_ref[row + count : row + count + 1, :] = (value - high.astype(F32)).astype(BF16)


def early_kernel(one_ref, two_ref, up_ref, out_ref):
    first = lax.axis_index("mp") == 0
    width = one_ref.shape[1]
    pieces = up_ref.shape[1] // width
    count = 3 + pieces
    out_ref[...] = jnp.zeros_like(out_ref)
    for row in range(3):
        put_split(out_ref, row, count, jnp.where(first, one_ref[row : row + 1, :], two_ref[row : row + 1, :]))
    for piece in range(pieces):
        put_split(out_ref, 3 + piece, count, up_ref[0:1, piece * width : (piece + 1) * width])


def late_kernel(pairs, keep_ref, g0, g1, sums_ref, rows_ref, out_ref):
    half = keep_ref.shape[0] // 2
    for index, source in enumerate((g0, g1)):
        at = slice(index * half, (index + 1) * half)
        rows_ref[at, :] = (keep_ref[at, :] + source[...].astype(F32)).astype(BF16)
    out_ref[...] = jnp.zeros_like(out_ref)
    for which in range(2):
        for pair in range(pairs):
            col = (which * pairs + pair) * PAIR
            value = sums_ref[pair, which : which + 1, :]
            high = value.astype(BF16)
            out_ref[0:1, col : col + PAIR] = high
            out_ref[1:2, col : col + PAIR] = (value - high.astype(F32)).astype(BF16)


def gathered_kernel(count, x_ref, out_ref):
    out_ref[...] = jnp.zeros_like(out_ref)

    @pl.loop(0, x_ref.shape[0])
    def _(i):
        x = x_ref[i].astype(F32)
        out_ref[...] += x[:count, :] + x[count : 2 * count, :]


def local(
    tokens, cotangent, lengths, deal_order, attn_in, attn_out, ffn_in, ffn_out,
    attn_bias, ffn_bias, norm_gain, shifts,
):
    dp_size = lax.axis_size("dp")
    mp_rank = lax.axis_index("mp")
    dp_rank = lax.axis_index("dp")
    axes = dp_axes(dp_size)
    low = axes[-2:]
    high = axes[:-2]
    order_one = high + low
    order_two = high + low[::-1]
    back_one = low[::-1] + high[::-1]
    back_two = low + high[::-1]

    width = tokens.shape[3]
    half_len = tokens.shape[1] * dp_size
    seq_len = 2 * half_len
    head_cols = attn_in.shape[3]
    hidden_cols = ffn_in.shape[2]
    pairs = head_cols // PAIR
    shard_rows = attn_in.shape[2]

    three = attn_in[0].reshape(3, shard_rows, pairs, PAIR).transpose(1, 2, 0, 3)
    three = three.reshape(shard_rows, 3 * head_cols)
    back_t = attn_out[0].T
    up = ffn_in[0]
    down_t = ffn_out[0].T

    cut_three = 128 * ((3 * head_cols // 128 + 1) // 2)
    pieces_three = [three[:, :cut_three], three[:, cut_three:]]
    rest = jnp.concatenate([back_t, up], axis=1)
    cut_rest = 128 * ((rest.shape[1] // 128 + 1) // 2)
    orders = [tuple(order_one), tuple(order_two)]

    first_three = gather_first(three, order_one, "ag_three")
    with jax.named_scope("in_tokens"):
        tok_own = exchange_in(tokens, deal_order, first_three)
    w_down = lax.all_gather(down_t, "dp", axis=0, tiled=True)
    next_three = [
        gather_next(first_three[:, :, :cut_three], order_one, "ag_three"),
        gather_next(first_three[:, :, cut_three:], order_two, "ag_three"),
    ]
    rest, *next_three = lax.optimization_barrier((rest, *next_three))
    with jax.named_scope("ag_rest_first"):
        first_got = [rest[None]]
        for shift, size in order_one[:-3]:
            first_got = [stage_gather(x, "dp", shift, size) for x in first_got]
        shift, size = order_one[-3]
        first_own = first_got[0]
        first_got = [xor_permute(first_own, "dp", j << shift) for j in range(1, size)]
    sides_three = gather_last(next_three[0], order_one, "ag_three") + gather_last(
        next_three[1], order_two, "ag_three"
    )
    (w_three,) = assemble(sides_three, orders, [3 * head_cols])
    hb = jnp.concatenate([tok_own] + from_other(tok_own), axis=0)
    length = lengths[deal_order[dp_rank]]
    place = jnp.arange(seq_len, dtype=jnp.int32)
    place = jnp.where(mp_rank == 0, place, (place + half_len) % seq_len)
    bias_col = jnp.where(place < length, 0.0, negative_fill).astype(F32)[:, None]

    def own_cols(v, count):
        return jnp.where(mp_rank == 0, v[..., :count], v[..., count:])

    bias_pair = own_cols(attn_bias[0].astype(F32), head_cols).reshape(2, pairs, PAIR)
    bias_three = jnp.stack([bias_pair[0], jnp.zeros_like(bias_pair[0]), bias_pair[1]], axis=1).reshape(1, -1)
    bias_up = own_cols(ffn_bias[0].astype(F32), hidden_cols)[None]
    scale_three = jnp.concatenate(
        [jnp.full((pairs, 1, PAIR), HEAD_DIM ** (-0.5), F32), jnp.ones((pairs, 2, PAIR), F32)], axis=1
    ).reshape(1, -1)
    vec = jnp.concatenate([norm_gain[0], shifts[0]], axis=0).astype(F32)
    hb, bias_up, vec, bias_col = lax.optimization_barrier((hb, bias_up, vec, bias_col))
    big, wide, hidden_shape = (seq_len, width), (seq_len, head_cols), (seq_len, hidden_cols)

    first_rest = jnp.concatenate([first_own] + first_got, axis=0)
    w_three, first_rest = lax.optimization_barrier((w_three, first_rest))
    (qkv,) = call(
        project_kernel, [((seq_len, 3 * head_cols), BF16)], (hb, w_three, bias_three, scale_three), "project", 2.4
    )
    own_rest = [first_rest[:, :, :cut_rest], first_rest[:, :, cut_rest:]]
    with jax.named_scope("ag_rest_next"):
        got_rest = [xor_permute(y, "dp", 1 << o[-2][0]) for y, o in zip(own_rest, orders)]

    attended = attend_forward(qkv, bias_col, 0, 1, pairs)
    attended, *got_rest = lax.optimization_barrier((attended, *got_rest))
    next_rest = [jnp.concatenate(pair, axis=0) for pair in zip(own_rest, got_rest)]
    attended, *next_rest = lax.optimization_barrier((attended, *next_rest))
    sides_rest = gather_last(next_rest[0], order_one, "ag_rest") + gather_last(
        next_rest[1], order_two, "ag_rest"
    )
    with jax.named_scope("in_cot"):
        cot_own = exchange_in(cotangent, deal_order, *next_rest)
    if pairs > 1:
        attended = attend_forward(qkv, bias_col, 1, pairs - 1, pairs, attended)
    context, lse = attended
    context, cot_own, w_down = lax.optimization_barrier((context, cot_own, w_down))
    w_back, w_up = assemble(sides_rest, orders, [head_cols, hidden_cols])
    mid_normed, mid_rstd, mid_low, hidden_low, slope = call(
        middle_kernel,
        [(big, BF16), ((seq_len, 1), F32), (big, BF16), (hidden_shape, BF16), (hidden_shape, BF16)],
        (hb, *exchanged_parts(context, w_back, "attn_part"), vec, w_up, bias_up),
        "middle",
        8,
    )

    result, grad_two_low, sums_two = call(
        outer_kernel,
        [((half_len, width), BF16), (big, BF16), ((3, width), F32)],
        (
            mid_normed,
            *exchanged_parts(hidden_low, w_down, "ffn_part"),
            cot_own,
            *from_other(cot_own),
            vec,
        ),
        "outer",
        4.5,
        scratch=[pltpu.VMEM(big, BF16)],
    )
    ffn = Scatter(
        [[(gradient(grad_two_low, hidden_low), 0, hidden_cols)], None], [back_one, back_two], axes, "rs_ffn"
    )
    dealt = ffn.deal_one(0)
    grad_two_low, dealt = lax.optimization_barrier((grad_two_low, dealt))
    ffn.send_one(0, dealt)
    grad_hidden_low, grad_up_bias = call(
        hidden_grad_kernel,
        [(hidden_shape, BF16), ((1, hidden_cols), F32)],
        (grad_two_low, w_down, slope),
        "hidden_grad",
        3.3,
    )
    parts = exchanged_parts(grad_hidden_low, w_up, "mid_part")
    grad_hidden_low = tie(grad_hidden_low, parts[1])
    ffn.set_part(1, [(gradient(mid_low, grad_hidden_low), 0, hidden_cols)])
    dealt = ffn.deal_one(1)
    parts[2], dealt = lax.optimization_barrier((parts[2], dealt))
    ffn.send_one(1, dealt)
    grad_one, grad_one_low, grad_context, sums_one = call(
        inner_kernel,
        [((half_len, width), F32), (big, BF16), (wide, BF16), ((3, width), F32)],
        (grad_two_low, *parts, mid_normed, mid_rstd, vec, w_back),
        "inner",
        3.5,
    )
    early_count = 3 + hidden_cols // width
    (early,) = call(
        early_kernel, [((16 * -(-2 * early_count // 16), width), BF16)], (sums_one, sums_two, grad_up_bias), "early", 0.5
    )
    out_tokens, early_all = exchange_out(result, early)
    grad_w_back = gradient(grad_one_low, context)

    given = attend_backward(qkv, grad_context, lse, bias_col, 0, 1, pairs)
    ffn.after(given)
    ffn.deal()
    given, ffn.dealt = lax.optimization_barrier((given, ffn.dealt))
    ffn.send()
    if pairs > 2:
        given = attend_backward(qkv, grad_context, lse, bias_col, 1, pairs - 2, pairs, given)
    ffn.after(given)
    ffn.deal()
    given, ffn.dealt = lax.optimization_barrier((given, ffn.dealt))
    ffn.send()
    if pairs > 1:
        given = attend_backward(qkv, grad_context, lse, bias_col, pairs - 1, 1, pairs, given)
    dqkv, pair_sums = given
    grad_w_three = gradient(hb, dqkv)
    cut = 128 * ((4 * head_cols // 128 + 1) // 2)
    tail = Scatter(
        [
            [(grad_w_three, 0, cut)],
            [(grad_w_three, cut, 3 * head_cols), (grad_w_back, 0, head_cols)],
        ],
        [back_one, back_two],
        axes,
        "rs_attn",
    )
    tail.deal()
    dqkv, tail.dealt = lax.optimization_barrier((dqkv, tail.dealt))
    tail.dealt = ffn.before(tail.dealt)
    tail.send()
    keep, sent = call(
        input_grad_kernel,
        [((half_len, width), F32), ((half_len, width), BF16)],
        (dqkv, w_three, grad_one),
        "input_grad",
        2.3,
    )
    got = from_other(sent)
    grad_in, late = call(
        functools.partial(late_kernel, pairs),
        [((half_len, width), BF16), ((8, 2 * head_cols), BF16)],
        (keep, *got, pair_sums),
        "late",
        1.0,
    )
    out_grad, late_all = exchange_out(grad_in, late)
    ffn_sum = ffn.finish()
    down_sum, up_sum = ffn_sum[:, :hidden_cols], ffn_sum[:, hidden_cols:]
    attn_sum = tail.finish()
    three_sum, back_sum = attn_sum[:, : 3 * head_cols], attn_sum[:, 3 * head_cols :]

    (early_sum,) = call(
        functools.partial(gathered_kernel, early_count), [((early_count, width), F32)], (early_all,), "early_sum", 0.5
    )
    (late_sum,) = call(functools.partial(gathered_kernel, 1), [((1, width), F32)], (late_all,), "late_sum", 0.5)

    def in_order(own):
        other = xor_permute(own, "mp", 1)
        return jnp.where(mp_rank == 0, own, other), jnp.where(mp_rank == 0, other, own)

    low_early, high_early = in_order(early_sum)
    low_late, high_late = in_order(late_sum)
    gain_out = jnp.stack([low_early[0], high_early[0]])[None]
    shift_out = jnp.stack([low_early[2], low_early[1], high_early[2], high_early[1]])[None]
    ffn_bias_out = jnp.concatenate([low_early[3:].reshape(1, -1), high_early[3:].reshape(1, -1)], axis=1)
    attn_bias_out = jnp.concatenate(
        [low_late.reshape(1, 2, head_cols), high_late.reshape(1, 2, head_cols)], axis=2
    )

    three_out = three_sum.reshape(shard_rows, pairs, 3, PAIR)
    three_out = three_out.transpose(2, 0, 1, 3).reshape(1, 3, shard_rows, head_cols)
    back_out = back_sum.T[None]
    up_out = up_sum[None]
    down_out = down_sum.T[None]
    return (
        out_tokens, out_grad, three_out, back_out, up_out, down_out,
        attn_bias_out, ffn_bias_out, gain_out, shift_out,
    )


def solution(mesh):
    placed = (
        P("mp", "dp", None, None),
        P("mp", "dp", None, None),
        P(),
        P(),
        P(None, None, "dp", "mp"),
        P(None, "mp", "dp"),
        P(None, "dp", "mp"),
        P(None, "mp", "dp"),
        P(),
        P(),
        P(),
        P(),
    )
    return jax.shard_map(
        local,
        mesh=mesh,
        in_specs=placed,
        out_specs=(
            P("mp", "dp", None, None),
            P("mp", "dp", None, None),
            P(None, None, "dp", "mp"),
            P(None, "mp", "dp"),
            P(None, "dp", "mp"),
            P(None, "mp", "dp"),
            P(),
            P(),
            P(),
            P(),
        ),
        check_vma=False,
    )
```

```python
import functools

import jax
import jax.numpy as jnp
from jax import lax
from jax.experimental import pallas as pl
from jax.experimental.pallas import tpu as pltpu
from jax.sharding import PartitionSpec as P

HEAD_DIM = 64
PAIR = 2 * HEAD_DIM

eps_norm = 1e-12
root_half = 0.7071067811865476
inv_root_two_pi = 0.3989422804014327
negative_fill = -1000000000.0
F32 = jnp.float32
BF16 = jnp.bfloat16


def matmul(a, b):
    return lax.dot_general(a, b, (((1,), (0,)), ((), ())), preferred_element_type=F32)


def matmul_nt(a, b):
    return lax.dot_general(a, b, (((1,), (1,)), ((), ())), preferred_element_type=F32)


def gradient(x, y):
    blocks = lax.axis_size("dp")
    if x.shape[1] % (16 * blocks) == 0:
        return Product(x, y, blocks)
    return matmul_tn(x, y).astype(BF16)


def matmul_tn(a, b):
    return lax.dot_general(a, b, (((0,), (0,)), ((), ())), preferred_element_type=F32)


FLOPS_PER_US = 172500000


def cost(us):
    return pl.CostEstimate(flops=int(us * FLOPS_PER_US), transcendentals=0, bytes_accessed=1000)


def xor_permute(x, axis, mask):
    n = lax.axis_size(axis)
    return lax.ppermute(x, axis, [(i, i ^ mask) for i in range(n)])


def dp_axes(n):
    bits = n.bit_length() - 1
    out, at = [], 0
    while at < bits:
        width = 1 if at < 2 else min(2, bits - at)
        out.append((at, 1 << width))
        at += width
    return out[::-1]


def stage_parts(x, shift, size):
    return [x] + [xor_permute(x, "dp", j << shift) for j in range(1, size)]


def stage_gather(x, axis, shift, size):
    return jnp.concatenate(stage_parts(x, shift, size), axis=0)


def assemble_kernel(count, orders, cuts, *refs):
    me = lax.axis_index("dp")
    sources = [(refs[2 * i], refs[2 * i + 1]) for i in range(len(orders))]
    targets = refs[2 * len(orders) :]

    @pl.loop(0, count)
    def _(block):
        place = lax.bitwise_xor(me, block)
        at = 0
        for (own, received), order in zip(sources, orders):
            spot, stride = 0, 1
            for shift, size in order[:-1]:
                spot = spot + stride * lax.bitwise_and(lax.shift_right_logical(place, shift), size - 1)
                stride *= size
            side = lax.bitwise_and(lax.shift_right_logical(place, order[-1][0]), 1)
            cols = own.shape[2]

            def write(source, at=at, cols=cols, spot=spot):
                start = 0
                for target, (low, high) in zip(targets, cuts):
                    first, last = max(low, at), min(high, at + cols)
                    if first < last:
                        target[block, :, first - low : last - low] = source[spot, :, first - at : last - at]

            @pl.when(side == 0)
            def _():
                write(own)

            @pl.when(side == 1)
            def _():
                write(received)

            at += cols


def tie(x, *others):
    return lax.optimization_barrier((x,) + others)[0]


def gather_first(x, order, name):
    with jax.named_scope(name + "_first"):
        y = x[None]
        for shift, size in order[:-2]:
            y = stage_gather(y, "dp", shift, size)
        return y


def gather_next(y, order, name):
    with jax.named_scope(name + "_next"):
        return stage_gather(y, "dp", *order[-2])


def gather_last(y, order, name):
    with jax.named_scope(name + "_last"):
        return [y, xor_permute(y, "dp", 1 << order[-1][0])]


def assemble(sides, orders, widths):
    count = lax.axis_size("dp")
    rows = sides[0].shape[1]
    cuts, at = [], 0
    for w in widths:
        cuts.append((at, at + w))
        at += w
    vmem = pl.BlockSpec(memory_space=pltpu.VMEM)
    outs = pl.pallas_call(
        functools.partial(assemble_kernel, count, tuple(tuple(o) for o in orders), tuple(cuts)),
        out_shape=tuple(jax.ShapeDtypeStruct((count, rows, w), sides[0].dtype) for w in widths),
        in_specs=[vmem] * len(sides),
        out_specs=(vmem,) * len(widths),
        compiler_params=pltpu.CompilerParams(vmem_limit_bytes=6 << 20),
        cost_estimate=cost(1.0),
        name="assemble",
    )(*sides)
    return [o.reshape(count * rows, -1) for o in outs]


class Product:
    def __init__(self, x, y, blocks):
        self.x, self.y = x, y
        self.shape = (blocks, x.shape[1] // blocks, y.shape[1])
        self.size = x.shape[1] * y.shape[1]


def route_kernel(plan, kinds, count_out, *refs):
    me = lax.axis_index("dp")
    ins, outs, refs = [], [], list(refs)
    for is_product in kinds:
        ins.append((refs.pop(0), refs.pop(0)) if is_product else refs.pop(0))
    outs, made = refs[:count_out], refs[count_out:]
    for index, is_product in enumerate(kinds):
        if is_product:
            x_ref, y_ref = ins[index]
            ins[index] = made.pop(0)
            ins[index][...] = matmul_tn(x_ref[...], y_ref[...]).astype(BF16).reshape(ins[index].shape)
    for pieces, sizes, at, shift, grouped in plan:
        size = sizes[at]
        inner = 1
        for extent in sizes[at + 1 :]:
            inner *= extent
        rest = inner
        for extent in sizes[:at]:
            rest *= extent
        coord = lax.bitwise_and(lax.shift_right_logical(me, shift), size - 1)
        log_inner = inner.bit_length() - 1
        if grouped:
            whole = outs.pop(0)
            targets = [whole.at[j * rest : (j + 1) * rest] for j in range(size)]
        else:
            targets = [outs.pop(0) for _ in range(size)]
        for j, target in enumerate(targets):
            side = j if grouped else lax.bitwise_xor(coord, j)

            @pl.loop(0, rest)
            def _(r, target=target, side=side):
                upper = lax.shift_right_logical(r, log_inner)
                source = (upper * size + side) * inner + lax.bitwise_and(r, inner - 1)
                col = 0
                for piece in pieces:
                    width = piece[0][2] - piece[0][1]
                    first, low, high = piece[0]
                    value = ins[first][source, :, low:high]
                    if len(piece) > 1:
                        value = value.astype(F32)
                        for index, low, high in piece[1:]:
                            value = value + ins[index][source, :, low:high].astype(F32)
                    target[r, :, col : col + width] = value.astype(BF16)
                    col += width


def route(groups, name, grouped=False):
    arrays, plan, shapes = [], [], []
    for pieces, left, axis in groups:
        entries = []
        for piece in pieces:
            entry = []
            for array, low, high in piece:
                known = [i for i, other in enumerate(arrays) if other is array]
                if not known:
                    known = [len(arrays)]
                    arrays.append(array)
                entry.append((known[0], low, high))
            entries.append(tuple(entry))
        at = left.index(axis)
        plan.append((tuple(entries), tuple(size for _, size in left), at, axis[0], grouped))
        total = sum(piece[0][2] - piece[0][1] for piece in pieces)
        array = pieces[0][0][0]
        if grouped:
            shapes.append((1, (array.shape[0], array.shape[1], total)))
        else:
            shapes.append((axis[1], (array.shape[0] // axis[1], array.shape[1], total)))
    vmem = pl.BlockSpec(memory_space=pltpu.VMEM)
    out_shape = [jax.ShapeDtypeStruct(shape, BF16) for size, shape in shapes for _ in range(size)]
    kinds = tuple(isinstance(array, Product) for array in arrays)
    operands, scratch = [], []
    for array, is_product in zip(arrays, kinds):
        operands += [array.x, array.y] if is_product else [array]
        if is_product:
            scratch.append(pltpu.VMEM(array.shape, BF16))
    flat = pl.pallas_call(
        functools.partial(route_kernel, tuple(plan), kinds, len(out_shape)),
        out_shape=out_shape,
        in_specs=[vmem] * len(operands),
        out_specs=[vmem] * len(out_shape),
        scratch_shapes=scratch,
        compiler_params=pltpu.CompilerParams(vmem_limit_bytes=(20 if scratch else 6) << 20),
        cost_estimate=cost(1.0),
        name=name,
    )(*operands)
    outs = []
    for size, _ in shapes:
        outs.append(list(flat[:size]))
        flat = flat[size:]
    return outs


class Scatter:
    def __init__(self, arrays, orders, axes, name, group_last=False):
        self.group_last = group_last
        n = lax.axis_size("dp")
        self.name = name
        self.orders = [list(o) for o in orders]
        self.lefts = [list(axes) for _ in orders]
        self.pieces = []
        shaped = {}
        for parts in arrays:
            pieces = []
            if parts is None:
                self.pieces.append(None)
                continue
            for g, low, high in parts:
                if id(g) not in shaped:
                    shaped[id(g)] = g if isinstance(g, Product) else g.reshape(n, g.shape[0] // n, g.shape[1])
                pieces.append([(shaped[id(g)], low, high)])
            self.pieces.append(pieces)
        self.count = 0

    def deal(self):
        self.count += 1
        merged = len(self.pieces) > 1 and len(self.lefts[0]) < 3 and self.lefts[0] == self.lefts[1]
        groups = []
        if merged:
            groups.append((sum(self.pieces, []), self.lefts[0], self.orders[0][0]))
            self.orders, self.lefts = self.orders[:1], self.lefts[:1]
        else:
            for parts, left, order in zip(self.pieces, self.lefts, self.orders):
                groups.append((parts, left, order[0]))
        self.grouped = self.group_last and len(groups) == 1 and len(self.lefts[0]) == 1
        self.dealt = route(groups, f"{self.name}_deal_{self.count}", self.grouped)
        return self.dealt

    def send(self):
        pieces, lefts, orders = [], [], []
        for parts, left, order in zip(self.dealt, self.lefts, self.orders):
            shift, size = order[0]
            with jax.named_scope(f"{self.name}_{self.count}"):
                if self.grouped:
                    n = lax.axis_size("dp")
                    members = [[i | (j << shift) for j in range(size)] for i in range(n) if not (i >> shift) % size]
                    whole = lax.all_to_all(
                        parts[0], "dp", split_axis=0, concat_axis=0, axis_index_groups=members, tiled=True
                    )
                    rest = whole.shape[0] // size
                    got = [whole[j * rest : (j + 1) * rest] for j in range(size)]
                else:
                    got = [parts[0]] + [
                        xor_permute(parts[j], "dp", j << shift) for j in range(1, size)
                    ]
            pieces.append([[(x, 0, x.shape[2]) for x in got]])
            lefts.append([axis for axis in left if axis != order[0]])
            orders.append(order[1:])
        self.pieces, self.lefts, self.orders = pieces, lefts, orders

    def set_part(self, i, parts):
        self.pieces[i] = Scatter([parts], [self.orders[i]], self.lefts[i], self.name).pieces[0]

    def deal_one(self, i):
        return route([(self.pieces[i], self.lefts[i], self.orders[i][0])], f"{self.name}_deal_1{i}")[0]

    def send_one(self, i, parts):
        self.count = 1
        shift, size = self.orders[i][0]
        with jax.named_scope(f"{self.name}_1{i}"):
            got = [parts[0]] + [xor_permute(parts[j], "dp", j << shift) for j in range(1, size)]
        self.pieces[i] = [[(x, 0, x.shape[2]) for x in got]]
        self.lefts[i] = [axis for axis in self.lefts[i] if axis != self.orders[i][0]]
        self.orders[i] = self.orders[i][1:]

    def after(self, *others):
        arrays = [x for (piece,) in self.pieces for x, _, _ in piece[1:]]
        arrays = list(lax.optimization_barrier((tuple(arrays), others))[0])
        self.pieces = [
            [[piece[0]] + [(arrays.pop(0), low, high) for _, low, high in piece[1:]]] for (piece,) in self.pieces
        ]

    def before(self, x):
        arrays = [y for (piece,) in self.pieces for y, _, _ in piece]
        x, arrays = lax.optimization_barrier((x, tuple(arrays)))
        arrays = list(arrays)
        self.pieces = [[[(arrays.pop(0), low, high) for _, low, high in piece]] for (piece,) in self.pieces]
        return x

    def total(self):
        outs = []
        for (piece,) in self.pieces:
            parts = [x[0].astype(F32) for x, _, _ in piece]
            while len(parts) > 1:
                parts = [parts[i] + parts[i + 1] for i in range(0, len(parts), 2)]
            outs.append(parts[0])
        return outs[0] if len(outs) == 1 else jnp.concatenate(outs, axis=1)

    def finish_stages(self):
        while self.orders[0]:
            self.deal()
            self.send()

    def finish(self):
        self.finish_stages()
        return self.total()


def attend_forward_kernel(block, qkv_ref, bias_ref, *refs):
    ctx_ref, lse_ref = refs[-2:]
    length = qkv_ref.shape[0]
    bias = bias_ref[...]
    for head in range(2):
        low = head * HEAD_DIM
        keys = qkv_ref[:, PAIR + low : PAIR + low + HEAD_DIM]
        values_t = qkv_ref[:, 2 * PAIR + low : 2 * PAIR + low + HEAD_DIM].T
        for start in range(0, length, block):
            queries = qkv_ref[start : start + block, low : low + HEAD_DIM]
            scores = matmul_nt(keys, queries) + bias
            top = jnp.max(scores, axis=0, keepdims=True)
            exponent = jnp.exp(scores - top)
            total = jnp.sum(exponent, axis=0, keepdims=True)
            context_t = matmul(values_t, exponent.astype(BF16)) * (1.0 / total)
            ctx_ref[start : start + block, low : low + HEAD_DIM] = context_t.T.astype(BF16)
            lse_ref[0, head : head + 1, start : start + block] = top + jnp.log(total)


def attend_forward(qkv, bias, first, pairs, total, known=()):
    length = qkv.shape[0]
    return pl.pallas_call(
        functools.partial(attend_forward_kernel, min(256, length)),
        grid=(pairs,),
        out_shape=(
            jax.ShapeDtypeStruct((length, total * PAIR), BF16),
            jax.ShapeDtypeStruct((total, 2, length), F32),
        ),
        in_specs=[
            pl.BlockSpec((length, 3 * PAIR), lambda p: (0, p + first)),
            pl.BlockSpec((length, 1), lambda p: (0, 0)),
        ]
        + [pl.BlockSpec(memory_space=pl.ANY)] * len(known),
        out_specs=(
            pl.BlockSpec((length, PAIR), lambda p: (0, p + first)),
            pl.BlockSpec((1, 2, length), lambda p: (p + first, 0, 0)),
        ),
        input_output_aliases={2: 0, 3: 1} if known else {},
        compiler_params=pltpu.CompilerParams(vmem_limit_bytes=10 << 20),
        cost_estimate=cost(5.9 * pairs),
        name="attend_forward",
    )(qkv, bias, *known)


def attend_backward_kernel(block, qkv_ref, dctx_ref, lse_ref, bias_ref, *refs):
    out_ref, sums_ref, dk_ref, dv_ref = refs[-4:]
    length = qkv_ref.shape[0]
    bias = bias_ref[...]
    for head in range(2):
        low = head * HEAD_DIM
        keys = qkv_ref[:, PAIR + low : PAIR + low + HEAD_DIM]
        keys_t = keys.T
        values = qkv_ref[:, 2 * PAIR + low : 2 * PAIR + low + HEAD_DIM]
        query_sum = jnp.zeros((1, HEAD_DIM), F32)
        for start in range(0, length, block):
            queries = qkv_ref[start : start + block, low : low + HEAD_DIM]
            grads = dctx_ref[start : start + block, low : low + HEAD_DIM]
            lse = lse_ref[0, head : head + 1, start : start + block]
            probs = jnp.exp(matmul_nt(keys, queries) + bias - lse)
            grad_probs = matmul_nt(values, grads)
            inner = jnp.sum(probs * grad_probs, axis=0, keepdims=True)
            grad_scores = (probs * (grad_probs - inner)).astype(BF16)
            dv = matmul(probs.astype(BF16), grads)
            dk = matmul(grad_scores, queries)
            if start == 0:
                dk_ref[...] = dk
                dv_ref[...] = dv
            else:
                dk_ref[...] += dk
                dv_ref[...] += dv
            dq = (matmul(keys_t, grad_scores) * HEAD_DIM ** (-0.5)).T
            query_sum = query_sum + jnp.sum(dq, axis=0, keepdims=True)
            out_ref[start : start + block, low : low + HEAD_DIM] = dq.astype(BF16)
        dk = dk_ref[...]
        dv = dv_ref[...]
        out_ref[:, PAIR + low : PAIR + low + HEAD_DIM] = dk.astype(BF16)
        out_ref[:, 2 * PAIR + low : 2 * PAIR + low + HEAD_DIM] = dv.astype(BF16)
        sums_ref[0, 0:1, low : low + HEAD_DIM] = query_sum
        sums_ref[0, 1:2, low : low + HEAD_DIM] = jnp.sum(dv, axis=0, keepdims=True)


def attend_backward(qkv, dctx, lse, bias, first, pairs, total, known=()):
    length = qkv.shape[0]
    return pl.pallas_call(
        functools.partial(attend_backward_kernel, min(256, length)),
        grid=(pairs,),
        out_shape=(
            jax.ShapeDtypeStruct((length, total * 3 * PAIR), BF16),
            jax.ShapeDtypeStruct((total, 2, PAIR), F32),
        ),
        in_specs=[
            pl.BlockSpec((length, 3 * PAIR), lambda p: (0, p + first)),
            pl.BlockSpec((length, PAIR), lambda p: (0, p + first)),
            pl.BlockSpec((1, 2, length), lambda p: (p + first, 0, 0)),
            pl.BlockSpec((length, 1), lambda p: (0, 0)),
        ]
        + [pl.BlockSpec(memory_space=pl.ANY)] * len(known),
        out_specs=(
            pl.BlockSpec((length, 3 * PAIR), lambda p: (0, p + first)),
            pl.BlockSpec((1, 2, PAIR), lambda p: (p + first, 0, 0)),
        ),
        input_output_aliases={4: 0, 5: 1} if known else {},
        scratch_shapes=[pltpu.VMEM((length, HEAD_DIM), F32), pltpu.VMEM((length, HEAD_DIM), F32)],
        compiler_params=pltpu.CompilerParams(vmem_limit_bytes=10 << 20),
        cost_estimate=cost(7.3 * pairs),
        name="attend_backward",
    )(qkv, dctx, lse, bias, *known)


def call(kernel, outs, args, name, us, vmem_mib=10, scratch=()):
    spec = pl.BlockSpec(memory_space=pltpu.VMEM)
    return pl.pallas_call(
        kernel,
        out_shape=[jax.ShapeDtypeStruct(shape, kind) for shape, kind in outs],
        in_specs=[spec] * len(args),
        out_specs=[spec] * len(outs),
        scratch_shapes=list(scratch),
        compiler_params=pltpu.CompilerParams(vmem_limit_bytes=vmem_mib << 20),
        cost_estimate=cost(us),
        name=name,
    )(*args)


def row_blocks(rows, block):
    block = min(block, rows)
    return rows // block, block


def rows_at(i, block):
    return pl.ds(pl.multiple_of(i * block, block), block)


def project_kernel(x_ref, w_ref, bias_ref, scale_ref, out_ref):
    count, block = row_blocks(x_ref.shape[0], 512)

    @pl.loop(0, count)
    def _(i):
        at = rows_at(i, block)
        out_ref[at, :] = ((matmul(x_ref[at, :], w_ref[...]) + bias_ref[...]) * scale_ref[...]).astype(BF16)


def part_kernel(low, high, x_ref, w_ref, out_ref):
    out_ref[...] = matmul_nt(x_ref[low:high, :], w_ref[...]).astype(BF16)


def exchanged_parts(x, w, name):
    half = x.shape[0] // 2
    own, got = [], []
    for number in range(2):
        (part,) = call(
            functools.partial(part_kernel, number * half, (number + 1) * half),
            [((half, w.shape[0]), BF16)],
            (x, w),
            f"{name}_{number}",
            1.5,
        )
        if number == 0:
            x = tie(x, part)
        own.append(part)
        with jax.named_scope(f"{name}_{number}"):
            got.append(xor_permute(part, "mp", 1))
    return own + got[::-1]


def halves(parts, body, rows, block):
    count, block = row_blocks(rows // 2, block)
    for number in range(2):
        own_ref, got_ref = parts[number], parts[2 + number]

        @pl.loop(0, count)
        def _(i, number=number, own_ref=own_ref, got_ref=got_ref):
            at = rows_at(i, block)
            total = own_ref[at, :].astype(F32) + got_ref[at, :].astype(F32)
            body(number, at, rows_at(i + number * count, block), total)


def middle_kernel(x_ref, p0, p1, p2, p3, vec_ref, w_ref, bias_ref, normed_ref, rstd_ref, low_ref, act_ref, slope_ref):
    def body(number, half_at, at, total):
        mixed = x_ref[at, :].astype(F32) + total + vec_ref[2:3, :]
        normed, rstd = norm_forward(mixed)
        normed_ref[at, :] = normed.astype(BF16)
        rstd_ref[at, :] = rstd
        low = (normed * vec_ref[0:1, :] + vec_ref[3:4, :]).astype(BF16)
        low_ref[at, :] = low
        u = matmul(low, w_ref[...]) + bias_ref[...]
        half_cdf = 0.5 * (1.0 + lax.erf(u * root_half))
        act_ref[at, :] = (u * half_cdf).astype(BF16)
        slope_ref[at, :] = (half_cdf + u * jnp.exp(-0.5 * u * u) * inv_root_two_pi).astype(BF16)

    halves((p0, p1, p2, p3), body, x_ref.shape[0], 256)


def outer_kernel(normed_ref, p0, p1, p2, p3, cot_own_ref, cot_got0, cot_got1, vec_ref, out_ref, low_ref, sums_ref, cot_ref):
    sums_ref[...] = jnp.zeros_like(sums_ref)

    half = cot_own_ref.shape[0]
    for index, source in enumerate((cot_own_ref, cot_got0, cot_got1)):
        low = 0 if index == 0 else half + (index - 1) * (half // 2)
        cot_ref[low : low + source.shape[0], :] = source[...]

    def body(number, half_at, at, total):
        mixed = normed_ref[at, :].astype(F32) * vec_ref[0:1, :] + vec_ref[3:4, :] + total + vec_ref[4:5, :]
        normed, rstd = norm_forward(mixed)
        if number == 0:
            out_ref[at, :] = (normed * vec_ref[1:2, :] + vec_ref[5:6, :]).astype(BF16)
        cot = cot_ref[at, :].astype(F32)
        grad, grad_gain, grad_shift = norm_backward(cot, normed, rstd, vec_ref[1:2, :])
        low_ref[at, :] = grad.astype(BF16)
        sums_ref[0:1, :] += grad_gain
        sums_ref[1:2, :] += grad_shift
        sums_ref[2:3, :] += jnp.sum(grad, axis=0, keepdims=True)

    halves((p0, p1, p2, p3), body, normed_ref.shape[0], 256)


def hidden_grad_kernel(grad_ref, w_ref, slope_ref, out_ref, sums_ref):
    count, block = row_blocks(grad_ref.shape[0], 256)
    sums_ref[...] = jnp.zeros_like(sums_ref)

    @pl.loop(0, count)
    def _(i):
        at = rows_at(i, block)
        grad = matmul(grad_ref[at, :], w_ref[...]) * slope_ref[at, :].astype(F32)
        out_ref[at, :] = grad.astype(BF16)
        sums_ref[...] += jnp.sum(grad, axis=0, keepdims=True)


def inner_kernel(
    grad_in_ref, p0, p1, p2, p3, normed_ref, rstd_ref, vec_ref, w_ref, own_grad_ref, low_ref, ctx_ref, sums_ref
):
    sums_ref[...] = jnp.zeros_like(sums_ref)

    def body(number, half_at, at, total):
        given = grad_in_ref[at, :].astype(F32) + total
        grad, grad_gain, grad_shift = norm_backward(given, normed_ref[at, :].astype(F32), rstd_ref[at, :], vec_ref[0:1, :])
        low = grad.astype(BF16)
        low_ref[at, :] = low
        ctx_ref[at, :] = matmul(low, w_ref[...]).astype(BF16)
        sums_ref[0:1, :] += grad_gain
        sums_ref[1:2, :] += grad_shift
        sums_ref[2:3, :] += jnp.sum(grad, axis=0, keepdims=True)
        if number == 0:
            own_grad_ref[at, :] = grad

    halves((p0, p1, p2, p3), body, normed_ref.shape[0], 256)


def input_grad_kernel(x_ref, w_ref, grad_ref, keep_ref, send_ref):
    half = keep_ref.shape[0]
    send_ref[...] = matmul_nt(x_ref[half:, :], w_ref[...]).astype(BF16)
    keep_ref[...] = grad_ref[...] + matmul_nt(x_ref[:half, :], w_ref[...])


def norm_forward(rows):
    center = rows - jnp.mean(rows, axis=1, keepdims=True)
    rstd = lax.rsqrt(jnp.mean(center * center, axis=1, keepdims=True) + eps_norm)
    return center * rstd, rstd


def norm_backward(grad, normed, rstd, gain):
    scaled = grad * gain
    inner = (
        scaled
        - jnp.mean(scaled, axis=1, keepdims=True)
        - normed * jnp.mean(scaled * normed, axis=1, keepdims=True)
    )
    return (
        rstd * inner,
        jnp.sum(grad * normed, axis=0, keepdims=True),
        jnp.sum(grad, axis=0, keepdims=True),
    )


def from_other(x):
    half = x.shape[0] // 2
    return [xor_permute(x[:half], "mp", 1), xor_permute(x[half:], "mp", 1)]


def deal_rows(x, deal_order):
    return x[0].at[:, deal_order].get(mode="promise_in_bounds").transpose(1, 0, 2)


def exchange_in(dealt, *others):
    dealt = tie(dealt, *others)
    arrived = lax.all_to_all(dealt, "dp", split_axis=0, concat_axis=0, tiled=True)
    return arrived.reshape(-1, dealt.shape[2])


def exchange_out(rows, extra):
    n = lax.axis_size("dp")
    with jax.named_scope("out_rows"):
        blocks = rows.reshape(n, rows.shape[0] // n, rows.shape[1])
        blocks = jnp.concatenate([blocks, jnp.broadcast_to(extra, (n,) + extra.shape)], axis=1)
        return lax.all_to_all(blocks, "dp", split_axis=0, concat_axis=0, tiled=True)


def taken_out(sent, count):
    return sent[:, :count].transpose(1, 0, 2)[None], sent[:, count:]


def put_split(out_ref, row, count, value):
    high = value.astype(BF16)
    out_ref[row : row + 1, :] = high
    out_ref[row + count : row + count + 1, :] = (value - high.astype(F32)).astype(BF16)


def early_kernel(one_ref, two_ref, up_ref, out_ref):
    first = lax.axis_index("mp") == 0
    width = one_ref.shape[1]
    pieces = up_ref.shape[1] // width
    count = 3 + pieces
    out_ref[...] = jnp.zeros_like(out_ref)
    for row in range(3):
        put_split(out_ref, row, count, jnp.where(first, one_ref[row : row + 1, :], two_ref[row : row + 1, :]))
    for piece in range(pieces):
        put_split(out_ref, 3 + piece, count, up_ref[0:1, piece * width : (piece + 1) * width])


def late_kernel(pairs, keep_ref, g0, g1, sums_ref, rows_ref, out_ref):
    half = keep_ref.shape[0] // 2
    for index, source in enumerate((g0, g1)):
        at = slice(index * half, (index + 1) * half)
        rows_ref[at, :] = (keep_ref[at, :] + source[...].astype(F32)).astype(BF16)
    out_ref[...] = jnp.zeros_like(out_ref)
    for which in range(2):
        for pair in range(pairs):
            col = (which * pairs + pair) * PAIR
            value = sums_ref[pair, which : which + 1, :]
            high = value.astype(BF16)
            out_ref[0:1, col : col + PAIR] = high
            out_ref[1:2, col : col + PAIR] = (value - high.astype(F32)).astype(BF16)


def gathered_kernel(count, x_ref, out_ref):
    out_ref[...] = jnp.zeros_like(out_ref)

    @pl.loop(0, x_ref.shape[0])
    def _(i):
        x = x_ref[i].astype(F32)
        out_ref[...] += x[:count, :] + x[count : 2 * count, :]


def local(
    tokens, cotangent, lengths, deal_order, attn_in, attn_out, ffn_in, ffn_out,
    attn_bias, ffn_bias, norm_gain, shifts,
):
    dp_size = lax.axis_size("dp")
    mp_rank = lax.axis_index("mp")
    dp_rank = lax.axis_index("dp")
    axes = dp_axes(dp_size)
    low = axes[-2:]
    high = axes[:-2]
    order_one = high + low
    order_two = high + low[::-1]
    back_one = low[::-1] + high[::-1]
    back_two = low + high[::-1]

    width = tokens.shape[3]
    half_len = tokens.shape[1] * dp_size
    seq_len = 2 * half_len
    head_cols = attn_in.shape[3]
    hidden_cols = ffn_in.shape[2]
    pairs = head_cols // PAIR
    shard_rows = attn_in.shape[2]

    three = attn_in[0].reshape(3, shard_rows, pairs, PAIR).transpose(1, 2, 0, 3)
    three = three.reshape(shard_rows, 3 * head_cols)
    back_t = attn_out[0].T
    up = ffn_in[0]
    down_t = ffn_out[0].T

    cut_three = 128 * ((3 * head_cols // 128 + 1) // 2)
    pieces_three = [three[:, :cut_three], three[:, cut_three:]]
    rest = jnp.concatenate([back_t, up], axis=1)
    cut_rest = 128 * ((rest.shape[1] // 128 + 1) // 2)
    orders = [tuple(order_one), tuple(order_two)]

    first_three = gather_first(three, order_one, "ag_three")
    with jax.named_scope("in_tokens"):
        tok_own = exchange_in(deal_rows(tokens, deal_order), first_three)
        dealt_cot = deal_rows(cotangent, deal_order)
    w_down = lax.all_gather(down_t, "dp", axis=0, tiled=True)
    next_three = [
        gather_next(first_three[:, :, :cut_three], order_one, "ag_three"),
        gather_next(first_three[:, :, cut_three:], order_two, "ag_three"),
    ]
    rest, *next_three = lax.optimization_barrier((rest, *next_three))
    with jax.named_scope("ag_rest_first"):
        first_got = [rest[None]]
        for shift, size in order_one[:-3]:
            first_got = [stage_gather(x, "dp", shift, size) for x in first_got]
        shift, size = order_one[-3]
        first_own = first_got[0]
        first_got = [xor_permute(first_own, "dp", j << shift) for j in range(1, size)]
    sides_three = gather_last(next_three[0], order_one, "ag_three") + gather_last(
        next_three[1], order_two, "ag_three"
    )
    (w_three,) = assemble(sides_three, orders, [3 * head_cols])
    hb = jnp.concatenate([tok_own] + from_other(tok_own), axis=0)
    length = lengths[deal_order[dp_rank]]
    place = jnp.arange(seq_len, dtype=jnp.int32)
    place = jnp.where(mp_rank == 0, place, (place + half_len) % seq_len)
    bias_col = jnp.where(place < length, 0.0, negative_fill).astype(F32)[:, None]

    def own_cols(v, count):
        return jnp.where(mp_rank == 0, v[..., :count], v[..., count:])

    bias_pair = own_cols(attn_bias[0].astype(F32), head_cols).reshape(2, pairs, PAIR)
    bias_three = jnp.stack([bias_pair[0], jnp.zeros_like(bias_pair[0]), bias_pair[1]], axis=1).reshape(1, -1)
    bias_up = own_cols(ffn_bias[0].astype(F32), hidden_cols)[None]
    scale_three = jnp.concatenate(
        [jnp.full((pairs, 1, PAIR), HEAD_DIM ** (-0.5), F32), jnp.ones((pairs, 2, PAIR), F32)], axis=1
    ).reshape(1, -1)
    vec = jnp.concatenate([norm_gain[0], shifts[0]], axis=0).astype(F32)
    hb, bias_up, vec, bias_col, dealt_cot = lax.optimization_barrier((hb, bias_up, vec, bias_col, dealt_cot))
    big, wide, hidden_shape = (seq_len, width), (seq_len, head_cols), (seq_len, hidden_cols)

    (qkv,) = call(
        project_kernel, [((seq_len, 3 * head_cols), BF16)], (hb, w_three, bias_three, scale_three), "project", 2.4
    )
    attended = attend_forward(qkv, bias_col, 0, 1, pairs)
    attended, *first_got = lax.optimization_barrier((attended, *first_got))
    first_rest = jnp.concatenate([first_own] + first_got, axis=0)
    attended, first_rest = lax.optimization_barrier((attended, first_rest))
    own_rest = [first_rest[:, :, :cut_rest], first_rest[:, :, cut_rest:]]
    with jax.named_scope("ag_rest_next"):
        got_rest = [xor_permute(y, "dp", 1 << o[-2][0]) for y, o in zip(own_rest, orders)]
    if pairs > 2:
        attended = attend_forward(qkv, bias_col, 1, pairs - 2, pairs, attended)
    attended, *got_rest = lax.optimization_barrier((attended, *got_rest))
    next_rest = [jnp.concatenate(pair, axis=0) for pair in zip(own_rest, got_rest)]
    attended, *next_rest = lax.optimization_barrier((attended, *next_rest))
    sides_rest = gather_last(next_rest[0], order_one, "ag_rest") + gather_last(
        next_rest[1], order_two, "ag_rest"
    )
    if pairs > 1:
        attended = attend_forward(qkv, bias_col, pairs - 1, 1, pairs, attended)
    context, lse = attended
    with jax.named_scope("in_cot"):
        cot_own = exchange_in(dealt_cot, context)
    context, w_down = lax.optimization_barrier((context, w_down))
    w_back, w_up = assemble(sides_rest, orders, [head_cols, hidden_cols])
    mid_normed, mid_rstd, mid_low, hidden_low, slope = call(
        middle_kernel,
        [(big, BF16), ((seq_len, 1), F32), (big, BF16), (hidden_shape, BF16), (hidden_shape, BF16)],
        (hb, *exchanged_parts(context, w_back, "attn_part"), vec, w_up, bias_up),
        "middle",
        8,
    )

    result, grad_two_low, sums_two = call(
        outer_kernel,
        [((half_len, width), BF16), (big, BF16), ((3, width), F32)],
        (
            mid_normed,
            *exchanged_parts(hidden_low, w_down, "ffn_part"),
            cot_own,
            *from_other(cot_own),
            vec,
        ),
        "outer",
        4.5,
        scratch=[pltpu.VMEM(big, BF16)],
    )
    ffn = Scatter(
        [[(gradient(grad_two_low, hidden_low), 0, hidden_cols)], None], [back_one, back_two], axes, "rs_ffn", True
    )
    dealt = ffn.deal_one(0)
    grad_two_low, dealt = lax.optimization_barrier((grad_two_low, dealt))
    ffn.send_one(0, dealt)
    grad_hidden_low, grad_up_bias = call(
        hidden_grad_kernel,
        [(hidden_shape, BF16), ((1, hidden_cols), F32)],
        (grad_two_low, w_down, slope),
        "hidden_grad",
        3.3,
    )
    parts = exchanged_parts(grad_hidden_low, w_up, "mid_part")
    grad_hidden_low = tie(grad_hidden_low, parts[1])
    ffn.set_part(1, [(gradient(mid_low, grad_hidden_low), 0, hidden_cols)])
    dealt = ffn.deal_one(1)
    parts[2], dealt = lax.optimization_barrier((parts[2], dealt))
    ffn.send_one(1, dealt)
    grad_one, grad_one_low, grad_context, sums_one = call(
        inner_kernel,
        [((half_len, width), F32), (big, BF16), (wide, BF16), ((3, width), F32)],
        (grad_two_low, *parts, mid_normed, mid_rstd, vec, w_back),
        "inner",
        3.5,
    )
    early_count = 3 + hidden_cols // width
    (early,) = call(
        early_kernel, [((16 * -(-2 * early_count // 16), width), BF16)], (sums_one, sums_two, grad_up_bias), "early", 0.5
    )
    sent_tokens = exchange_out(result, early)
    grad_w_back = gradient(grad_one_low, context)

    given = ()
    if pairs > 1:
        given = attend_backward(qkv, grad_context, lse, bias_col, 0, pairs - 1, pairs)
        ffn.after(given)
    ffn.deal()
    grad_context, ffn.dealt = lax.optimization_barrier((grad_context, ffn.dealt))
    ffn.send()
    given = attend_backward(qkv, grad_context, lse, bias_col, pairs - 1, 1, pairs, given)
    dqkv, pair_sums = given
    ffn.after(given)
    ffn.deal()
    dqkv, ffn.dealt = lax.optimization_barrier((dqkv, ffn.dealt))
    ffn.send()
    grad_w_three = gradient(hb, dqkv)
    cut = 128 * ((4 * head_cols // 128 + 1) // 2)
    tail = Scatter(
        [
            [(grad_w_three, 0, cut)],
            [(grad_w_three, cut, 3 * head_cols), (grad_w_back, 0, head_cols)],
        ],
        [back_one, back_two],
        axes,
        "rs_attn",
    )
    tail.deal()
    dqkv, tail.dealt = lax.optimization_barrier((dqkv, tail.dealt))
    tail.send()
    keep, sent = call(
        input_grad_kernel,
        [((half_len, width), F32), ((half_len, width), BF16)],
        (dqkv, w_three, grad_one),
        "input_grad",
        2.3,
    )
    got = from_other(sent)
    got, sent_tokens = lax.optimization_barrier((got, sent_tokens))
    grad_in, late = call(
        functools.partial(late_kernel, pairs),
        [((half_len, width), BF16), ((8, 2 * head_cols), BF16)],
        (keep, *got, pair_sums),
        "late",
        1.0,
    )
    sent_grad = exchange_out(grad_in, late)
    block = half_len // dp_size
    out_tokens, early_all = taken_out(sent_tokens, block)
    out_grad, late_all = taken_out(sent_grad, block)
    ffn_sum = ffn.finish()
    down_sum, up_sum = ffn_sum[:, :hidden_cols], ffn_sum[:, hidden_cols:]
    attn_sum = tail.finish()
    three_sum, back_sum = attn_sum[:, : 3 * head_cols], attn_sum[:, 3 * head_cols :]

    (early_sum,) = call(
        functools.partial(gathered_kernel, early_count), [((early_count, width), F32)], (early_all,), "early_sum", 0.5
    )
    (late_sum,) = call(functools.partial(gathered_kernel, 1), [((1, width), F32)], (late_all,), "late_sum", 0.5)

    def in_order(own):
        other = xor_permute(own, "mp", 1)
        return jnp.where(mp_rank == 0, own, other), jnp.where(mp_rank == 0, other, own)

    low_early, high_early = in_order(early_sum)
    low_late, high_late = in_order(late_sum)
    gain_out = jnp.stack([low_early[0], high_early[0]])[None]
    shift_out = jnp.stack([low_early[2], low_early[1], high_early[2], high_early[1]])[None]
    ffn_bias_out = jnp.concatenate([low_early[3:].reshape(1, -1), high_early[3:].reshape(1, -1)], axis=1)
    attn_bias_out = jnp.concatenate(
        [low_late.reshape(1, 2, head_cols), high_late.reshape(1, 2, head_cols)], axis=2
    )

    three_out = three_sum.reshape(shard_rows, pairs, 3, PAIR)
    three_out = three_out.transpose(2, 0, 1, 3).reshape(1, 3, shard_rows, head_cols)
    back_out = back_sum.T[None]
    up_out = up_sum[None]
    down_out = down_sum.T[None]
    return (
        out_tokens, out_grad, three_out, back_out, up_out, down_out,
        attn_bias_out, ffn_bias_out, gain_out, shift_out,
    )


def solution(mesh):
    placed = (
        P("mp", "dp", None, None),
        P("mp", "dp", None, None),
        P(),
        P(),
        P(None, None, "dp", "mp"),
        P(None, "mp", "dp"),
        P(None, "dp", "mp"),
        P(None, "mp", "dp"),
        P(),
        P(),
        P(),
        P(),
    )
    return jax.shard_map(
        local,
        mesh=mesh,
        in_specs=placed,
        out_specs=(
            P("mp", "dp", None, None),
            P("mp", "dp", None, None),
            P(None, None, "dp", "mp"),
            P(None, "mp", "dp"),
            P(None, "dp", "mp"),
            P(None, "mp", "dp"),
            P(),
            P(),
            P(),
            P(),
        ),
        check_vma=False,
    )
```

```python
import functools

import jax
import jax.numpy as jnp
from jax import lax
from jax.experimental import pallas as pl
from jax.experimental.pallas import tpu as pltpu
from jax.sharding import PartitionSpec as P

HEAD_DIM = 64
PAIR = 2 * HEAD_DIM

eps_norm = 1e-12
root_half = 0.7071067811865476
inv_root_two_pi = 0.3989422804014327
negative_fill = -1000000000.0
F32 = jnp.float32
BF16 = jnp.bfloat16


def matmul(a, b):
    return lax.dot_general(a, b, (((1,), (0,)), ((), ())), preferred_element_type=F32)


def matmul_nt(a, b):
    return lax.dot_general(a, b, (((1,), (1,)), ((), ())), preferred_element_type=F32)


def gradient(x, y):
    blocks = lax.axis_size("dp")
    if x.shape[1] % (16 * blocks) == 0:
        return Product(x, y, blocks)
    return matmul_tn(x, y).astype(BF16)


def matmul_tn(a, b):
    return lax.dot_general(a, b, (((0,), (0,)), ((), ())), preferred_element_type=F32)


FLOPS_PER_US = 172500000


def cost(us):
    return pl.CostEstimate(flops=int(us * FLOPS_PER_US), transcendentals=0, bytes_accessed=1000)


def xor_permute(x, axis, mask):
    n = lax.axis_size(axis)
    return lax.ppermute(x, axis, [(i, i ^ mask) for i in range(n)])


def dp_axes(n):
    bits = n.bit_length() - 1
    out, at = [], 0
    while at < bits:
        width = 1 if at < 2 else min(2, bits - at)
        out.append((at, 1 << width))
        at += width
    return out[::-1]


def pairs_of(axes):
    out = []
    for shift, size in axes:
        width = size.bit_length() - 1
        out += [(shift + bit, 2) for bit in reversed(range(width))]
    return out


def stage_parts(x, shift, size):
    return [x] + [xor_permute(x, "dp", j << shift) for j in range(1, size)]


def stage_gather(x, axis, shift, size):
    return jnp.concatenate(stage_parts(x, shift, size), axis=0)


def assemble_kernel(count, orders, cuts, *refs):
    me = lax.axis_index("dp")
    sources = [(refs[2 * i], refs[2 * i + 1]) for i in range(len(orders))]
    targets = refs[2 * len(orders) :]

    @pl.loop(0, count)
    def _(block):
        place = lax.bitwise_xor(me, block)
        at = 0
        for (own, received), order in zip(sources, orders):
            spot, stride = 0, 1
            for shift, size in order[:-1]:
                spot = spot + stride * lax.bitwise_and(lax.shift_right_logical(place, shift), size - 1)
                stride *= size
            side = lax.bitwise_and(lax.shift_right_logical(place, order[-1][0]), 1)
            cols = own.shape[2]

            def write(source, at=at, cols=cols, spot=spot):
                start = 0
                for target, (low, high) in zip(targets, cuts):
                    first, last = max(low, at), min(high, at + cols)
                    if first < last:
                        target[block, :, first - low : last - low] = source[spot, :, first - at : last - at]

            @pl.when(side == 0)
            def _():
                write(own)

            @pl.when(side == 1)
            def _():
                write(received)

            at += cols


def tie(x, *others):
    return lax.optimization_barrier((x,) + others)[0]


def gather_first(x, order, name):
    with jax.named_scope(name + "_first"):
        y = x[None]
        for shift, size in order[:-2]:
            y = stage_gather(y, "dp", shift, size)
        return y


def gather_next(y, order, name):
    with jax.named_scope(name + "_next"):
        return stage_gather(y, "dp", *order[-2])


def gather_last(y, order, name):
    with jax.named_scope(name + "_last"):
        return [y, xor_permute(y, "dp", 1 << order[-1][0])]


def assemble(sides, orders, widths):
    count = lax.axis_size("dp")
    rows = sides[0].shape[1]
    cuts, at = [], 0
    for w in widths:
        cuts.append((at, at + w))
        at += w
    vmem = pl.BlockSpec(memory_space=pltpu.VMEM)
    outs = pl.pallas_call(
        functools.partial(assemble_kernel, count, tuple(tuple(o) for o in orders), tuple(cuts)),
        out_shape=tuple(jax.ShapeDtypeStruct((count, rows, w), sides[0].dtype) for w in widths),
        in_specs=[vmem] * len(sides),
        out_specs=(vmem,) * len(widths),
        compiler_params=pltpu.CompilerParams(vmem_limit_bytes=6 << 20),
        cost_estimate=cost(1.0),
        name="assemble",
    )(*sides)
    return [o.reshape(count * rows, -1) for o in outs]


class Product:
    def __init__(self, x, y, blocks):
        self.x, self.y = x, y
        self.shape = (blocks, x.shape[1] // blocks, y.shape[1])
        self.size = x.shape[1] * y.shape[1]


def route_kernel(plan, kinds, count_out, *refs):
    me = lax.axis_index("dp")
    ins, outs, refs = [], [], list(refs)
    for is_product in kinds:
        ins.append((refs.pop(0), refs.pop(0)) if is_product else refs.pop(0))
    outs, made = refs[:count_out], refs[count_out:]
    for index, is_product in enumerate(kinds):
        if is_product:
            x_ref, y_ref = ins[index]
            ins[index] = made.pop(0)
            ins[index][...] = matmul_tn(x_ref[...], y_ref[...]).astype(BF16).reshape(ins[index].shape)
    for pieces, sizes, at, shift, grouped in plan:
        size = sizes[at]
        inner = 1
        for extent in sizes[at + 1 :]:
            inner *= extent
        rest = inner
        for extent in sizes[:at]:
            rest *= extent
        coord = lax.bitwise_and(lax.shift_right_logical(me, shift), size - 1)
        log_inner = inner.bit_length() - 1
        if grouped:
            whole = outs.pop(0)
            targets = [whole.at[j * rest : (j + 1) * rest] for j in range(size)]
        else:
            targets = [outs.pop(0) for _ in range(size)]
        for j, target in enumerate(targets):
            side = j if grouped else lax.bitwise_xor(coord, j)

            @pl.loop(0, rest)
            def _(r, target=target, side=side):
                upper = lax.shift_right_logical(r, log_inner)
                source = (upper * size + side) * inner + lax.bitwise_and(r, inner - 1)
                col = 0
                for piece in pieces:
                    width = piece[0][2] - piece[0][1]
                    first, low, high = piece[0]
                    value = ins[first][source, :, low:high]
                    if len(piece) > 1:
                        value = value.astype(F32)
                        for index, low, high in piece[1:]:
                            value = value + ins[index][source, :, low:high].astype(F32)
                    target[r, :, col : col + width] = value.astype(BF16)
                    col += width


def route(groups, name, grouped=False):
    arrays, plan, shapes = [], [], []
    for pieces, left, axis in groups:
        entries = []
        for piece in pieces:
            entry = []
            for array, low, high in piece:
                known = [i for i, other in enumerate(arrays) if other is array]
                if not known:
                    known = [len(arrays)]
                    arrays.append(array)
                entry.append((known[0], low, high))
            entries.append(tuple(entry))
        at = left.index(axis)
        plan.append((tuple(entries), tuple(size for _, size in left), at, axis[0], grouped))
        total = sum(piece[0][2] - piece[0][1] for piece in pieces)
        array = pieces[0][0][0]
        if grouped:
            shapes.append((1, (array.shape[0], array.shape[1], total)))
        else:
            shapes.append((axis[1], (array.shape[0] // axis[1], array.shape[1], total)))
    vmem = pl.BlockSpec(memory_space=pltpu.VMEM)
    out_shape = [jax.ShapeDtypeStruct(shape, BF16) for size, shape in shapes for _ in range(size)]
    kinds = tuple(isinstance(array, Product) for array in arrays)
    operands, scratch = [], []
    for array, is_product in zip(arrays, kinds):
        operands += [array.x, array.y] if is_product else [array]
        if is_product:
            scratch.append(pltpu.VMEM(array.shape, BF16))
    flat = pl.pallas_call(
        functools.partial(route_kernel, tuple(plan), kinds, len(out_shape)),
        out_shape=out_shape,
        in_specs=[vmem] * len(operands),
        out_specs=[vmem] * len(out_shape),
        scratch_shapes=scratch,
        compiler_params=pltpu.CompilerParams(vmem_limit_bytes=(20 if scratch else 6) << 20),
        cost_estimate=cost(1.0),
        name=name,
    )(*operands)
    outs = []
    for size, _ in shapes:
        outs.append(list(flat[:size]))
        flat = flat[size:]
    return outs


class Scatter:
    def __init__(self, arrays, orders, axes, name, group_last=False):
        self.group_last = group_last
        n = lax.axis_size("dp")
        self.name = name
        self.orders = [list(o) for o in orders]
        self.lefts = [list(axes) for _ in orders]
        self.pieces = []
        shaped = {}
        for parts in arrays:
            pieces = []
            if parts is None:
                self.pieces.append(None)
                continue
            for g, low, high in parts:
                if id(g) not in shaped:
                    shaped[id(g)] = g if isinstance(g, Product) else g.reshape(n, g.shape[0] // n, g.shape[1])
                pieces.append([(shaped[id(g)], low, high)])
            self.pieces.append(pieces)
        self.count = 0

    def deal(self):
        self.count += 1
        merged = len(self.pieces) > 1 and len(self.lefts[0]) < 3 and self.lefts[0] == self.lefts[1]
        groups = []
        if merged:
            groups.append((sum(self.pieces, []), self.lefts[0], self.orders[0][0]))
            self.orders, self.lefts = self.orders[:1], self.lefts[:1]
        else:
            for parts, left, order in zip(self.pieces, self.lefts, self.orders):
                groups.append((parts, left, order[0]))
        self.grouped = self.group_last and len(groups) == 1 and len(self.lefts[0]) == 1
        self.dealt = route(groups, f"{self.name}_deal_{self.count}", self.grouped)
        return self.dealt

    def send(self):
        pieces, lefts, orders = [], [], []
        for parts, left, order in zip(self.dealt, self.lefts, self.orders):
            shift, size = order[0]
            with jax.named_scope(f"{self.name}_{self.count}"):
                if self.grouped:
                    n = lax.axis_size("dp")
                    members = [[i | (j << shift) for j in range(size)] for i in range(n) if not (i >> shift) % size]
                    whole = lax.all_to_all(
                        parts[0], "dp", split_axis=0, concat_axis=0, axis_index_groups=members, tiled=True
                    )
                    rest = whole.shape[0] // size
                    got = [whole[j * rest : (j + 1) * rest] for j in range(size)]
                else:
                    got = [parts[0]] + [
                        xor_permute(parts[j], "dp", j << shift) for j in range(1, size)
                    ]
            pieces.append([[(x, 0, x.shape[2]) for x in got]])
            lefts.append([axis for axis in left if axis != order[0]])
            orders.append(order[1:])
        self.pieces, self.lefts, self.orders = pieces, lefts, orders

    def set_part(self, i, parts):
        self.pieces[i] = Scatter([parts], [self.orders[i]], self.lefts[i], self.name).pieces[0]

    def deal_one(self, i):
        return route([(self.pieces[i], self.lefts[i], self.orders[i][0])], f"{self.name}_deal_1{i}")[0]

    def send_one(self, i, parts):
        self.count = 1
        shift, size = self.orders[i][0]
        with jax.named_scope(f"{self.name}_1{i}"):
            got = [parts[0]] + [xor_permute(parts[j], "dp", j << shift) for j in range(1, size)]
        self.pieces[i] = [[(x, 0, x.shape[2]) for x in got]]
        self.lefts[i] = [axis for axis in self.lefts[i] if axis != self.orders[i][0]]
        self.orders[i] = self.orders[i][1:]

    def after(self, *others):
        arrays = [x for (piece,) in self.pieces for x, _, _ in piece[1:]]
        arrays = list(lax.optimization_barrier((tuple(arrays), others))[0])
        self.pieces = [
            [[piece[0]] + [(arrays.pop(0), low, high) for _, low, high in piece[1:]]] for (piece,) in self.pieces
        ]

    def before(self, x):
        arrays = [y for (piece,) in self.pieces for y, _, _ in piece]
        x, arrays = lax.optimization_barrier((x, tuple(arrays)))
        arrays = list(arrays)
        self.pieces = [[[(arrays.pop(0), low, high) for _, low, high in piece]] for (piece,) in self.pieces]
        return x

    def total(self):
        outs = []
        for (piece,) in self.pieces:
            parts = [x[0].astype(F32) for x, _, _ in piece]
            while len(parts) > 1:
                parts = [parts[i] + parts[i + 1] for i in range(0, len(parts), 2)]
            outs.append(parts[0])
        return outs[0] if len(outs) == 1 else jnp.concatenate(outs, axis=1)

    def finish_stages(self):
        while self.orders[0]:
            self.deal()
            self.send()

    def finish(self):
        self.finish_stages()
        return self.total()


def attend_forward_kernel(block, qkv_ref, bias_ref, *refs):
    ctx_ref, lse_ref = refs[-2:]
    length = qkv_ref.shape[0]
    bias = bias_ref[...]
    for head in range(2):
        low = head * HEAD_DIM
        keys = qkv_ref[:, PAIR + low : PAIR + low + HEAD_DIM]
        values_t = qkv_ref[:, 2 * PAIR + low : 2 * PAIR + low + HEAD_DIM].T
        for start in range(0, length, block):
            queries = qkv_ref[start : start + block, low : low + HEAD_DIM]
            scores = matmul_nt(keys, queries) + bias
            top = jnp.max(scores, axis=0, keepdims=True)
            exponent = jnp.exp(scores - top)
            total = jnp.sum(exponent, axis=0, keepdims=True)
            context_t = matmul(values_t, exponent.astype(BF16)) * (1.0 / total)
            ctx_ref[start : start + block, low : low + HEAD_DIM] = context_t.T.astype(BF16)
            lse_ref[0, head : head + 1, start : start + block] = top + jnp.log(total)


def attend_forward(qkv, bias, first, pairs, total, known=()):
    length = qkv.shape[0]
    return pl.pallas_call(
        functools.partial(attend_forward_kernel, min(256, length)),
        grid=(pairs,),
        out_shape=(
            jax.ShapeDtypeStruct((length, total * PAIR), BF16),
            jax.ShapeDtypeStruct((total, 2, length), F32),
        ),
        in_specs=[
            pl.BlockSpec((length, 3 * PAIR), lambda p: (0, p + first)),
            pl.BlockSpec((length, 1), lambda p: (0, 0)),
        ]
        + [pl.BlockSpec(memory_space=pl.ANY)] * len(known),
        out_specs=(
            pl.BlockSpec((length, PAIR), lambda p: (0, p + first)),
            pl.BlockSpec((1, 2, length), lambda p: (p + first, 0, 0)),
        ),
        input_output_aliases={2: 0, 3: 1} if known else {},
        compiler_params=pltpu.CompilerParams(vmem_limit_bytes=10 << 20),
        cost_estimate=cost(5.9 * pairs),
        name="attend_forward",
    )(qkv, bias, *known)


def attend_backward_kernel(block, qkv_ref, dctx_ref, lse_ref, bias_ref, *refs):
    out_ref, sums_ref, dk_ref, dv_ref = refs[-4:]
    length = qkv_ref.shape[0]
    bias = bias_ref[...]
    for head in range(2):
        low = head * HEAD_DIM
        keys = qkv_ref[:, PAIR + low : PAIR + low + HEAD_DIM]
        keys_t = keys.T
        values = qkv_ref[:, 2 * PAIR + low : 2 * PAIR + low + HEAD_DIM]
        query_sum = jnp.zeros((1, HEAD_DIM), F32)
        for start in range(0, length, block):
            queries = qkv_ref[start : start + block, low : low + HEAD_DIM]
            grads = dctx_ref[start : start + block, low : low + HEAD_DIM]
            lse = lse_ref[0, head : head + 1, start : start + block]
            probs = jnp.exp(matmul_nt(keys, queries) + bias - lse)
            grad_probs = matmul_nt(values, grads)
            inner = jnp.sum(probs * grad_probs, axis=0, keepdims=True)
            grad_scores = (probs * (grad_probs - inner)).astype(BF16)
            dv = matmul(probs.astype(BF16), grads)
            dk = matmul(grad_scores, queries)
            if start == 0:
                dk_ref[...] = dk
                dv_ref[...] = dv
            else:
                dk_ref[...] += dk
                dv_ref[...] += dv
            dq = (matmul(keys_t, grad_scores) * HEAD_DIM ** (-0.5)).T
            query_sum = query_sum + jnp.sum(dq, axis=0, keepdims=True)
            out_ref[start : start + block, low : low + HEAD_DIM] = dq.astype(BF16)
        dk = dk_ref[...]
        dv = dv_ref[...]
        out_ref[:, PAIR + low : PAIR + low + HEAD_DIM] = dk.astype(BF16)
        out_ref[:, 2 * PAIR + low : 2 * PAIR + low + HEAD_DIM] = dv.astype(BF16)
        sums_ref[0, 0:1, low : low + HEAD_DIM] = query_sum
        sums_ref[0, 1:2, low : low + HEAD_DIM] = jnp.sum(dv, axis=0, keepdims=True)


def attend_backward(qkv, dctx, lse, bias, first, pairs, total, known=()):
    length = qkv.shape[0]
    return pl.pallas_call(
        functools.partial(attend_backward_kernel, min(256, length)),
        grid=(pairs,),
        out_shape=(
            jax.ShapeDtypeStruct((length, total * 3 * PAIR), BF16),
            jax.ShapeDtypeStruct((total, 2, PAIR), F32),
        ),
        in_specs=[
            pl.BlockSpec((length, 3 * PAIR), lambda p: (0, p + first)),
            pl.BlockSpec((length, PAIR), lambda p: (0, p + first)),
            pl.BlockSpec((1, 2, length), lambda p: (p + first, 0, 0)),
            pl.BlockSpec((length, 1), lambda p: (0, 0)),
        ]
        + [pl.BlockSpec(memory_space=pl.ANY)] * len(known),
        out_specs=(
            pl.BlockSpec((length, 3 * PAIR), lambda p: (0, p + first)),
            pl.BlockSpec((1, 2, PAIR), lambda p: (p + first, 0, 0)),
        ),
        input_output_aliases={4: 0, 5: 1} if known else {},
        scratch_shapes=[pltpu.VMEM((length, HEAD_DIM), F32), pltpu.VMEM((length, HEAD_DIM), F32)],
        compiler_params=pltpu.CompilerParams(vmem_limit_bytes=10 << 20),
        cost_estimate=cost(7.3 * pairs),
        name="attend_backward",
    )(qkv, dctx, lse, bias, *known)


def call(kernel, outs, args, name, us, vmem_mib=10, scratch=()):
    spec = pl.BlockSpec(memory_space=pltpu.VMEM)
    return pl.pallas_call(
        kernel,
        out_shape=[jax.ShapeDtypeStruct(shape, kind) for shape, kind in outs],
        in_specs=[spec] * len(args),
        out_specs=[spec] * len(outs),
        scratch_shapes=list(scratch),
        compiler_params=pltpu.CompilerParams(vmem_limit_bytes=vmem_mib << 20),
        cost_estimate=cost(us),
        name=name,
    )(*args)


def row_blocks(rows, block):
    block = min(block, rows)
    return rows // block, block


def rows_at(i, block):
    return pl.ds(pl.multiple_of(i * block, block), block)


def project_kernel(x_ref, w_ref, bias_ref, scale_ref, out_ref):
    count, block = row_blocks(x_ref.shape[0], 512)

    @pl.loop(0, count)
    def _(i):
        at = rows_at(i, block)
        out_ref[at, :] = ((matmul(x_ref[at, :], w_ref[...]) + bias_ref[...]) * scale_ref[...]).astype(BF16)


def part_kernel(low, high, x_ref, w_ref, out_ref):
    out_ref[...] = matmul_nt(x_ref[low:high, :], w_ref[...]).astype(BF16)


def exchanged_parts(x, w, name):
    half = x.shape[0] // 2
    own, got = [], []
    for number in range(2):
        (part,) = call(
            functools.partial(part_kernel, number * half, (number + 1) * half),
            [((half, w.shape[0]), BF16)],
            (x, w),
            f"{name}_{number}",
            1.5,
        )
        if number == 0:
            x = tie(x, part)
        own.append(part)
        with jax.named_scope(f"{name}_{number}"):
            got.append(xor_permute(part, "mp", 1))
    return own + got[::-1]


def halves(parts, body, rows, block):
    count, block = row_blocks(rows // 2, block)
    for number in range(2):
        own_ref, got_ref = parts[number], parts[2 + number]

        @pl.loop(0, count)
        def _(i, number=number, own_ref=own_ref, got_ref=got_ref):
            at = rows_at(i, block)
            total = own_ref[at, :].astype(F32) + got_ref[at, :].astype(F32)
            body(number, at, rows_at(i + number * count, block), total)


def middle_kernel(x_ref, p0, p1, p2, p3, vec_ref, w_ref, bias_ref, normed_ref, rstd_ref, low_ref, act_ref, slope_ref):
    def body(number, half_at, at, total):
        mixed = x_ref[at, :].astype(F32) + total + vec_ref[2:3, :]
        normed, rstd = norm_forward(mixed)
        normed_ref[at, :] = normed.astype(BF16)
        rstd_ref[at, :] = rstd
        low = (normed * vec_ref[0:1, :] + vec_ref[3:4, :]).astype(BF16)
        low_ref[at, :] = low
        u = matmul(low, w_ref[...]) + bias_ref[...]
        half_cdf = 0.5 * (1.0 + lax.erf(u * root_half))
        act_ref[at, :] = (u * half_cdf).astype(BF16)
        slope_ref[at, :] = (half_cdf + u * jnp.exp(-0.5 * u * u) * inv_root_two_pi).astype(BF16)

    halves((p0, p1, p2, p3), body, x_ref.shape[0], 256)


def outer_kernel(normed_ref, p0, p1, p2, p3, cot_own_ref, cot_got0, cot_got1, vec_ref, out_ref, low_ref, sums_ref, cot_ref):
    sums_ref[...] = jnp.zeros_like(sums_ref)

    half = cot_own_ref.shape[0]
    for index, source in enumerate((cot_own_ref, cot_got0, cot_got1)):
        low = 0 if index == 0 else half + (index - 1) * (half // 2)
        cot_ref[low : low + source.shape[0], :] = source[...]

    def body(number, half_at, at, total):
        mixed = normed_ref[at, :].astype(F32) * vec_ref[0:1, :] + vec_ref[3:4, :] + total + vec_ref[4:5, :]
        normed, rstd = norm_forward(mixed)
        if number == 0:
            out_ref[at, :] = (normed * vec_ref[1:2, :] + vec_ref[5:6, :]).astype(BF16)
        cot = cot_ref[at, :].astype(F32)
        grad, grad_gain, grad_shift = norm_backward(cot, normed, rstd, vec_ref[1:2, :])
        low_ref[at, :] = grad.astype(BF16)
        sums_ref[0:1, :] += grad_gain
        sums_ref[1:2, :] += grad_shift
        sums_ref[2:3, :] += jnp.sum(grad, axis=0, keepdims=True)

    halves((p0, p1, p2, p3), body, normed_ref.shape[0], 256)


def hidden_grad_kernel(grad_ref, w_ref, slope_ref, out_ref, sums_ref):
    count, block = row_blocks(grad_ref.shape[0], 256)
    sums_ref[...] = jnp.zeros_like(sums_ref)

    @pl.loop(0, count)
    def _(i):
        at = rows_at(i, block)
        grad = matmul(grad_ref[at, :], w_ref[...]) * slope_ref[at, :].astype(F32)
        out_ref[at, :] = grad.astype(BF16)
        sums_ref[...] += jnp.sum(grad, axis=0, keepdims=True)


def inner_kernel(
    grad_in_ref, p0, p1, p2, p3, normed_ref, rstd_ref, vec_ref, w_ref, own_grad_ref, low_ref, ctx_ref, sums_ref
):
    sums_ref[...] = jnp.zeros_like(sums_ref)

    def body(number, half_at, at, total):
        given = grad_in_ref[at, :].astype(F32) + total
        grad, grad_gain, grad_shift = norm_backward(given, normed_ref[at, :].astype(F32), rstd_ref[at, :], vec_ref[0:1, :])
        low = grad.astype(BF16)
        low_ref[at, :] = low
        ctx_ref[at, :] = matmul(low, w_ref[...]).astype(BF16)
        sums_ref[0:1, :] += grad_gain
        sums_ref[1:2, :] += grad_shift
        sums_ref[2:3, :] += jnp.sum(grad, axis=0, keepdims=True)
        if number == 0:
            own_grad_ref[at, :] = grad

    halves((p0, p1, p2, p3), body, normed_ref.shape[0], 256)


def input_grad_kernel(x_ref, w_ref, grad_ref, keep_ref, send_ref):
    half = keep_ref.shape[0]
    send_ref[...] = matmul_nt(x_ref[half:, :], w_ref[...]).astype(BF16)
    keep_ref[...] = grad_ref[...] + matmul_nt(x_ref[:half, :], w_ref[...])


def norm_forward(rows):
    center = rows - jnp.mean(rows, axis=1, keepdims=True)
    rstd = lax.rsqrt(jnp.mean(center * center, axis=1, keepdims=True) + eps_norm)
    return center * rstd, rstd


def norm_backward(grad, normed, rstd, gain):
    scaled = grad * gain
    inner = (
        scaled
        - jnp.mean(scaled, axis=1, keepdims=True)
        - normed * jnp.mean(scaled * normed, axis=1, keepdims=True)
    )
    return (
        rstd * inner,
        jnp.sum(grad * normed, axis=0, keepdims=True),
        jnp.sum(grad, axis=0, keepdims=True),
    )


def from_other(x):
    half = x.shape[0] // 2
    return [xor_permute(x[:half], "mp", 1), xor_permute(x[half:], "mp", 1)]


def deal_rows(x, deal_order):
    return x[0].at[:, deal_order].get(mode="promise_in_bounds").transpose(1, 0, 2)


def exchange_in(dealt, *others):
    dealt = tie(dealt, *others)
    arrived = lax.all_to_all(dealt, "dp", split_axis=0, concat_axis=0, tiled=True)
    return arrived.reshape(-1, dealt.shape[2])


def exchange_out(rows, extra):
    n = lax.axis_size("dp")
    with jax.named_scope("out_rows"):
        blocks = rows.reshape(n, rows.shape[0] // n, rows.shape[1])
        blocks = jnp.concatenate([blocks, jnp.broadcast_to(extra, (n,) + extra.shape)], axis=1)
        return lax.all_to_all(blocks, "dp", split_axis=0, concat_axis=0, tiled=True)


def taken_out(sent, count):
    return sent[:, :count].transpose(1, 0, 2)[None], sent[:, count:]


def put_split(out_ref, row, count, value):
    high = value.astype(BF16)
    out_ref[row : row + 1, :] = high
    out_ref[row + count : row + count + 1, :] = (value - high.astype(F32)).astype(BF16)


def early_kernel(one_ref, two_ref, up_ref, out_ref):
    first = lax.axis_index("mp") == 0
    width = one_ref.shape[1]
    pieces = up_ref.shape[1] // width
    count = 3 + pieces
    out_ref[...] = jnp.zeros_like(out_ref)
    for row in range(3):
        put_split(out_ref, row, count, jnp.where(first, one_ref[row : row + 1, :], two_ref[row : row + 1, :]))
    for piece in range(pieces):
        put_split(out_ref, 3 + piece, count, up_ref[0:1, piece * width : (piece + 1) * width])


def late_kernel(pairs, keep_ref, g0, g1, sums_ref, rows_ref, out_ref):
    half = keep_ref.shape[0] // 2
    for index, source in enumerate((g0, g1)):
        at = slice(index * half, (index + 1) * half)
        rows_ref[at, :] = (keep_ref[at, :] + source[...].astype(F32)).astype(BF16)
    out_ref[...] = jnp.zeros_like(out_ref)
    for which in range(2):
        for pair in range(pairs):
            col = (which * pairs + pair) * PAIR
            value = sums_ref[pair, which : which + 1, :]
            high = value.astype(BF16)
            out_ref[0:1, col : col + PAIR] = high
            out_ref[1:2, col : col + PAIR] = (value - high.astype(F32)).astype(BF16)


def gathered_kernel(count, x_ref, out_ref):
    out_ref[...] = jnp.zeros_like(out_ref)

    @pl.loop(0, x_ref.shape[0])
    def _(i):
        x = x_ref[i].astype(F32)
        out_ref[...] += x[:count, :] + x[count : 2 * count, :]


def local(
    tokens, cotangent, lengths, deal_order, attn_in, attn_out, ffn_in, ffn_out,
    attn_bias, ffn_bias, norm_gain, shifts,
):
    dp_size = lax.axis_size("dp")
    mp_rank = lax.axis_index("mp")
    dp_rank = lax.axis_index("dp")
    axes = dp_axes(dp_size)
    low = axes[-2:]
    high = axes[:-2]
    order_one = high + low
    order_two = high + low[::-1]
    high_two = pairs_of(high)
    back_one = low[::-1] + high[::-1]
    back_two = low + high[::-1]

    width = tokens.shape[3]
    half_len = tokens.shape[1] * dp_size
    seq_len = 2 * half_len
    head_cols = attn_in.shape[3]
    hidden_cols = ffn_in.shape[2]
    pairs = head_cols // PAIR
    shard_rows = attn_in.shape[2]

    three = attn_in[0].reshape(3, shard_rows, pairs, PAIR).transpose(1, 2, 0, 3)
    three = three.reshape(shard_rows, 3 * head_cols)
    back_t = attn_out[0].T
    up = ffn_in[0]
    down_t = ffn_out[0].T

    cut_three = 128 * ((3 * head_cols // 128 + 1) // 2)
    pieces_three = [three[:, :cut_three], three[:, cut_three:]]
    rest = jnp.concatenate([back_t, up], axis=1)
    cut_rest = 128 * ((rest.shape[1] // 128 + 1) // 2)
    orders = [tuple(order_one), tuple(order_two)]

    first_three = gather_first(three, order_one, "ag_three")
    with jax.named_scope("in_tokens"):
        tok_own = exchange_in(deal_rows(tokens, deal_order), first_three)
        dealt_cot = deal_rows(cotangent, deal_order)
    w_down = lax.all_gather(down_t, "dp", axis=0, tiled=True)
    next_three = [
        gather_next(first_three[:, :, :cut_three], order_one, "ag_three"),
        gather_next(first_three[:, :, cut_three:], order_two, "ag_three"),
    ]
    rest, *next_three = lax.optimization_barrier((rest, *next_three))
    with jax.named_scope("ag_rest_first"):
        first_got = [rest[None]]
        for shift, size in order_one[:-3]:
            first_got = [stage_gather(x, "dp", shift, size) for x in first_got]
        shift, size = order_one[-3]
        first_own = first_got[0]
        first_got = [xor_permute(first_own, "dp", j << shift) for j in range(1, size)]
    sides_three = gather_last(next_three[0], order_one, "ag_three") + gather_last(
        next_three[1], order_two, "ag_three"
    )
    (w_three,) = assemble(sides_three, orders, [3 * head_cols])
    hb = jnp.concatenate([tok_own] + from_other(tok_own), axis=0)
    length = lengths[deal_order[dp_rank]]
    place = jnp.arange(seq_len, dtype=jnp.int32)
    place = jnp.where(mp_rank == 0, place, (place + half_len) % seq_len)
    bias_col = jnp.where(place < length, 0.0, negative_fill).astype(F32)[:, None]

    def own_cols(v, count):
        return jnp.where(mp_rank == 0, v[..., :count], v[..., count:])

    bias_pair = own_cols(attn_bias[0].astype(F32), head_cols).reshape(2, pairs, PAIR)
    bias_three = jnp.stack([bias_pair[0], jnp.zeros_like(bias_pair[0]), bias_pair[1]], axis=1).reshape(1, -1)
    bias_up = own_cols(ffn_bias[0].astype(F32), hidden_cols)[None]
    scale_three = jnp.concatenate(
        [jnp.full((pairs, 1, PAIR), HEAD_DIM ** (-0.5), F32), jnp.ones((pairs, 2, PAIR), F32)], axis=1
    ).reshape(1, -1)
    vec = jnp.concatenate([norm_gain[0], shifts[0]], axis=0).astype(F32)
    hb, bias_up, vec, bias_col, dealt_cot = lax.optimization_barrier((hb, bias_up, vec, bias_col, dealt_cot))
    big, wide, hidden_shape = (seq_len, width), (seq_len, head_cols), (seq_len, hidden_cols)

    (qkv,) = call(
        project_kernel, [((seq_len, 3 * head_cols), BF16)], (hb, w_three, bias_three, scale_three), "project", 2.4
    )
    attended = attend_forward(qkv, bias_col, 0, 1, pairs)
    attended, *first_got = lax.optimization_barrier((attended, *first_got))
    first_rest = jnp.concatenate([first_own] + first_got, axis=0)
    attended, first_rest = lax.optimization_barrier((attended, first_rest))
    own_rest = [first_rest[:, :, :cut_rest], first_rest[:, :, cut_rest:]]
    with jax.named_scope("ag_rest_next"):
        got_rest = [xor_permute(y, "dp", 1 << o[-2][0]) for y, o in zip(own_rest, orders)]
    if pairs > 2:
        attended = attend_forward(qkv, bias_col, 1, pairs - 2, pairs, attended)
    attended, *got_rest = lax.optimization_barrier((attended, *got_rest))
    next_rest = [jnp.concatenate(pair, axis=0) for pair in zip(own_rest, got_rest)]
    attended, *next_rest = lax.optimization_barrier((attended, *next_rest))
    sides_rest = gather_last(next_rest[0], order_one, "ag_rest") + gather_last(
        next_rest[1], order_two, "ag_rest"
    )
    if pairs > 1:
        attended = attend_forward(qkv, bias_col, pairs - 1, 1, pairs, attended)
    context, lse = attended
    with jax.named_scope("in_cot"):
        cot_own = exchange_in(dealt_cot, context)
    context, w_down = lax.optimization_barrier((context, w_down))
    w_back, w_up = assemble(sides_rest, orders, [head_cols, hidden_cols])
    mid_normed, mid_rstd, mid_low, hidden_low, slope = call(
        middle_kernel,
        [(big, BF16), ((seq_len, 1), F32), (big, BF16), (hidden_shape, BF16), (hidden_shape, BF16)],
        (hb, *exchanged_parts(context, w_back, "attn_part"), vec, w_up, bias_up),
        "middle",
        8,
    )

    result, grad_two_low, sums_two = call(
        outer_kernel,
        [((half_len, width), BF16), (big, BF16), ((3, width), F32)],
        (
            mid_normed,
            *exchanged_parts(hidden_low, w_down, "ffn_part"),
            cot_own,
            *from_other(cot_own),
            vec,
        ),
        "outer",
        4.5,
        scratch=[pltpu.VMEM(big, BF16)],
    )
    ffn = Scatter(
        [[(gradient(grad_two_low, hidden_low), 0, hidden_cols)], None],
        [low[::-1] + high_two[::-1], low + high_two[::-1]],
        high_two + low,
        "rs_ffn",
    )
    dealt = ffn.deal_one(0)
    grad_two_low, dealt = lax.optimization_barrier((grad_two_low, dealt))
    ffn.send_one(0, dealt)
    grad_hidden_low, grad_up_bias = call(
        hidden_grad_kernel,
        [(hidden_shape, BF16), ((1, hidden_cols), F32)],
        (grad_two_low, w_down, slope),
        "hidden_grad",
        3.3,
    )
    parts = exchanged_parts(grad_hidden_low, w_up, "mid_part")
    grad_hidden_low = tie(grad_hidden_low, parts[1])
    ffn.set_part(1, [(gradient(mid_low, grad_hidden_low), 0, hidden_cols)])
    dealt = ffn.deal_one(1)
    parts[2], dealt = lax.optimization_barrier((parts[2], dealt))
    ffn.send_one(1, dealt)
    grad_one, grad_one_low, grad_context, sums_one = call(
        inner_kernel,
        [((half_len, width), F32), (big, BF16), (wide, BF16), ((3, width), F32)],
        (grad_two_low, *parts, mid_normed, mid_rstd, vec, w_back),
        "inner",
        3.5,
    )
    early_count = 3 + hidden_cols // width
    (early,) = call(
        early_kernel, [((16 * -(-2 * early_count // 16), width), BF16)], (sums_one, sums_two, grad_up_bias), "early", 0.5
    )
    sent_tokens = exchange_out(result, early)
    grad_w_back = gradient(grad_one_low, context)

    given = ()
    if pairs > 1:
        given = attend_backward(qkv, grad_context, lse, bias_col, 0, pairs - 1, pairs)
        ffn.after(given)
    ffn.deal()
    grad_context, ffn.dealt = lax.optimization_barrier((grad_context, ffn.dealt))
    ffn.send()
    given = attend_backward(qkv, grad_context, lse, bias_col, pairs - 1, 1, pairs, given)
    dqkv, pair_sums = given
    ffn.after(given)
    ffn.deal()
    dqkv, ffn.dealt = lax.optimization_barrier((dqkv, ffn.dealt))
    ffn.send()
    grad_w_three = gradient(hb, dqkv)
    cut = 128 * ((4 * head_cols // 128 + 1) // 2)
    tail = Scatter(
        [
            [(grad_w_three, 0, cut)],
            [(grad_w_three, cut, 3 * head_cols), (grad_w_back, 0, head_cols)],
        ],
        [low[::-1] + high_two[::-1], low + high_two[::-1]],
        high_two + low,
        "rs_attn",
    )
    tail.deal()
    dqkv, tail.dealt = lax.optimization_barrier((dqkv, tail.dealt))
    tail.send()
    keep, sent = call(
        input_grad_kernel,
        [((half_len, width), F32), ((half_len, width), BF16)],
        (dqkv, w_three, grad_one),
        "input_grad",
        2.3,
    )
    got = from_other(sent)
    grad_in, late = call(
        functools.partial(late_kernel, pairs),
        [((half_len, width), BF16), ((8, 2 * head_cols), BF16)],
        (keep, *got, pair_sums),
        "late",
        1.0,
    )
    sent_grad = exchange_out(grad_in, late)
    block = half_len // dp_size
    out_tokens, early_all = taken_out(sent_tokens, block)
    out_grad, late_all = taken_out(sent_grad, block)
    tail.deal()
    ffn.deal()
    tail.dealt, ffn.dealt = lax.optimization_barrier((tail.dealt, ffn.dealt))
    ffn.send()
    tail.send()
    ffn_sum = ffn.finish()
    down_sum, up_sum = ffn_sum[:, :hidden_cols], ffn_sum[:, hidden_cols:]
    attn_sum = tail.finish()
    three_sum, back_sum = attn_sum[:, : 3 * head_cols], attn_sum[:, 3 * head_cols :]

    (early_sum,) = call(
        functools.partial(gathered_kernel, early_count), [((early_count, width), F32)], (early_all,), "early_sum", 0.5
    )
    (late_sum,) = call(functools.partial(gathered_kernel, 1), [((1, width), F32)], (late_all,), "late_sum", 0.5)

    def in_order(own):
        other = xor_permute(own, "mp", 1)
        return jnp.where(mp_rank == 0, own, other), jnp.where(mp_rank == 0, other, own)

    low_early, high_early = in_order(early_sum)
    low_late, high_late = in_order(late_sum)
    gain_out = jnp.stack([low_early[0], high_early[0]])[None]
    shift_out = jnp.stack([low_early[2], low_early[1], high_early[2], high_early[1]])[None]
    ffn_bias_out = jnp.concatenate([low_early[3:].reshape(1, -1), high_early[3:].reshape(1, -1)], axis=1)
    attn_bias_out = jnp.concatenate(
        [low_late.reshape(1, 2, head_cols), high_late.reshape(1, 2, head_cols)], axis=2
    )

    three_out = three_sum.reshape(shard_rows, pairs, 3, PAIR)
    three_out = three_out.transpose(2, 0, 1, 3).reshape(1, 3, shard_rows, head_cols)
    back_out = back_sum.T[None]
    up_out = up_sum[None]
    down_out = down_sum.T[None]
    return (
        out_tokens, out_grad, three_out, back_out, up_out, down_out,
        attn_bias_out, ffn_bias_out, gain_out, shift_out,
    )


def solution(mesh):
    placed = (
        P("mp", "dp", None, None),
        P("mp", "dp", None, None),
        P(),
        P(),
        P(None, None, "dp", "mp"),
        P(None, "mp", "dp"),
        P(None, "dp", "mp"),
        P(None, "mp", "dp"),
        P(),
        P(),
        P(),
        P(),
    )
    return jax.shard_map(
        local,
        mesh=mesh,
        in_specs=placed,
        out_specs=(
            P("mp", "dp", None, None),
            P("mp", "dp", None, None),
            P(None, None, "dp", "mp"),
            P(None, "mp", "dp"),
            P(None, "dp", "mp"),
            P(None, "mp", "dp"),
            P(),
            P(),
            P(),
            P(),
        ),
        check_vma=False,
    )
```

```python
import functools

import jax
import jax.numpy as jnp
from jax import lax
from jax.experimental import pallas as pl
from jax.experimental.pallas import tpu as pltpu
from jax.sharding import PartitionSpec as P

HEAD_DIM = 64
PAIR = 2 * HEAD_DIM

eps_norm = 1e-12
root_half = 0.7071067811865476
inv_root_two_pi = 0.3989422804014327
negative_fill = -1000000000.0
F32 = jnp.float32
BF16 = jnp.bfloat16


def matmul(a, b):
    return lax.dot_general(a, b, (((1,), (0,)), ((), ())), preferred_element_type=F32)


def matmul_nt(a, b):
    return lax.dot_general(a, b, (((1,), (1,)), ((), ())), preferred_element_type=F32)


def gradient(x, y):
    blocks = lax.axis_size("dp")
    if x.shape[1] % (16 * blocks) == 0:
        return Product(x, y, blocks)
    return matmul_tn(x, y).astype(BF16)


def matmul_tn(a, b):
    return lax.dot_general(a, b, (((0,), (0,)), ((), ())), preferred_element_type=F32)


FLOPS_PER_US = 172500000


def cost(us):
    return pl.CostEstimate(flops=int(us * FLOPS_PER_US), transcendentals=0, bytes_accessed=1000)


def xor_permute(x, axis, mask):
    n = lax.axis_size(axis)
    return lax.ppermute(x, axis, [(i, i ^ mask) for i in range(n)])


def dp_axes(n):
    bits = n.bit_length() - 1
    out, at = [], 0
    while at < bits:
        width = 1 if at < 2 else min(2, bits - at)
        out.append((at, 1 << width))
        at += width
    return out[::-1]


def pairs_of(axes):
    out = []
    for shift, size in axes:
        width = size.bit_length() - 1
        out += [(shift + bit, 2) for bit in reversed(range(width))]
    return out


def stage_parts(x, shift, size):
    return [x] + [xor_permute(x, "dp", j << shift) for j in range(1, size)]


def stage_gather(x, axis, shift, size):
    return jnp.concatenate(stage_parts(x, shift, size), axis=0)


def assemble_kernel(count, orders, cuts, *refs):
    me = lax.axis_index("dp")
    sources = [(refs[2 * i], refs[2 * i + 1]) for i in range(len(orders))]
    targets = refs[2 * len(orders) :]

    @pl.loop(0, count)
    def _(block):
        place = lax.bitwise_xor(me, block)
        at = 0
        for (own, received), order in zip(sources, orders):
            spot, stride = 0, 1
            for shift, size in order[:-1]:
                spot = spot + stride * lax.bitwise_and(lax.shift_right_logical(place, shift), size - 1)
                stride *= size
            side = lax.bitwise_and(lax.shift_right_logical(place, order[-1][0]), 1)
            cols = own.shape[2]

            def write(source, at=at, cols=cols, spot=spot):
                start = 0
                for target, (low, high) in zip(targets, cuts):
                    first, last = max(low, at), min(high, at + cols)
                    if first < last:
                        target[block, :, first - low : last - low] = source[spot, :, first - at : last - at]

            @pl.when(side == 0)
            def _():
                write(own)

            @pl.when(side == 1)
            def _():
                write(received)

            at += cols


def tie(x, *others):
    return lax.optimization_barrier((x,) + others)[0]


def gather_first(x, order, name):
    with jax.named_scope(name + "_first"):
        y = x[None]
        for shift, size in order[:-2]:
            y = stage_gather(y, "dp", shift, size)
        return y


def gather_next(y, order, name):
    with jax.named_scope(name + "_next"):
        return stage_gather(y, "dp", *order[-2])


def gather_last(y, order, name):
    with jax.named_scope(name + "_last"):
        return [y, xor_permute(y, "dp", 1 << order[-1][0])]


def assemble(sides, orders, widths):
    count = lax.axis_size("dp")
    rows = sides[0].shape[1]
    cuts, at = [], 0
    for w in widths:
        cuts.append((at, at + w))
        at += w
    vmem = pl.BlockSpec(memory_space=pltpu.VMEM)
    outs = pl.pallas_call(
        functools.partial(assemble_kernel, count, tuple(tuple(o) for o in orders), tuple(cuts)),
        out_shape=tuple(jax.ShapeDtypeStruct((count, rows, w), sides[0].dtype) for w in widths),
        in_specs=[vmem] * len(sides),
        out_specs=(vmem,) * len(widths),
        compiler_params=pltpu.CompilerParams(vmem_limit_bytes=6 << 20),
        cost_estimate=cost(1.0),
        name="assemble",
    )(*sides)
    return [o.reshape(count * rows, -1) for o in outs]


class Product:
    def __init__(self, x, y, blocks):
        self.x, self.y = x, y
        self.shape = (blocks, x.shape[1] // blocks, y.shape[1])
        self.size = x.shape[1] * y.shape[1]


def route_kernel(plan, kinds, count_out, *refs):
    me = lax.axis_index("dp")
    ins, outs, refs = [], [], list(refs)
    for is_product in kinds:
        ins.append((refs.pop(0), refs.pop(0)) if is_product else refs.pop(0))
    outs, made = refs[:count_out], refs[count_out:]
    for index, is_product in enumerate(kinds):
        if is_product:
            x_ref, y_ref = ins[index]
            ins[index] = made.pop(0)
            ins[index][...] = matmul_tn(x_ref[...], y_ref[...]).astype(BF16).reshape(ins[index].shape)
    for pieces, sizes, at, shift, grouped in plan:
        size = sizes[at]
        inner = 1
        for extent in sizes[at + 1 :]:
            inner *= extent
        rest = inner
        for extent in sizes[:at]:
            rest *= extent
        coord = lax.bitwise_and(lax.shift_right_logical(me, shift), size - 1)
        log_inner = inner.bit_length() - 1
        if grouped:
            whole = outs.pop(0)
            targets = [whole.at[j * rest : (j + 1) * rest] for j in range(size)]
        else:
            targets = [outs.pop(0) for _ in range(size)]
        for j, target in enumerate(targets):
            side = j if grouped else lax.bitwise_xor(coord, j)

            @pl.loop(0, rest)
            def _(r, target=target, side=side):
                upper = lax.shift_right_logical(r, log_inner)
                source = (upper * size + side) * inner + lax.bitwise_and(r, inner - 1)
                col = 0
                for piece in pieces:
                    width = piece[0][2] - piece[0][1]
                    first, low, high = piece[0]
                    value = ins[first][source, :, low:high]
                    if len(piece) > 1:
                        value = value.astype(F32)
                        for index, low, high in piece[1:]:
                            value = value + ins[index][source, :, low:high].astype(F32)
                    target[r, :, col : col + width] = value.astype(BF16)
                    col += width


def route(groups, name, grouped=False):
    arrays, plan, shapes = [], [], []
    for pieces, left, axis in groups:
        entries = []
        for piece in pieces:
            entry = []
            for array, low, high in piece:
                known = [i for i, other in enumerate(arrays) if other is array]
                if not known:
                    known = [len(arrays)]
                    arrays.append(array)
                entry.append((known[0], low, high))
            entries.append(tuple(entry))
        at = left.index(axis)
        plan.append((tuple(entries), tuple(size for _, size in left), at, axis[0], grouped))
        total = sum(piece[0][2] - piece[0][1] for piece in pieces)
        array = pieces[0][0][0]
        if grouped:
            shapes.append((1, (array.shape[0], array.shape[1], total)))
        else:
            shapes.append((axis[1], (array.shape[0] // axis[1], array.shape[1], total)))
    vmem = pl.BlockSpec(memory_space=pltpu.VMEM)
    out_shape = [jax.ShapeDtypeStruct(shape, BF16) for size, shape in shapes for _ in range(size)]
    kinds = tuple(isinstance(array, Product) for array in arrays)
    operands, scratch = [], []
    for array, is_product in zip(arrays, kinds):
        operands += [array.x, array.y] if is_product else [array]
        if is_product:
            scratch.append(pltpu.VMEM(array.shape, BF16))
    flat = pl.pallas_call(
        functools.partial(route_kernel, tuple(plan), kinds, len(out_shape)),
        out_shape=out_shape,
        in_specs=[vmem] * len(operands),
        out_specs=[vmem] * len(out_shape),
        scratch_shapes=scratch,
        compiler_params=pltpu.CompilerParams(vmem_limit_bytes=(20 if scratch else 6) << 20),
        cost_estimate=cost(1.0),
        name=name,
    )(*operands)
    outs = []
    for size, _ in shapes:
        outs.append(list(flat[:size]))
        flat = flat[size:]
    return outs


class Scatter:
    def __init__(self, arrays, orders, axes, name, group_last=False):
        self.group_last = group_last
        n = lax.axis_size("dp")
        self.name = name
        self.orders = [list(o) for o in orders]
        self.lefts = [list(axes) for _ in orders]
        self.pieces = []
        shaped = {}
        for parts in arrays:
            pieces = []
            if parts is None:
                self.pieces.append(None)
                continue
            for g, low, high in parts:
                if id(g) not in shaped:
                    shaped[id(g)] = g if isinstance(g, Product) else g.reshape(n, g.shape[0] // n, g.shape[1])
                pieces.append([(shaped[id(g)], low, high)])
            self.pieces.append(pieces)
        self.count = 0

    def deal(self):
        self.count += 1
        merged = len(self.pieces) > 1 and len(self.lefts[0]) < 3 and self.lefts[0] == self.lefts[1]
        groups = []
        if merged:
            groups.append((sum(self.pieces, []), self.lefts[0], self.orders[0][0]))
            self.orders, self.lefts = self.orders[:1], self.lefts[:1]
        else:
            for parts, left, order in zip(self.pieces, self.lefts, self.orders):
                groups.append((parts, left, order[0]))
        self.grouped = self.group_last and len(groups) == 1 and len(self.lefts[0]) == 1
        self.dealt = route(groups, f"{self.name}_deal_{self.count}", self.grouped)
        return self.dealt

    def send(self):
        pieces, lefts, orders = [], [], []
        for parts, left, order in zip(self.dealt, self.lefts, self.orders):
            shift, size = order[0]
            with jax.named_scope(f"{self.name}_{self.count}"):
                if self.grouped:
                    n = lax.axis_size("dp")
                    members = [[i | (j << shift) for j in range(size)] for i in range(n) if not (i >> shift) % size]
                    whole = lax.all_to_all(
                        parts[0], "dp", split_axis=0, concat_axis=0, axis_index_groups=members, tiled=True
                    )
                    rest = whole.shape[0] // size
                    got = [whole[j * rest : (j + 1) * rest] for j in range(size)]
                else:
                    got = [parts[0]] + [
                        xor_permute(parts[j], "dp", j << shift) for j in range(1, size)
                    ]
            pieces.append([[(x, 0, x.shape[2]) for x in got]])
            lefts.append([axis for axis in left if axis != order[0]])
            orders.append(order[1:])
        self.pieces, self.lefts, self.orders = pieces, lefts, orders

    def set_part(self, i, parts):
        self.pieces[i] = Scatter([parts], [self.orders[i]], self.lefts[i], self.name).pieces[0]

    def deal_one(self, i):
        return route([(self.pieces[i], self.lefts[i], self.orders[i][0])], f"{self.name}_deal_1{i}")[0]

    def send_one(self, i, parts):
        self.count = 1
        shift, size = self.orders[i][0]
        with jax.named_scope(f"{self.name}_1{i}"):
            got = [parts[0]] + [xor_permute(parts[j], "dp", j << shift) for j in range(1, size)]
        self.pieces[i] = [[(x, 0, x.shape[2]) for x in got]]
        self.lefts[i] = [axis for axis in self.lefts[i] if axis != self.orders[i][0]]
        self.orders[i] = self.orders[i][1:]

    def after(self, *others):
        arrays = [x for (piece,) in self.pieces for x, _, _ in piece[1:]]
        arrays = list(lax.optimization_barrier((tuple(arrays), others))[0])
        self.pieces = [
            [[piece[0]] + [(arrays.pop(0), low, high) for _, low, high in piece[1:]]] for (piece,) in self.pieces
        ]

    def before(self, x):
        arrays = [y for (piece,) in self.pieces for y, _, _ in piece]
        x, arrays = lax.optimization_barrier((x, tuple(arrays)))
        arrays = list(arrays)
        self.pieces = [[[(arrays.pop(0), low, high) for _, low, high in piece]] for (piece,) in self.pieces]
        return x

    def total(self):
        outs = []
        for (piece,) in self.pieces:
            parts = [x[0].astype(F32) for x, _, _ in piece]
            while len(parts) > 1:
                parts = [parts[i] + parts[i + 1] for i in range(0, len(parts), 2)]
            outs.append(parts[0])
        return outs[0] if len(outs) == 1 else jnp.concatenate(outs, axis=1)

    def finish_stages(self):
        while self.orders[0]:
            self.deal()
            self.send()

    def finish(self):
        self.finish_stages()
        return self.total()


def attend_forward_kernel(block, qkv_ref, bias_ref, *refs):
    ctx_ref, lse_ref = refs[-2:]
    length = qkv_ref.shape[0]
    bias = bias_ref[...]
    for head in range(2):
        low = head * HEAD_DIM
        keys = qkv_ref[:, PAIR + low : PAIR + low + HEAD_DIM]
        values_t = qkv_ref[:, 2 * PAIR + low : 2 * PAIR + low + HEAD_DIM].T
        for start in range(0, length, block):
            queries = qkv_ref[start : start + block, low : low + HEAD_DIM]
            scores = matmul_nt(keys, queries) + bias
            top = jnp.max(scores, axis=0, keepdims=True)
            exponent = jnp.exp(scores - top)
            total = jnp.sum(exponent, axis=0, keepdims=True)
            context_t = matmul(values_t, exponent.astype(BF16)) * (1.0 / total)
            ctx_ref[start : start + block, low : low + HEAD_DIM] = context_t.T.astype(BF16)
            lse_ref[0, head : head + 1, start : start + block] = top + jnp.log(total)


def attend_forward(qkv, bias, first, pairs, total, known=()):
    length = qkv.shape[0]
    return pl.pallas_call(
        functools.partial(attend_forward_kernel, min(256, length)),
        grid=(pairs,),
        out_shape=(
            jax.ShapeDtypeStruct((length, total * PAIR), BF16),
            jax.ShapeDtypeStruct((total, 2, length), F32),
        ),
        in_specs=[
            pl.BlockSpec((length, 3 * PAIR), lambda p: (0, p + first)),
            pl.BlockSpec((length, 1), lambda p: (0, 0)),
        ]
        + [pl.BlockSpec(memory_space=pl.ANY)] * len(known),
        out_specs=(
            pl.BlockSpec((length, PAIR), lambda p: (0, p + first)),
            pl.BlockSpec((1, 2, length), lambda p: (p + first, 0, 0)),
        ),
        input_output_aliases={2: 0, 3: 1} if known else {},
        compiler_params=pltpu.CompilerParams(vmem_limit_bytes=10 << 20),
        cost_estimate=cost(5.9 * pairs),
        name="attend_forward",
    )(qkv, bias, *known)


def attend_backward_kernel(block, qkv_ref, dctx_ref, lse_ref, bias_ref, *refs):
    out_ref, sums_ref, dk_ref, dv_ref = refs[-4:]
    length = qkv_ref.shape[0]
    bias = bias_ref[...]
    for head in range(2):
        low = head * HEAD_DIM
        keys = qkv_ref[:, PAIR + low : PAIR + low + HEAD_DIM]
        keys_t = keys.T
        values = qkv_ref[:, 2 * PAIR + low : 2 * PAIR + low + HEAD_DIM]
        query_sum = jnp.zeros((1, HEAD_DIM), F32)
        for start in range(0, length, block):
            queries = qkv_ref[start : start + block, low : low + HEAD_DIM]
            grads = dctx_ref[start : start + block, low : low + HEAD_DIM]
            lse = lse_ref[0, head : head + 1, start : start + block]
            probs = jnp.exp(matmul_nt(keys, queries) + bias - lse)
            grad_probs = matmul_nt(values, grads)
            inner = jnp.sum(probs * grad_probs, axis=0, keepdims=True)
            grad_scores = (probs * (grad_probs - inner)).astype(BF16)
            dv = matmul(probs.astype(BF16), grads)
            dk = matmul(grad_scores, queries)
            if start == 0:
                dk_ref[...] = dk
                dv_ref[...] = dv
            else:
                dk_ref[...] += dk
                dv_ref[...] += dv
            dq = (matmul(keys_t, grad_scores) * HEAD_DIM ** (-0.5)).T
            query_sum = query_sum + jnp.sum(dq, axis=0, keepdims=True)
            out_ref[start : start + block, low : low + HEAD_DIM] = dq.astype(BF16)
        dk = dk_ref[...]
        dv = dv_ref[...]
        out_ref[:, PAIR + low : PAIR + low + HEAD_DIM] = dk.astype(BF16)
        out_ref[:, 2 * PAIR + low : 2 * PAIR + low + HEAD_DIM] = dv.astype(BF16)
        sums_ref[0, 0:1, low : low + HEAD_DIM] = query_sum
        sums_ref[0, 1:2, low : low + HEAD_DIM] = jnp.sum(dv, axis=0, keepdims=True)


def attend_backward(qkv, dctx, lse, bias, first, pairs, total, known=()):
    length = qkv.shape[0]
    return pl.pallas_call(
        functools.partial(attend_backward_kernel, min(256, length)),
        grid=(pairs,),
        out_shape=(
            jax.ShapeDtypeStruct((length, total * 3 * PAIR), BF16),
            jax.ShapeDtypeStruct((total, 2, PAIR), F32),
        ),
        in_specs=[
            pl.BlockSpec((length, 3 * PAIR), lambda p: (0, p + first)),
            pl.BlockSpec((length, PAIR), lambda p: (0, p + first)),
            pl.BlockSpec((1, 2, length), lambda p: (p + first, 0, 0)),
            pl.BlockSpec((length, 1), lambda p: (0, 0)),
        ]
        + [pl.BlockSpec(memory_space=pl.ANY)] * len(known),
        out_specs=(
            pl.BlockSpec((length, 3 * PAIR), lambda p: (0, p + first)),
            pl.BlockSpec((1, 2, PAIR), lambda p: (p + first, 0, 0)),
        ),
        input_output_aliases={4: 0, 5: 1} if known else {},
        scratch_shapes=[pltpu.VMEM((length, HEAD_DIM), F32), pltpu.VMEM((length, HEAD_DIM), F32)],
        compiler_params=pltpu.CompilerParams(vmem_limit_bytes=10 << 20),
        cost_estimate=cost(7.3 * pairs),
        name="attend_backward",
    )(qkv, dctx, lse, bias, *known)


def call(kernel, outs, args, name, us, vmem_mib=10, scratch=()):
    spec = pl.BlockSpec(memory_space=pltpu.VMEM)
    return pl.pallas_call(
        kernel,
        out_shape=[jax.ShapeDtypeStruct(shape, kind) for shape, kind in outs],
        in_specs=[spec] * len(args),
        out_specs=[spec] * len(outs),
        scratch_shapes=list(scratch),
        compiler_params=pltpu.CompilerParams(vmem_limit_bytes=vmem_mib << 20),
        cost_estimate=cost(us),
        name=name,
    )(*args)


def row_blocks(rows, block):
    block = min(block, rows)
    return rows // block, block


def rows_at(i, block):
    return pl.ds(pl.multiple_of(i * block, block), block)


def project_kernel(x_ref, w_ref, bias_ref, scale_ref, out_ref):
    count, block = row_blocks(x_ref.shape[0], 512)

    @pl.loop(0, count)
    def _(i):
        at = rows_at(i, block)
        out_ref[at, :] = ((matmul(x_ref[at, :], w_ref[...]) + bias_ref[...]) * scale_ref[...]).astype(BF16)


def part_kernel(low, high, x_ref, w_ref, out_ref):
    out_ref[...] = matmul_nt(x_ref[low:high, :], w_ref[...]).astype(BF16)


def exchanged_parts(x, w, name):
    half = x.shape[0] // 2
    own, got = [], []
    for number in range(2):
        (part,) = call(
            functools.partial(part_kernel, number * half, (number + 1) * half),
            [((half, w.shape[0]), BF16)],
            (x, w),
            f"{name}_{number}",
            1.5,
        )
        if number == 0:
            x = tie(x, part)
        own.append(part)
        with jax.named_scope(f"{name}_{number}"):
            got.append(xor_permute(part, "mp", 1))
    return own + got[::-1]


def halves(parts, body, rows, block):
    count, block = row_blocks(rows // 2, block)
    for number in range(2):
        own_ref, got_ref = parts[number], parts[2 + number]

        @pl.loop(0, count)
        def _(i, number=number, own_ref=own_ref, got_ref=got_ref):
            at = rows_at(i, block)
            total = own_ref[at, :].astype(F32) + got_ref[at, :].astype(F32)
            body(number, at, rows_at(i + number * count, block), total)


def middle_kernel(x_ref, p0, p1, p2, p3, vec_ref, w_ref, bias_ref, normed_ref, rstd_ref, low_ref, act_ref, slope_ref):
    def body(number, half_at, at, total):
        mixed = x_ref[at, :].astype(F32) + total + vec_ref[2:3, :]
        normed, rstd = norm_forward(mixed)
        normed_ref[at, :] = normed.astype(BF16)
        rstd_ref[at, :] = rstd
        low = (normed * vec_ref[0:1, :] + vec_ref[3:4, :]).astype(BF16)
        low_ref[at, :] = low
        u = matmul(low, w_ref[...]) + bias_ref[...]
        half_cdf = 0.5 * (1.0 + lax.erf(u * root_half))
        act_ref[at, :] = (u * half_cdf).astype(BF16)
        slope_ref[at, :] = (half_cdf + u * jnp.exp(-0.5 * u * u) * inv_root_two_pi).astype(BF16)

    halves((p0, p1, p2, p3), body, x_ref.shape[0], 256)


def outer_kernel(normed_ref, p0, p1, p2, p3, cot_own_ref, cot_got0, cot_got1, vec_ref, out_ref, low_ref, sums_ref, cot_ref):
    sums_ref[...] = jnp.zeros_like(sums_ref)

    half = cot_own_ref.shape[0]
    for index, source in enumerate((cot_own_ref, cot_got0, cot_got1)):
        low = 0 if index == 0 else half + (index - 1) * (half // 2)
        cot_ref[low : low + source.shape[0], :] = source[...]

    def body(number, half_at, at, total):
        mixed = normed_ref[at, :].astype(F32) * vec_ref[0:1, :] + vec_ref[3:4, :] + total + vec_ref[4:5, :]
        normed, rstd = norm_forward(mixed)
        if number == 0:
            out_ref[at, :] = (normed * vec_ref[1:2, :] + vec_ref[5:6, :]).astype(BF16)
        cot = cot_ref[at, :].astype(F32)
        grad, grad_gain, grad_shift = norm_backward(cot, normed, rstd, vec_ref[1:2, :])
        low_ref[at, :] = grad.astype(BF16)
        sums_ref[0:1, :] += grad_gain
        sums_ref[1:2, :] += grad_shift
        sums_ref[2:3, :] += jnp.sum(grad, axis=0, keepdims=True)

    halves((p0, p1, p2, p3), body, normed_ref.shape[0], 256)


def hidden_grad_kernel(grad_ref, w_ref, slope_ref, out_ref, sums_ref):
    count, block = row_blocks(grad_ref.shape[0], 256)
    sums_ref[...] = jnp.zeros_like(sums_ref)

    @pl.loop(0, count)
    def _(i):
        at = rows_at(i, block)
        grad = matmul(grad_ref[at, :], w_ref[...]) * slope_ref[at, :].astype(F32)
        out_ref[at, :] = grad.astype(BF16)
        sums_ref[...] += jnp.sum(grad, axis=0, keepdims=True)


def inner_kernel(
    grad_in_ref, p0, p1, p2, p3, normed_ref, rstd_ref, vec_ref, w_ref, own_grad_ref, low_ref, ctx_ref, sums_ref
):
    sums_ref[...] = jnp.zeros_like(sums_ref)

    def body(number, half_at, at, total):
        given = grad_in_ref[at, :].astype(F32) + total
        grad, grad_gain, grad_shift = norm_backward(given, normed_ref[at, :].astype(F32), rstd_ref[at, :], vec_ref[0:1, :])
        low = grad.astype(BF16)
        low_ref[at, :] = low
        ctx_ref[at, :] = matmul(low, w_ref[...]).astype(BF16)
        sums_ref[0:1, :] += grad_gain
        sums_ref[1:2, :] += grad_shift
        sums_ref[2:3, :] += jnp.sum(grad, axis=0, keepdims=True)
        if number == 0:
            own_grad_ref[at, :] = grad

    halves((p0, p1, p2, p3), body, normed_ref.shape[0], 256)


def input_grad_kernel(x_ref, w_ref, grad_ref, keep_ref, send_ref):
    half = keep_ref.shape[0]
    send_ref[...] = matmul_nt(x_ref[half:, :], w_ref[...]).astype(BF16)
    keep_ref[...] = grad_ref[...] + matmul_nt(x_ref[:half, :], w_ref[...])


def norm_forward(rows):
    center = rows - jnp.mean(rows, axis=1, keepdims=True)
    rstd = lax.rsqrt(jnp.mean(center * center, axis=1, keepdims=True) + eps_norm)
    return center * rstd, rstd


def norm_backward(grad, normed, rstd, gain):
    scaled = grad * gain
    inner = (
        scaled
        - jnp.mean(scaled, axis=1, keepdims=True)
        - normed * jnp.mean(scaled * normed, axis=1, keepdims=True)
    )
    return (
        rstd * inner,
        jnp.sum(grad * normed, axis=0, keepdims=True),
        jnp.sum(grad, axis=0, keepdims=True),
    )


def from_other(x):
    half = x.shape[0] // 2
    return [xor_permute(x[:half], "mp", 1), xor_permute(x[half:], "mp", 1)]


def deal_rows(x, deal_order):
    return x[0].at[:, deal_order].get(mode="promise_in_bounds").transpose(1, 0, 2)


def exchange_in(dealt, *others):
    dealt = tie(dealt, *others)
    arrived = lax.all_to_all(dealt, "dp", split_axis=0, concat_axis=0, tiled=True)
    return arrived.reshape(-1, dealt.shape[2])


def exchange_out(rows, extra):
    n = lax.axis_size("dp")
    with jax.named_scope("out_rows"):
        blocks = rows.reshape(n, rows.shape[0] // n, rows.shape[1])
        blocks = jnp.concatenate([blocks, jnp.broadcast_to(extra, (n,) + extra.shape)], axis=1)
        return lax.all_to_all(blocks, "dp", split_axis=0, concat_axis=0, tiled=True)


def taken_out(sent, count):
    return sent[:, :count].transpose(1, 0, 2)[None], sent[:, count:]


def put_split(out_ref, row, count, value):
    high = value.astype(BF16)
    out_ref[row : row + 1, :] = high
    out_ref[row + count : row + count + 1, :] = (value - high.astype(F32)).astype(BF16)


def early_kernel(one_ref, two_ref, up_ref, out_ref):
    first = lax.axis_index("mp") == 0
    width = one_ref.shape[1]
    pieces = up_ref.shape[1] // width
    count = 3 + pieces
    out_ref[...] = jnp.zeros_like(out_ref)
    for row in range(3):
        put_split(out_ref, row, count, jnp.where(first, one_ref[row : row + 1, :], two_ref[row : row + 1, :]))
    for piece in range(pieces):
        put_split(out_ref, 3 + piece, count, up_ref[0:1, piece * width : (piece + 1) * width])


def late_kernel(pairs, keep_ref, g0, g1, sums_ref, rows_ref, out_ref):
    half = keep_ref.shape[0] // 2
    for index, source in enumerate((g0, g1)):
        at = slice(index * half, (index + 1) * half)
        rows_ref[at, :] = (keep_ref[at, :] + source[...].astype(F32)).astype(BF16)
    out_ref[...] = jnp.zeros_like(out_ref)
    for which in range(2):
        for pair in range(pairs):
            col = (which * pairs + pair) * PAIR
            value = sums_ref[pair, which : which + 1, :]
            high = value.astype(BF16)
            out_ref[0:1, col : col + PAIR] = high
            out_ref[1:2, col : col + PAIR] = (value - high.astype(F32)).astype(BF16)


def gathered_kernel(count, x_ref, out_ref):
    out_ref[...] = jnp.zeros_like(out_ref)

    @pl.loop(0, x_ref.shape[0])
    def _(i):
        x = x_ref[i].astype(F32)
        out_ref[...] += x[:count, :] + x[count : 2 * count, :]


def local(
    tokens, cotangent, lengths, deal_order, attn_in, attn_out, ffn_in, ffn_out,
    attn_bias, ffn_bias, norm_gain, shifts,
):
    dp_size = lax.axis_size("dp")
    mp_rank = lax.axis_index("mp")
    dp_rank = lax.axis_index("dp")
    axes = dp_axes(dp_size)
    low = axes[-2:]
    high = axes[:-2]
    order_one = high + low
    order_two = high + low[::-1]
    high_two = pairs_of(high)
    back_one = low[::-1] + high[::-1]
    back_two = low + high[::-1]

    width = tokens.shape[3]
    half_len = tokens.shape[1] * dp_size
    seq_len = 2 * half_len
    head_cols = attn_in.shape[3]
    hidden_cols = ffn_in.shape[2]
    pairs = head_cols // PAIR
    shard_rows = attn_in.shape[2]

    three = attn_in[0].reshape(3, shard_rows, pairs, PAIR).transpose(1, 2, 0, 3)
    three = three.reshape(shard_rows, 3 * head_cols)
    back_t = attn_out[0].T
    up = ffn_in[0]
    down_t = ffn_out[0].T

    cut_three = 128 * ((3 * head_cols // 128 + 1) // 2)
    pieces_three = [three[:, :cut_three], three[:, cut_three:]]
    rest = jnp.concatenate([back_t, up], axis=1)
    cut_rest = 128 * ((rest.shape[1] // 128 + 1) // 2)
    orders = [tuple(order_one), tuple(order_two)]

    first_three = gather_first(three, order_one, "ag_three")
    with jax.named_scope("in_tokens"):
        tok_own = exchange_in(deal_rows(tokens, deal_order), first_three)
        dealt_cot = deal_rows(cotangent, deal_order)
    w_down = lax.all_gather(down_t, "dp", axis=0, tiled=True)
    next_three = [
        gather_next(first_three[:, :, :cut_three], order_one, "ag_three"),
        gather_next(first_three[:, :, cut_three:], order_two, "ag_three"),
    ]
    rest, *next_three = lax.optimization_barrier((rest, *next_three))
    with jax.named_scope("ag_rest_first"):
        first_got = [rest[None]]
        for shift, size in order_one[:-3]:
            first_got = [stage_gather(x, "dp", shift, size) for x in first_got]
        shift, size = order_one[-3]
        first_own = first_got[0]
        first_got = [xor_permute(first_own, "dp", j << shift) for j in range(1, size)]
    sides_three = gather_last(next_three[0], order_one, "ag_three") + gather_last(
        next_three[1], order_two, "ag_three"
    )
    (w_three,) = assemble(sides_three, orders, [3 * head_cols])
    hb = jnp.concatenate([tok_own] + from_other(tok_own), axis=0)
    length = lengths[deal_order[dp_rank]]
    place = jnp.arange(seq_len, dtype=jnp.int32)
    place = jnp.where(mp_rank == 0, place, (place + half_len) % seq_len)
    bias_col = jnp.where(place < length, 0.0, negative_fill).astype(F32)[:, None]

    def own_cols(v, count):
        return jnp.where(mp_rank == 0, v[..., :count], v[..., count:])

    bias_pair = own_cols(attn_bias[0].astype(F32), head_cols).reshape(2, pairs, PAIR)
    bias_three = jnp.stack([bias_pair[0], jnp.zeros_like(bias_pair[0]), bias_pair[1]], axis=1).reshape(1, -1)
    bias_up = own_cols(ffn_bias[0].astype(F32), hidden_cols)[None]
    scale_three = jnp.concatenate(
        [jnp.full((pairs, 1, PAIR), HEAD_DIM ** (-0.5), F32), jnp.ones((pairs, 2, PAIR), F32)], axis=1
    ).reshape(1, -1)
    vec = jnp.concatenate([norm_gain[0], shifts[0]], axis=0).astype(F32)
    hb, bias_up, vec, bias_col, dealt_cot = lax.optimization_barrier((hb, bias_up, vec, bias_col, dealt_cot))
    big, wide, hidden_shape = (seq_len, width), (seq_len, head_cols), (seq_len, hidden_cols)

    (qkv,) = call(
        project_kernel, [((seq_len, 3 * head_cols), BF16)], (hb, w_three, bias_three, scale_three), "project", 2.4
    )
    attended = attend_forward(qkv, bias_col, 0, 1, pairs)
    attended, *first_got = lax.optimization_barrier((attended, *first_got))
    first_rest = jnp.concatenate([first_own] + first_got, axis=0)
    attended, first_rest = lax.optimization_barrier((attended, first_rest))
    own_rest = [first_rest[:, :, :cut_rest], first_rest[:, :, cut_rest:]]
    with jax.named_scope("ag_rest_next"):
        got_rest = [xor_permute(y, "dp", 1 << o[-2][0]) for y, o in zip(own_rest, orders)]
    if pairs > 2:
        attended = attend_forward(qkv, bias_col, 1, pairs - 2, pairs, attended)
    attended, *got_rest = lax.optimization_barrier((attended, *got_rest))
    next_rest = [jnp.concatenate(pair, axis=0) for pair in zip(own_rest, got_rest)]
    attended, *next_rest = lax.optimization_barrier((attended, *next_rest))
    sides_rest = gather_last(next_rest[0], order_one, "ag_rest") + gather_last(
        next_rest[1], order_two, "ag_rest"
    )
    if pairs > 1:
        attended = attend_forward(qkv, bias_col, pairs - 1, 1, pairs, attended)
    context, lse = attended
    with jax.named_scope("in_cot"):
        cot_own = exchange_in(dealt_cot, context)
    context, w_down = lax.optimization_barrier((context, w_down))
    w_back, w_up = assemble(sides_rest, orders, [head_cols, hidden_cols])
    mid_normed, mid_rstd, mid_low, hidden_low, slope = call(
        middle_kernel,
        [(big, BF16), ((seq_len, 1), F32), (big, BF16), (hidden_shape, BF16), (hidden_shape, BF16)],
        (hb, *exchanged_parts(context, w_back, "attn_part"), vec, w_up, bias_up),
        "middle",
        8,
    )

    result, grad_two_low, sums_two = call(
        outer_kernel,
        [((half_len, width), BF16), (big, BF16), ((3, width), F32)],
        (
            mid_normed,
            *exchanged_parts(hidden_low, w_down, "ffn_part"),
            cot_own,
            *from_other(cot_own),
            vec,
        ),
        "outer",
        4.5,
        scratch=[pltpu.VMEM(big, BF16)],
    )
    ffn = Scatter(
        [[(gradient(grad_two_low, hidden_low), 0, hidden_cols)], None],
        [low[::-1] + high_two[::-1], low + high_two[::-1]],
        high_two + low,
        "rs_ffn",
    )
    dealt = ffn.deal_one(0)
    grad_two_low, dealt = lax.optimization_barrier((grad_two_low, dealt))
    ffn.send_one(0, dealt)
    grad_hidden_low, grad_up_bias = call(
        hidden_grad_kernel,
        [(hidden_shape, BF16), ((1, hidden_cols), F32)],
        (grad_two_low, w_down, slope),
        "hidden_grad",
        3.3,
    )
    parts = exchanged_parts(grad_hidden_low, w_up, "mid_part")
    grad_hidden_low = tie(grad_hidden_low, parts[1])
    ffn.set_part(1, [(gradient(mid_low, grad_hidden_low), 0, hidden_cols)])
    dealt = ffn.deal_one(1)
    parts[2], dealt = lax.optimization_barrier((parts[2], dealt))
    ffn.send_one(1, dealt)
    grad_one, grad_one_low, grad_context, sums_one = call(
        inner_kernel,
        [((half_len, width), F32), (big, BF16), (wide, BF16), ((3, width), F32)],
        (grad_two_low, *parts, mid_normed, mid_rstd, vec, w_back),
        "inner",
        3.5,
    )
    early_count = 3 + hidden_cols // width
    (early,) = call(
        early_kernel, [((16 * -(-2 * early_count // 16), width), BF16)], (sums_one, sums_two, grad_up_bias), "early", 0.5
    )
    sent_tokens = exchange_out(result, early)
    grad_w_back = gradient(grad_one_low, context)

    given = ()
    if pairs > 1:
        given = attend_backward(qkv, grad_context, lse, bias_col, 0, pairs - 1, pairs)
        ffn.after(given)
    ffn.deal()
    grad_context, ffn.dealt = lax.optimization_barrier((grad_context, ffn.dealt))
    ffn.send()
    given = attend_backward(qkv, grad_context, lse, bias_col, pairs - 1, 1, pairs, given)
    dqkv, pair_sums = given
    ffn.after(given)
    ffn.deal()
    dqkv, ffn.dealt = lax.optimization_barrier((dqkv, ffn.dealt))
    ffn.send()
    grad_w_three = gradient(hb, dqkv)
    cut = 128 * ((4 * head_cols // 128 + 1) // 2)
    tail = Scatter(
        [
            [(grad_w_three, 0, cut)],
            [(grad_w_three, cut, 3 * head_cols), (grad_w_back, 0, head_cols)],
        ],
        [low[::-1] + high_two[::-1], low + high_two[::-1]],
        high_two + low,
        "rs_attn",
    )
    tail.deal()
    dqkv, tail.dealt = lax.optimization_barrier((dqkv, tail.dealt))
    tail.send()
    keep, sent = call(
        input_grad_kernel,
        [((half_len, width), F32), ((half_len, width), BF16)],
        (dqkv, w_three, grad_one),
        "input_grad",
        2.3,
    )
    got = from_other(sent)
    grad_in, late = call(
        functools.partial(late_kernel, pairs),
        [((half_len, width), BF16), ((8, 2 * head_cols), BF16)],
        (keep, *got, pair_sums),
        "late",
        1.0,
    )
    sent_grad = exchange_out(grad_in, late)
    block = half_len // dp_size
    out_tokens, early_all = taken_out(sent_tokens, block)
    out_grad, late_all = taken_out(sent_grad, block)
    tail.deal()
    ffn.after(tail.dealt)
    tail.send()
    ffn.deal()
    tail.deal()
    tail.dealt, ffn.dealt = lax.optimization_barrier((tail.dealt, ffn.dealt))
    ffn.send()
    tail.send()
    tail.deal()
    ffn.after(tail.dealt)
    tail.send()
    ffn_sum = ffn.finish()
    down_sum, up_sum = ffn_sum[:, :hidden_cols], ffn_sum[:, hidden_cols:]

    (early_sum,) = call(
        functools.partial(gathered_kernel, early_count), [((early_count, width), F32)], (early_all,), "early_sum", 0.5
    )
    (late_sum,) = call(functools.partial(gathered_kernel, 1), [((1, width), F32)], (late_all,), "late_sum", 0.5)

    def in_order(own):
        other = xor_permute(own, "mp", 1)
        return jnp.where(mp_rank == 0, own, other), jnp.where(mp_rank == 0, other, own)

    low_early, high_early = in_order(early_sum)
    low_late, high_late = in_order(late_sum)
    gain_out = jnp.stack([low_early[0], high_early[0]])[None]
    shift_out = jnp.stack([low_early[2], low_early[1], high_early[2], high_early[1]])[None]
    ffn_bias_out = jnp.concatenate([low_early[3:].reshape(1, -1), high_early[3:].reshape(1, -1)], axis=1)
    attn_bias_out = jnp.concatenate(
        [low_late.reshape(1, 2, head_cols), high_late.reshape(1, 2, head_cols)], axis=2
    )

    tail.after(out_grad)
    attn_sum = tail.finish()
    three_sum, back_sum = attn_sum[:, : 3 * head_cols], attn_sum[:, 3 * head_cols :]
    three_out = three_sum.reshape(shard_rows, pairs, 3, PAIR)
    three_out = three_out.transpose(2, 0, 1, 3).reshape(1, 3, shard_rows, head_cols)
    back_out = back_sum.T[None]
    up_out = up_sum[None]
    down_out = down_sum.T[None]
    return (
        out_tokens, out_grad, three_out, back_out, up_out, down_out,
        attn_bias_out, ffn_bias_out, gain_out, shift_out,
    )


def solution(mesh):
    placed = (
        P("mp", "dp", None, None),
        P("mp", "dp", None, None),
        P(),
        P(),
        P(None, None, "dp", "mp"),
        P(None, "mp", "dp"),
        P(None, "dp", "mp"),
        P(None, "mp", "dp"),
        P(),
        P(),
        P(),
        P(),
    )
    return jax.shard_map(
        local,
        mesh=mesh,
        in_specs=placed,
        out_specs=(
            P("mp", "dp", None, None),
            P("mp", "dp", None, None),
            P(None, None, "dp", "mp"),
            P(None, "mp", "dp"),
            P(None, "dp", "mp"),
            P(None, "mp", "dp"),
            P(),
            P(),
            P(),
            P(),
        ),
        check_vma=False,
    )
```

```python
import functools

import jax
import jax.numpy as jnp
from jax import lax
from jax.experimental import pallas as pl
from jax.experimental.pallas import tpu as pltpu
from jax.sharding import PartitionSpec as P

HEAD_DIM = 64
PAIR = 2 * HEAD_DIM

eps_norm = 1e-12
root_half = 0.7071067811865476
inv_root_two_pi = 0.3989422804014327
negative_fill = -1000000000.0
F32 = jnp.float32
BF16 = jnp.bfloat16


def matmul(a, b):
    return lax.dot_general(a, b, (((1,), (0,)), ((), ())), preferred_element_type=F32)


def matmul_nt(a, b):
    return lax.dot_general(a, b, (((1,), (1,)), ((), ())), preferred_element_type=F32)


def gradient(x, y):
    blocks = lax.axis_size("dp")
    if x.shape[1] % (16 * blocks) == 0:
        return Product(x, y, blocks)
    return matmul_tn(x, y).astype(BF16)


def matmul_tn(a, b):
    return lax.dot_general(a, b, (((0,), (0,)), ((), ())), preferred_element_type=F32)


FLOPS_PER_US = 172500000


def cost(us):
    return pl.CostEstimate(flops=int(us * FLOPS_PER_US), transcendentals=0, bytes_accessed=1000)


def xor_permute(x, axis, mask):
    n = lax.axis_size(axis)
    return lax.ppermute(x, axis, [(i, i ^ mask) for i in range(n)])


def dp_axes(n):
    bits = n.bit_length() - 1
    out, at = [], 0
    while at < bits:
        width = 1 if at < 2 else min(2, bits - at)
        out.append((at, 1 << width))
        at += width
    return out[::-1]


def pairs_of(axes):
    out = []
    for shift, size in axes:
        width = size.bit_length() - 1
        out += [(shift + bit, 2) for bit in reversed(range(width))]
    return out


def stage_parts(x, shift, size):
    return [x] + [xor_permute(x, "dp", j << shift) for j in range(1, size)]


def stage_gather(x, axis, shift, size):
    return jnp.concatenate(stage_parts(x, shift, size), axis=0)


def assemble_kernel(count, orders, cuts, *refs):
    me = lax.axis_index("dp")
    sources = [(refs[2 * i], refs[2 * i + 1]) for i in range(len(orders))]
    targets = refs[2 * len(orders) :]

    @pl.loop(0, count)
    def _(block):
        place = lax.bitwise_xor(me, block)
        at = 0
        for (own, received), order in zip(sources, orders):
            spot, stride = 0, 1
            for shift, size in order[:-1]:
                spot = spot + stride * lax.bitwise_and(lax.shift_right_logical(place, shift), size - 1)
                stride *= size
            side = lax.bitwise_and(lax.shift_right_logical(place, order[-1][0]), 1)
            cols = own.shape[2]

            def write(source, at=at, cols=cols, spot=spot):
                start = 0
                for target, (low, high) in zip(targets, cuts):
                    first, last = max(low, at), min(high, at + cols)
                    if first < last:
                        target[block, :, first - low : last - low] = source[spot, :, first - at : last - at]

            @pl.when(side == 0)
            def _():
                write(own)

            @pl.when(side == 1)
            def _():
                write(received)

            at += cols


def tie(x, *others):
    return lax.optimization_barrier((x,) + others)[0]


def gather_first(x, order, name):
    with jax.named_scope(name + "_first"):
        y = x[None]
        for shift, size in order[:-2]:
            y = stage_gather(y, "dp", shift, size)
        return y


def gather_next(y, order, name):
    with jax.named_scope(name + "_next"):
        return stage_gather(y, "dp", *order[-2])


def gather_last(y, order, name):
    with jax.named_scope(name + "_last"):
        return [y, xor_permute(y, "dp", 1 << order[-1][0])]


def assemble(sides, orders, widths):
    count = lax.axis_size("dp")
    rows = sides[0].shape[1]
    cuts, at = [], 0
    for w in widths:
        cuts.append((at, at + w))
        at += w
    vmem = pl.BlockSpec(memory_space=pltpu.VMEM)
    outs = pl.pallas_call(
        functools.partial(assemble_kernel, count, tuple(tuple(o) for o in orders), tuple(cuts)),
        out_shape=tuple(jax.ShapeDtypeStruct((count, rows, w), sides[0].dtype) for w in widths),
        in_specs=[vmem] * len(sides),
        out_specs=(vmem,) * len(widths),
        compiler_params=pltpu.CompilerParams(vmem_limit_bytes=6 << 20),
        cost_estimate=cost(1.0),
        name="assemble",
    )(*sides)
    return [o.reshape(count * rows, -1) for o in outs]


class Product:
    def __init__(self, x, y, blocks):
        self.x, self.y = x, y
        self.shape = (blocks, x.shape[1] // blocks, y.shape[1])
        self.size = x.shape[1] * y.shape[1]


def route_kernel(plan, kinds, count_out, *refs):
    me = lax.axis_index("dp")
    ins, outs, refs = [], [], list(refs)
    for is_product in kinds:
        ins.append((refs.pop(0), refs.pop(0)) if is_product else refs.pop(0))
    outs, made = refs[:count_out], refs[count_out:]
    for index, is_product in enumerate(kinds):
        if is_product:
            x_ref, y_ref = ins[index]
            ins[index] = made.pop(0)
            ins[index][...] = matmul_tn(x_ref[...], y_ref[...]).astype(BF16).reshape(ins[index].shape)
    for pieces, sizes, at, shift, grouped in plan:
        size = sizes[at]
        inner = 1
        for extent in sizes[at + 1 :]:
            inner *= extent
        rest = inner
        for extent in sizes[:at]:
            rest *= extent
        coord = lax.bitwise_and(lax.shift_right_logical(me, shift), size - 1)
        log_inner = inner.bit_length() - 1
        if grouped:
            whole = outs.pop(0)
            targets = [whole.at[j * rest : (j + 1) * rest] for j in range(size)]
        else:
            targets = [outs.pop(0) for _ in range(size)]
        for j, target in enumerate(targets):
            side = j if grouped else lax.bitwise_xor(coord, j)

            @pl.loop(0, rest)
            def _(r, target=target, side=side):
                upper = lax.shift_right_logical(r, log_inner)
                source = (upper * size + side) * inner + lax.bitwise_and(r, inner - 1)
                col = 0
                for piece in pieces:
                    width = piece[0][2] - piece[0][1]
                    first, low, high = piece[0]
                    value = ins[first][source, :, low:high]
                    if len(piece) > 1:
                        value = value.astype(F32)
                        for index, low, high in piece[1:]:
                            value = value + ins[index][source, :, low:high].astype(F32)
                    target[r, :, col : col + width] = value.astype(BF16)
                    col += width


def route(groups, name, grouped=False):
    arrays, plan, shapes = [], [], []
    for pieces, left, axis in groups:
        entries = []
        for piece in pieces:
            entry = []
            for array, low, high in piece:
                known = [i for i, other in enumerate(arrays) if other is array]
                if not known:
                    known = [len(arrays)]
                    arrays.append(array)
                entry.append((known[0], low, high))
            entries.append(tuple(entry))
        at = left.index(axis)
        plan.append((tuple(entries), tuple(size for _, size in left), at, axis[0], grouped))
        total = sum(piece[0][2] - piece[0][1] for piece in pieces)
        array = pieces[0][0][0]
        if grouped:
            shapes.append((1, (array.shape[0], array.shape[1], total)))
        else:
            shapes.append((axis[1], (array.shape[0] // axis[1], array.shape[1], total)))
    vmem = pl.BlockSpec(memory_space=pltpu.VMEM)
    out_shape = [jax.ShapeDtypeStruct(shape, BF16) for size, shape in shapes for _ in range(size)]
    kinds = tuple(isinstance(array, Product) for array in arrays)
    operands, scratch = [], []
    for array, is_product in zip(arrays, kinds):
        operands += [array.x, array.y] if is_product else [array]
        if is_product:
            scratch.append(pltpu.VMEM(array.shape, BF16))
    flat = pl.pallas_call(
        functools.partial(route_kernel, tuple(plan), kinds, len(out_shape)),
        out_shape=out_shape,
        in_specs=[vmem] * len(operands),
        out_specs=[vmem] * len(out_shape),
        scratch_shapes=scratch,
        compiler_params=pltpu.CompilerParams(vmem_limit_bytes=(20 if scratch else 6) << 20),
        cost_estimate=cost(1.0),
        name=name,
    )(*operands)
    outs = []
    for size, _ in shapes:
        outs.append(list(flat[:size]))
        flat = flat[size:]
    return outs


class Scatter:
    def __init__(self, arrays, orders, axes, name, group_last=False):
        self.group_last = group_last
        n = lax.axis_size("dp")
        self.name = name
        self.orders = [list(o) for o in orders]
        self.lefts = [list(axes) for _ in orders]
        self.pieces = []
        shaped = {}
        for parts in arrays:
            pieces = []
            if parts is None:
                self.pieces.append(None)
                continue
            for g, low, high in parts:
                if id(g) not in shaped:
                    shaped[id(g)] = g if isinstance(g, Product) else g.reshape(n, g.shape[0] // n, g.shape[1])
                pieces.append([(shaped[id(g)], low, high)])
            self.pieces.append(pieces)
        self.count = 0

    def deal(self):
        self.count += 1
        merged = len(self.pieces) > 1 and len(self.lefts[0]) < 3 and self.lefts[0] == self.lefts[1]
        groups = []
        if merged:
            groups.append((sum(self.pieces, []), self.lefts[0], self.orders[0][0]))
            self.orders, self.lefts = self.orders[:1], self.lefts[:1]
        else:
            for parts, left, order in zip(self.pieces, self.lefts, self.orders):
                groups.append((parts, left, order[0]))
        self.grouped = self.group_last and len(groups) == 1 and len(self.lefts[0]) == 1
        self.dealt = route(groups, f"{self.name}_deal_{self.count}", self.grouped)
        return self.dealt

    def send(self):
        pieces, lefts, orders = [], [], []
        for parts, left, order in zip(self.dealt, self.lefts, self.orders):
            shift, size = order[0]
            with jax.named_scope(f"{self.name}_{self.count}"):
                if self.grouped:
                    n = lax.axis_size("dp")
                    members = [[i | (j << shift) for j in range(size)] for i in range(n) if not (i >> shift) % size]
                    whole = lax.all_to_all(
                        parts[0], "dp", split_axis=0, concat_axis=0, axis_index_groups=members, tiled=True
                    )
                    rest = whole.shape[0] // size
                    got = [whole[j * rest : (j + 1) * rest] for j in range(size)]
                else:
                    got = [parts[0]] + [
                        xor_permute(parts[j], "dp", j << shift) for j in range(1, size)
                    ]
            pieces.append([[(x, 0, x.shape[2]) for x in got]])
            lefts.append([axis for axis in left if axis != order[0]])
            orders.append(order[1:])
        self.pieces, self.lefts, self.orders = pieces, lefts, orders

    def set_part(self, i, parts):
        self.pieces[i] = Scatter([parts], [self.orders[i]], self.lefts[i], self.name).pieces[0]

    def deal_one(self, i):
        return route([(self.pieces[i], self.lefts[i], self.orders[i][0])], f"{self.name}_deal_1{i}")[0]

    def send_one(self, i, parts):
        self.count = 1
        shift, size = self.orders[i][0]
        with jax.named_scope(f"{self.name}_1{i}"):
            got = [parts[0]] + [xor_permute(parts[j], "dp", j << shift) for j in range(1, size)]
        self.pieces[i] = [[(x, 0, x.shape[2]) for x in got]]
        self.lefts[i] = [axis for axis in self.lefts[i] if axis != self.orders[i][0]]
        self.orders[i] = self.orders[i][1:]

    def after(self, *others):
        arrays = [x for (piece,) in self.pieces for x, _, _ in piece[1:]]
        arrays = list(lax.optimization_barrier((tuple(arrays), others))[0])
        self.pieces = [
            [[piece[0]] + [(arrays.pop(0), low, high) for _, low, high in piece[1:]]] for (piece,) in self.pieces
        ]

    def before(self, x):
        arrays = [y for (piece,) in self.pieces for y, _, _ in piece]
        x, arrays = lax.optimization_barrier((x, tuple(arrays)))
        arrays = list(arrays)
        self.pieces = [[[(arrays.pop(0), low, high) for _, low, high in piece]] for (piece,) in self.pieces]
        return x

    def total(self):
        outs = []
        for (piece,) in self.pieces:
            parts = [x[0].astype(F32) for x, _, _ in piece]
            while len(parts) > 1:
                parts = [parts[i] + parts[i + 1] for i in range(0, len(parts), 2)]
            outs.append(parts[0])
        return outs[0] if len(outs) == 1 else jnp.concatenate(outs, axis=1)

    def finish_stages(self):
        while self.orders[0]:
            self.deal()
            self.send()

    def finish(self):
        self.finish_stages()
        return self.total()


def attend_forward_kernel(block, qkv_ref, bias_ref, *refs):
    ctx_ref, lse_ref = refs[-2:]
    length = qkv_ref.shape[0]
    bias = bias_ref[...]
    for head in range(2):
        low = head * HEAD_DIM
        keys = qkv_ref[:, PAIR + low : PAIR + low + HEAD_DIM]
        values_t = qkv_ref[:, 2 * PAIR + low : 2 * PAIR + low + HEAD_DIM].T
        for start in range(0, length, block):
            queries = qkv_ref[start : start + block, low : low + HEAD_DIM]
            scores = matmul_nt(keys, queries) + bias
            top = jnp.max(scores, axis=0, keepdims=True)
            exponent = jnp.exp(scores - top)
            total = jnp.sum(exponent, axis=0, keepdims=True)
            context_t = matmul(values_t, exponent.astype(BF16)) * (1.0 / total)
            ctx_ref[start : start + block, low : low + HEAD_DIM] = context_t.T.astype(BF16)
            lse_ref[0, head : head + 1, start : start + block] = top + jnp.log(total)


def attend_forward(qkv, bias, first, pairs, total, known=()):
    length = qkv.shape[0]
    return pl.pallas_call(
        functools.partial(attend_forward_kernel, min(512, length)),
        grid=(pairs,),
        out_shape=(
            jax.ShapeDtypeStruct((length, total * PAIR), BF16),
            jax.ShapeDtypeStruct((total, 2, length), F32),
        ),
        in_specs=[
            pl.BlockSpec((length, 3 * PAIR), lambda p: (0, p + first)),
            pl.BlockSpec((length, 1), lambda p: (0, 0)),
        ]
        + [pl.BlockSpec(memory_space=pl.ANY)] * len(known),
        out_specs=(
            pl.BlockSpec((length, PAIR), lambda p: (0, p + first)),
            pl.BlockSpec((1, 2, length), lambda p: (p + first, 0, 0)),
        ),
        input_output_aliases={2: 0, 3: 1} if known else {},
        compiler_params=pltpu.CompilerParams(vmem_limit_bytes=16 << 20),
        cost_estimate=cost(5.9 * pairs),
        name="attend_forward",
    )(qkv, bias, *known)


def attend_backward_kernel(block, qkv_ref, dctx_ref, lse_ref, bias_ref, *refs):
    out_ref, sums_ref, dk_ref, dv_ref = refs[-4:]
    length = qkv_ref.shape[0]
    bias = bias_ref[...]
    for head in range(2):
        low = head * HEAD_DIM
        keys = qkv_ref[:, PAIR + low : PAIR + low + HEAD_DIM]
        keys_t = keys.T
        values = qkv_ref[:, 2 * PAIR + low : 2 * PAIR + low + HEAD_DIM]
        query_sum = jnp.zeros((1, HEAD_DIM), F32)
        for start in range(0, length, block):
            queries = qkv_ref[start : start + block, low : low + HEAD_DIM]
            grads = dctx_ref[start : start + block, low : low + HEAD_DIM]
            lse = lse_ref[0, head : head + 1, start : start + block]
            probs = jnp.exp(matmul_nt(keys, queries) + bias - lse)
            grad_probs = matmul_nt(values, grads)
            inner = jnp.sum(probs * grad_probs, axis=0, keepdims=True)
            grad_scores = (probs * (grad_probs - inner)).astype(BF16)
            dv = matmul(probs.astype(BF16), grads)
            dk = matmul(grad_scores, queries)
            if start == 0:
                dk_ref[...] = dk
                dv_ref[...] = dv
            else:
                dk_ref[...] += dk
                dv_ref[...] += dv
            dq = (matmul(keys_t, grad_scores) * HEAD_DIM ** (-0.5)).T
            query_sum = query_sum + jnp.sum(dq, axis=0, keepdims=True)
            out_ref[start : start + block, low : low + HEAD_DIM] = dq.astype(BF16)
        dk = dk_ref[...]
        dv = dv_ref[...]
        out_ref[:, PAIR + low : PAIR + low + HEAD_DIM] = dk.astype(BF16)
        out_ref[:, 2 * PAIR + low : 2 * PAIR + low + HEAD_DIM] = dv.astype(BF16)
        sums_ref[0, 0:1, low : low + HEAD_DIM] = query_sum
        sums_ref[0, 1:2, low : low + HEAD_DIM] = jnp.sum(dv, axis=0, keepdims=True)


def attend_backward(qkv, dctx, lse, bias, first, pairs, total, known=()):
    length = qkv.shape[0]
    return pl.pallas_call(
        functools.partial(attend_backward_kernel, min(256, length)),
        grid=(pairs,),
        out_shape=(
            jax.ShapeDtypeStruct((length, total * 3 * PAIR), BF16),
            jax.ShapeDtypeStruct((total, 2, PAIR), F32),
        ),
        in_specs=[
            pl.BlockSpec((length, 3 * PAIR), lambda p: (0, p + first)),
            pl.BlockSpec((length, PAIR), lambda p: (0, p + first)),
            pl.BlockSpec((1, 2, length), lambda p: (p + first, 0, 0)),
            pl.BlockSpec((length, 1), lambda p: (0, 0)),
        ]
        + [pl.BlockSpec(memory_space=pl.ANY)] * len(known),
        out_specs=(
            pl.BlockSpec((length, 3 * PAIR), lambda p: (0, p + first)),
            pl.BlockSpec((1, 2, PAIR), lambda p: (p + first, 0, 0)),
        ),
        input_output_aliases={4: 0, 5: 1} if known else {},
        scratch_shapes=[pltpu.VMEM((length, HEAD_DIM), F32), pltpu.VMEM((length, HEAD_DIM), F32)],
        compiler_params=pltpu.CompilerParams(vmem_limit_bytes=16 << 20),
        cost_estimate=cost(7.3 * pairs),
        name="attend_backward",
    )(qkv, dctx, lse, bias, *known)


def call(kernel, outs, args, name, us, vmem_mib=10, scratch=()):
    spec = pl.BlockSpec(memory_space=pltpu.VMEM)
    return pl.pallas_call(
        kernel,
        out_shape=[jax.ShapeDtypeStruct(shape, kind) for shape, kind in outs],
        in_specs=[spec] * len(args),
        out_specs=[spec] * len(outs),
        scratch_shapes=list(scratch),
        compiler_params=pltpu.CompilerParams(vmem_limit_bytes=vmem_mib << 20),
        cost_estimate=cost(us),
        name=name,
    )(*args)


def row_blocks(rows, block):
    block = min(block, rows)
    return rows // block, block


def rows_at(i, block):
    return pl.ds(pl.multiple_of(i * block, block), block)


def project_kernel(x_ref, w_ref, bias_ref, scale_ref, out_ref):
    count, block = row_blocks(x_ref.shape[0], 512)

    @pl.loop(0, count)
    def _(i):
        at = rows_at(i, block)
        out_ref[at, :] = ((matmul(x_ref[at, :], w_ref[...]) + bias_ref[...]) * scale_ref[...]).astype(BF16)


def part_kernel(low, high, x_ref, w_ref, out_ref):
    out_ref[...] = matmul_nt(x_ref[low:high, :], w_ref[...]).astype(BF16)


def exchanged_parts(x, w, name):
    half = x.shape[0] // 2
    own, got = [], []
    for number in range(2):
        (part,) = call(
            functools.partial(part_kernel, number * half, (number + 1) * half),
            [((half, w.shape[0]), BF16)],
            (x, w),
            f"{name}_{number}",
            1.5,
        )
        if number == 0:
            x = tie(x, part)
        own.append(part)
        with jax.named_scope(f"{name}_{number}"):
            got.append(xor_permute(part, "mp", 1))
    return own + got[::-1]


def halves(parts, body, rows, block):
    count, block = row_blocks(rows // 2, block)
    for number in range(2):
        own_ref, got_ref = parts[number], parts[2 + number]

        @pl.loop(0, count)
        def _(i, number=number, own_ref=own_ref, got_ref=got_ref):
            at = rows_at(i, block)
            total = own_ref[at, :].astype(F32) + got_ref[at, :].astype(F32)
            body(number, at, rows_at(i + number * count, block), total)


def middle_kernel(x_ref, p0, p1, p2, p3, vec_ref, w_ref, bias_ref, normed_ref, rstd_ref, low_ref, act_ref, slope_ref):
    def body(number, half_at, at, total):
        mixed = x_ref[at, :].astype(F32) + total + vec_ref[2:3, :]
        normed, rstd = norm_forward(mixed)
        normed_ref[at, :] = normed.astype(BF16)
        rstd_ref[at, :] = rstd
        low = (normed * vec_ref[0:1, :] + vec_ref[3:4, :]).astype(BF16)
        low_ref[at, :] = low
        u = matmul(low, w_ref[...]) + bias_ref[...]
        half_cdf = 0.5 * (1.0 + lax.erf(u * root_half))
        act_ref[at, :] = (u * half_cdf).astype(BF16)
        slope_ref[at, :] = (half_cdf + u * jnp.exp(-0.5 * u * u) * inv_root_two_pi).astype(BF16)

    halves((p0, p1, p2, p3), body, x_ref.shape[0], 256)


def outer_kernel(normed_ref, p0, p1, p2, p3, cot_own_ref, cot_got0, cot_got1, vec_ref, out_ref, low_ref, sums_ref, cot_ref):
    sums_ref[...] = jnp.zeros_like(sums_ref)

    half = cot_own_ref.shape[0]
    for index, source in enumerate((cot_own_ref, cot_got0, cot_got1)):
        low = 0 if index == 0 else half + (index - 1) * (half // 2)
        cot_ref[low : low + source.shape[0], :] = source[...]

    def body(number, half_at, at, total):
        mixed = normed_ref[at, :].astype(F32) * vec_ref[0:1, :] + vec_ref[3:4, :] + total + vec_ref[4:5, :]
        normed, rstd = norm_forward(mixed)
        if number == 0:
            out_ref[at, :] = (normed * vec_ref[1:2, :] + vec_ref[5:6, :]).astype(BF16)
        cot = cot_ref[at, :].astype(F32)
        grad, grad_gain, grad_shift = norm_backward(cot, normed, rstd, vec_ref[1:2, :])
        low_ref[at, :] = grad.astype(BF16)
        sums_ref[0:1, :] += grad_gain
        sums_ref[1:2, :] += grad_shift
        sums_ref[2:3, :] += jnp.sum(grad, axis=0, keepdims=True)

    halves((p0, p1, p2, p3), body, normed_ref.shape[0], 256)


def hidden_grad_kernel(grad_ref, w_ref, slope_ref, out_ref, sums_ref):
    count, block = row_blocks(grad_ref.shape[0], 256)
    sums_ref[...] = jnp.zeros_like(sums_ref)

    @pl.loop(0, count)
    def _(i):
        at = rows_at(i, block)
        grad = matmul(grad_ref[at, :], w_ref[...]) * slope_ref[at, :].astype(F32)
        out_ref[at, :] = grad.astype(BF16)
        sums_ref[...] += jnp.sum(grad, axis=0, keepdims=True)


def inner_kernel(
    grad_in_ref, p0, p1, p2, p3, normed_ref, rstd_ref, vec_ref, w_ref, own_grad_ref, low_ref, ctx_ref, sums_ref
):
    sums_ref[...] = jnp.zeros_like(sums_ref)

    def body(number, half_at, at, total):
        given = grad_in_ref[at, :].astype(F32) + total
        grad, grad_gain, grad_shift = norm_backward(given, normed_ref[at, :].astype(F32), rstd_ref[at, :], vec_ref[0:1, :])
        low = grad.astype(BF16)
        low_ref[at, :] = low
        ctx_ref[at, :] = matmul(low, w_ref[...]).astype(BF16)
        sums_ref[0:1, :] += grad_gain
        sums_ref[1:2, :] += grad_shift
        sums_ref[2:3, :] += jnp.sum(grad, axis=0, keepdims=True)
        if number == 0:
            own_grad_ref[at, :] = grad

    halves((p0, p1, p2, p3), body, normed_ref.shape[0], 256)


def input_grad_kernel(x_ref, w_ref, grad_ref, keep_ref, send_ref):
    half = keep_ref.shape[0]
    send_ref[...] = matmul_nt(x_ref[half:, :], w_ref[...]).astype(BF16)
    keep_ref[...] = grad_ref[...] + matmul_nt(x_ref[:half, :], w_ref[...])


def norm_forward(rows):
    center = rows - jnp.mean(rows, axis=1, keepdims=True)
    rstd = lax.rsqrt(jnp.mean(center * center, axis=1, keepdims=True) + eps_norm)
    return center * rstd, rstd


def norm_backward(grad, normed, rstd, gain):
    scaled = grad * gain
    inner = (
        scaled
        - jnp.mean(scaled, axis=1, keepdims=True)
        - normed * jnp.mean(scaled * normed, axis=1, keepdims=True)
    )
    return (
        rstd * inner,
        jnp.sum(grad * normed, axis=0, keepdims=True),
        jnp.sum(grad, axis=0, keepdims=True),
    )


def from_other(x):
    half = x.shape[0] // 2
    return [xor_permute(x[:half], "mp", 1), xor_permute(x[half:], "mp", 1)]


def deal_rows(x, deal_order):
    return x[0].at[:, deal_order].get(mode="promise_in_bounds").transpose(1, 0, 2)


def exchange_in(dealt, *others):
    dealt = tie(dealt, *others)
    arrived = lax.all_to_all(dealt, "dp", split_axis=0, concat_axis=0, tiled=True)
    return arrived.reshape(-1, dealt.shape[2])


def exchange_out(rows, extra):
    n = lax.axis_size("dp")
    with jax.named_scope("out_rows"):
        blocks = rows.reshape(n, rows.shape[0] // n, rows.shape[1])
        blocks = jnp.concatenate([blocks, jnp.broadcast_to(extra, (n,) + extra.shape)], axis=1)
        return lax.all_to_all(blocks, "dp", split_axis=0, concat_axis=0, tiled=True)


def taken_out(sent, count):
    return sent[:, :count].transpose(1, 0, 2)[None], sent[:, count:]


def put_split(out_ref, row, count, value):
    high = value.astype(BF16)
    out_ref[row : row + 1, :] = high
    out_ref[row + count : row + count + 1, :] = (value - high.astype(F32)).astype(BF16)


def early_kernel(one_ref, two_ref, up_ref, out_ref):
    first = lax.axis_index("mp") == 0
    width = one_ref.shape[1]
    pieces = up_ref.shape[1] // width
    count = 3 + pieces
    out_ref[...] = jnp.zeros_like(out_ref)
    for row in range(3):
        put_split(out_ref, row, count, jnp.where(first, one_ref[row : row + 1, :], two_ref[row : row + 1, :]))
    for piece in range(pieces):
        put_split(out_ref, 3 + piece, count, up_ref[0:1, piece * width : (piece + 1) * width])


def late_kernel(pairs, keep_ref, g0, g1, sums_ref, rows_ref, out_ref):
    half = keep_ref.shape[0] // 2
    for index, source in enumerate((g0, g1)):
        at = slice(index * half, (index + 1) * half)
        rows_ref[at, :] = (keep_ref[at, :] + source[...].astype(F32)).astype(BF16)
    out_ref[...] = jnp.zeros_like(out_ref)
    for which in range(2):
        for pair in range(pairs):
            col = (which * pairs + pair) * PAIR
            value = sums_ref[pair, which : which + 1, :]
            high = value.astype(BF16)
            out_ref[0:1, col : col + PAIR] = high
            out_ref[1:2, col : col + PAIR] = (value - high.astype(F32)).astype(BF16)


def gathered_kernel(count, x_ref, out_ref):
    out_ref[...] = jnp.zeros_like(out_ref)

    @pl.loop(0, x_ref.shape[0])
    def _(i):
        x = x_ref[i].astype(F32)
        out_ref[...] += x[:count, :] + x[count : 2 * count, :]


def local(
    tokens, cotangent, lengths, deal_order, attn_in, attn_out, ffn_in, ffn_out,
    attn_bias, ffn_bias, norm_gain, shifts,
):
    dp_size = lax.axis_size("dp")
    mp_rank = lax.axis_index("mp")
    dp_rank = lax.axis_index("dp")
    axes = dp_axes(dp_size)
    low = axes[-2:]
    high = axes[:-2]
    order_one = high + low
    order_two = high + low[::-1]
    high_two = pairs_of(high)
    back_one = low[::-1] + high[::-1]
    back_two = low + high[::-1]

    width = tokens.shape[3]
    half_len = tokens.shape[1] * dp_size
    seq_len = 2 * half_len
    head_cols = attn_in.shape[3]
    hidden_cols = ffn_in.shape[2]
    pairs = head_cols // PAIR
    shard_rows = attn_in.shape[2]

    three = attn_in[0].reshape(3, shard_rows, pairs, PAIR).transpose(1, 2, 0, 3)
    three = three.reshape(shard_rows, 3 * head_cols)
    back_t = attn_out[0].T
    up = ffn_in[0]
    down_t = ffn_out[0].T

    cut_three = 128 * ((3 * head_cols // 128 + 1) // 2)
    pieces_three = [three[:, :cut_three], three[:, cut_three:]]
    rest = jnp.concatenate([back_t, up], axis=1)
    cut_rest = 128 * ((rest.shape[1] // 128 + 1) // 2)
    orders = [tuple(order_one), tuple(order_two)]

    first_three = gather_first(three, order_one, "ag_three")
    with jax.named_scope("in_tokens"):
        tok_own = exchange_in(deal_rows(tokens, deal_order), first_three)
        dealt_cot = deal_rows(cotangent, deal_order)
    w_down = lax.all_gather(down_t, "dp", axis=0, tiled=True)
    next_three = [
        gather_next(first_three[:, :, :cut_three], order_one, "ag_three"),
        gather_next(first_three[:, :, cut_three:], order_two, "ag_three"),
    ]
    rest, *next_three = lax.optimization_barrier((rest, *next_three))
    with jax.named_scope("ag_rest_first"):
        first_got = [rest[None]]
        for shift, size in order_one[:-3]:
            first_got = [stage_gather(x, "dp", shift, size) for x in first_got]
        shift, size = order_one[-3]
        first_own = first_got[0]
        first_got = [xor_permute(first_own, "dp", j << shift) for j in range(1, size)]
    sides_three = gather_last(next_three[0], order_one, "ag_three") + gather_last(
        next_three[1], order_two, "ag_three"
    )
    (w_three,) = assemble(sides_three, orders, [3 * head_cols])
    hb = jnp.concatenate([tok_own] + from_other(tok_own), axis=0)
    length = lengths[deal_order[dp_rank]]
    place = jnp.arange(seq_len, dtype=jnp.int32)
    place = jnp.where(mp_rank == 0, place, (place + half_len) % seq_len)
    bias_col = jnp.where(place < length, 0.0, negative_fill).astype(F32)[:, None]

    def own_cols(v, count):
        return jnp.where(mp_rank == 0, v[..., :count], v[..., count:])

    bias_pair = own_cols(attn_bias[0].astype(F32), head_cols).reshape(2, pairs, PAIR)
    bias_three = jnp.stack([bias_pair[0], jnp.zeros_like(bias_pair[0]), bias_pair[1]], axis=1).reshape(1, -1)
    bias_up = own_cols(ffn_bias[0].astype(F32), hidden_cols)[None]
    scale_three = jnp.concatenate(
        [jnp.full((pairs, 1, PAIR), HEAD_DIM ** (-0.5), F32), jnp.ones((pairs, 2, PAIR), F32)], axis=1
    ).reshape(1, -1)
    vec = jnp.concatenate([norm_gain[0], shifts[0]], axis=0).astype(F32)
    hb, bias_up, vec, bias_col, dealt_cot = lax.optimization_barrier((hb, bias_up, vec, bias_col, dealt_cot))
    big, wide, hidden_shape = (seq_len, width), (seq_len, head_cols), (seq_len, hidden_cols)

    (qkv,) = call(
        project_kernel, [((seq_len, 3 * head_cols), BF16)], (hb, w_three, bias_three, scale_three), "project", 2.4
    )
    attended = attend_forward(qkv, bias_col, 0, 1, pairs)
    attended, *first_got = lax.optimization_barrier((attended, *first_got))
    first_rest = jnp.concatenate([first_own] + first_got, axis=0)
    attended, first_rest = lax.optimization_barrier((attended, first_rest))
    own_rest = [first_rest[:, :, :cut_rest], first_rest[:, :, cut_rest:]]
    with jax.named_scope("ag_rest_next"):
        got_rest = [xor_permute(y, "dp", 1 << o[-2][0]) for y, o in zip(own_rest, orders)]
    if pairs > 2:
        attended = attend_forward(qkv, bias_col, 1, pairs - 2, pairs, attended)
    attended, *got_rest = lax.optimization_barrier((attended, *got_rest))
    next_rest = [jnp.concatenate(pair, axis=0) for pair in zip(own_rest, got_rest)]
    attended, *next_rest = lax.optimization_barrier((attended, *next_rest))
    sides_rest = gather_last(next_rest[0], order_one, "ag_rest") + gather_last(
        next_rest[1], order_two, "ag_rest"
    )
    if pairs > 1:
        attended = attend_forward(qkv, bias_col, pairs - 1, 1, pairs, attended)
    context, lse = attended
    with jax.named_scope("in_cot"):
        cot_own = exchange_in(dealt_cot, context)
    context, w_down = lax.optimization_barrier((context, w_down))
    w_back, w_up = assemble(sides_rest, orders, [head_cols, hidden_cols])
    mid_normed, mid_rstd, mid_low, hidden_low, slope = call(
        middle_kernel,
        [(big, BF16), ((seq_len, 1), F32), (big, BF16), (hidden_shape, BF16), (hidden_shape, BF16)],
        (hb, *exchanged_parts(context, w_back, "attn_part"), vec, w_up, bias_up),
        "middle",
        8,
    )

    result, grad_two_low, sums_two = call(
        outer_kernel,
        [((half_len, width), BF16), (big, BF16), ((3, width), F32)],
        (
            mid_normed,
            *exchanged_parts(hidden_low, w_down, "ffn_part"),
            cot_own,
            *from_other(cot_own),
            vec,
        ),
        "outer",
        4.5,
        scratch=[pltpu.VMEM(big, BF16)],
    )
    ffn = Scatter(
        [[(gradient(grad_two_low, hidden_low), 0, hidden_cols)], None],
        [low[::-1] + high_two[::-1], low + high_two[::-1]],
        high_two + low,
        "rs_ffn",
    )
    dealt = ffn.deal_one(0)
    grad_two_low, dealt = lax.optimization_barrier((grad_two_low, dealt))
    ffn.send_one(0, dealt)
    grad_hidden_low, grad_up_bias = call(
        hidden_grad_kernel,
        [(hidden_shape, BF16), ((1, hidden_cols), F32)],
        (grad_two_low, w_down, slope),
        "hidden_grad",
        3.3,
    )
    parts = exchanged_parts(grad_hidden_low, w_up, "mid_part")
    grad_hidden_low = tie(grad_hidden_low, parts[1])
    ffn.set_part(1, [(gradient(mid_low, grad_hidden_low), 0, hidden_cols)])
    dealt = ffn.deal_one(1)
    parts[2], dealt = lax.optimization_barrier((parts[2], dealt))
    ffn.send_one(1, dealt)
    grad_one, grad_one_low, grad_context, sums_one = call(
        inner_kernel,
        [((half_len, width), F32), (big, BF16), (wide, BF16), ((3, width), F32)],
        (grad_two_low, *parts, mid_normed, mid_rstd, vec, w_back),
        "inner",
        3.5,
    )
    early_count = 3 + hidden_cols // width
    (early,) = call(
        early_kernel, [((16 * -(-2 * early_count // 16), width), BF16)], (sums_one, sums_two, grad_up_bias), "early", 0.5
    )
    sent_tokens = exchange_out(result, early)
    grad_w_back = gradient(grad_one_low, context)

    given = ()
    if pairs > 1:
        given = attend_backward(qkv, grad_context, lse, bias_col, 0, pairs - 1, pairs)
        ffn.after(given)
    ffn.deal()
    grad_context, ffn.dealt = lax.optimization_barrier((grad_context, ffn.dealt))
    ffn.send()
    given = attend_backward(qkv, grad_context, lse, bias_col, pairs - 1, 1, pairs, given)
    dqkv, pair_sums = given
    ffn.after(given)
    ffn.deal()
    dqkv, ffn.dealt = lax.optimization_barrier((dqkv, ffn.dealt))
    ffn.send()
    grad_w_three = gradient(hb, dqkv)
    cut = 128 * ((4 * head_cols // 128 + 1) // 2)
    tail = Scatter(
        [
            [(grad_w_three, 0, cut)],
            [(grad_w_three, cut, 3 * head_cols), (grad_w_back, 0, head_cols)],
        ],
        [low[::-1] + high_two[::-1], low + high_two[::-1]],
        high_two + low,
        "rs_attn",
    )
    tail.deal()
    dqkv, tail.dealt = lax.optimization_barrier((dqkv, tail.dealt))
    tail.send()
    keep, sent = call(
        input_grad_kernel,
        [((half_len, width), F32), ((half_len, width), BF16)],
        (dqkv, w_three, grad_one),
        "input_grad",
        2.3,
    )
    got = from_other(sent)
    grad_in, late = call(
        functools.partial(late_kernel, pairs),
        [((half_len, width), BF16), ((8, 2 * head_cols), BF16)],
        (keep, *got, pair_sums),
        "late",
        1.0,
    )
    sent_grad = exchange_out(grad_in, late)
    block = half_len // dp_size
    out_tokens, early_all = taken_out(sent_tokens, block)
    out_grad, late_all = taken_out(sent_grad, block)
    tail.deal()
    ffn.after(tail.dealt)
    tail.send()
    ffn.deal()
    tail.deal()
    tail.dealt, ffn.dealt = lax.optimization_barrier((tail.dealt, ffn.dealt))
    ffn.send()
    tail.send()
    tail.deal()
    ffn.after(tail.dealt)
    tail.send()
    ffn_sum = ffn.finish()
    down_sum, up_sum = ffn_sum[:, :hidden_cols], ffn_sum[:, hidden_cols:]

    (early_sum,) = call(
        functools.partial(gathered_kernel, early_count), [((early_count, width), F32)], (early_all,), "early_sum", 0.5
    )
    (late_sum,) = call(functools.partial(gathered_kernel, 1), [((1, width), F32)], (late_all,), "late_sum", 0.5)

    def in_order(own):
        other = xor_permute(own, "mp", 1)
        return jnp.where(mp_rank == 0, own, other), jnp.where(mp_rank == 0, other, own)

    low_early, high_early = in_order(early_sum)
    low_late, high_late = in_order(late_sum)
    gain_out = jnp.stack([low_early[0], high_early[0]])[None]
    shift_out = jnp.stack([low_early[2], low_early[1], high_early[2], high_early[1]])[None]
    ffn_bias_out = jnp.concatenate([low_early[3:].reshape(1, -1), high_early[3:].reshape(1, -1)], axis=1)
    attn_bias_out = jnp.concatenate(
        [low_late.reshape(1, 2, head_cols), high_late.reshape(1, 2, head_cols)], axis=2
    )

    tail.after(out_grad)
    attn_sum = tail.finish()
    three_sum, back_sum = attn_sum[:, : 3 * head_cols], attn_sum[:, 3 * head_cols :]
    three_out = three_sum.reshape(shard_rows, pairs, 3, PAIR)
    three_out = three_out.transpose(2, 0, 1, 3).reshape(1, 3, shard_rows, head_cols)
    back_out = back_sum.T[None]
    up_out = up_sum[None]
    down_out = down_sum.T[None]
    return (
        out_tokens, out_grad, three_out, back_out, up_out, down_out,
        attn_bias_out, ffn_bias_out, gain_out, shift_out,
    )


def solution(mesh):
    placed = (
        P("mp", "dp", None, None),
        P("mp", "dp", None, None),
        P(),
        P(),
        P(None, None, "dp", "mp"),
        P(None, "mp", "dp"),
        P(None, "dp", "mp"),
        P(None, "mp", "dp"),
        P(),
        P(),
        P(),
        P(),
    )
    return jax.shard_map(
        local,
        mesh=mesh,
        in_specs=placed,
        out_specs=(
            P("mp", "dp", None, None),
            P("mp", "dp", None, None),
            P(None, None, "dp", "mp"),
            P(None, "mp", "dp"),
            P(None, "dp", "mp"),
            P(None, "mp", "dp"),
            P(),
            P(),
            P(),
            P(),
        ),
        check_vma=False,
    )
```
